32 devices in a mesh: wide: 8 (over z, x), narrow: 4 (over y, core).
Axes of the slice: x: 2, y: 2, z: 4, core: 2. Of those that a mesh axis runs over, the one named last changes fastest.
Arguments:
- layer_input: bfloat16 [32, 1024, 768], P(('wide', 'narrow')), may hold values from -6 to 6
- cotangent: bfloat16 [32, 1024, 768], P(('wide', 'narrow')), may hold values from -6 to 6
- block_size: int32 [32], P(('wide', 'narrow')), may hold values from 4 to 16, as said below
- gain_attn: bfloat16 [768], P('narrow'), may hold values from 0.5 to 1.5
- w_qkv: bfloat16 [768, 2304], P('narrow'), may hold values from -0.21875 to 0.21875
- w_out: bfloat16 [768, 768], P('narrow'), may hold values from -0.875 to 0.875
- gain_mlp: bfloat16 [768], P('narrow'), may hold values from 0.5 to 1.5
- w_up: bfloat16 [768, 3072], P('narrow'), may hold values from -0.21875 to 0.21875
- b_up: bfloat16 [3072], P('narrow'), may hold values from -3 to 3
- w_down: bfloat16 [3072, 768], P('narrow'), may hold values from -0.109375 to 0.109375
- b_down: bfloat16 [768], P('narrow'), may hold values from -3 to 3
Outputs:
- layer_output: bfloat16 [32, 1024, 768], P(('wide', 'narrow'))
- d_x: bfloat16 [32, 1024, 768], P(('wide', 'narrow'))
- grad_gain_attn: float32 [768], P('narrow')
- grad_qkv: float32 [768, 2304], P('narrow')
- grad_out: float32 [768, 768], P('narrow')
- grad_gain_mlp: float32 [768], P('narrow')
- grad_up: float32 [768, 3072], P('narrow')
- grad_b_up: float32 [3072], P('narrow')
- grad_down: float32 [3072, 768], P('narrow')
- grad_b_down: float32 [768], P('narrow')
The draws below stay inside these ranges and needn't reach their ends.
Inputs may be any that keep to these rules, and one draw needn't show every extreme that they name: `block_size`: each example's block size is 4, 8 or 16; every draw has examples with 4 and with 16.
All inputs are finite; a program needn't handle non-finite values.
Results may differ from the reference program's by a relative error of at most 0.015.
Values may be sent and summed in bfloat16 or wider, within the bound.
No kernel may reach another device: no remote copies, remote signals or barrier semaphores. Data moves between devices by JAX's collectives and lax.ppermute only.
A program may use at most 256 MiB of HBM per device.

```python
import jax
import jax.numpy as jnp
from jax import lax

D = 768
HEAD = 64
FF = 3072
SEQ = 512
EXAMPLES = 32


def draw_block_size(key, part):
    level = jax.random.randint(key, (EXAMPLES,), 0, 3)
    sizes = jnp.left_shift(jnp.int32(4), level.astype(jnp.int32))
    return sizes.at[0].set(16).at[1].set(4).astype(jnp.int32)


def block_scale(own_key, shape, shards, low, top_value):
    level, own = 1.0, jax.random.fold_in(own_key, 6)
    for axis_at, shards_of in shards:
        heights = jnp.exp(jax.random.uniform(jax.random.fold_in(own, axis_at), (shards_of,), jnp.float32, low / len(shards), top_value / len(shards)))
        level = level * jnp.repeat(heights, shape[axis_at] // shards_of).reshape([-1 if axis == axis_at else 1 for axis in range(len(shape))])
    return level


def normal_values(own_key, shape, scale, most, split=(), held_as=jnp.bfloat16):
    drawn = jax.random.normal(own_key, shape, jnp.float32) * scale
    if len(split) > 0:
        drawn = block_scale(own_key, shape, split, -0.22, 0.18) * drawn
    return jnp.clip(drawn, min=-most, max=most).astype(held_as)


def setup_inputs(seed: int = 0) -> dict:
    streams_of = jax.random.split(jax.random.key(seed), 12)
    return {
        "layer_input": normal_values(streams_of[0], (EXAMPLES, 2 * SEQ, D), 1.0, 6.0, ((0, 32),)),
        "cotangent": normal_values(streams_of[1], (EXAMPLES, 2 * SEQ, D), 1.0, 6.0, ((0, 32),)),
        "block_size": draw_block_size(jax.random.fold_in(streams_of[11], 71), 0),
        "gain_attn": jnp.clip(1.0 + 0.1 * jax.random.normal(streams_of[3], (D,), jnp.float32), 0.5, 1.5).astype(jnp.bfloat16),
        "w_qkv": normal_values(streams_of[4], (D, 3 * D), D ** -0.5, 0.21875, ((0, 4),)),
        "w_out": normal_values(streams_of[5], (D, D), (D // 16) ** -0.5, 0.875, ((0, 4),)),
        "gain_mlp": jnp.clip(1.0 + 0.1 * jax.random.normal(streams_of[6], (D,), jnp.float32), 0.5, 1.5).astype(jnp.bfloat16),
        "w_up": normal_values(streams_of[7], (D, FF), D ** -0.5, 0.21875, ((0, 4),)),
        "b_up": normal_values(streams_of[8], (FF,), 0.5, 3.0, ((0, 4),)),
        "w_down": normal_values(streams_of[9], (FF, D), FF ** -0.5, 0.109375, ((0, 4),)),
        "b_down": normal_values(streams_of[10], (D,), 0.5, 3.0, ((0, 4),)),
    }


@jax.custom_vjp
def low(v):
    return lax.optimization_barrier(v.astype(jnp.bfloat16)).astype(jnp.float32)

@jax.custom_vjp
def low_back(v):
    return v

def low_keep(v):
    return (low(v), None)

def low_pass(kept, grad):
    return (grad,)

def back_keep(v):
    return (v, None)

def back_low(kept, grad):
    return (low(grad),)
low.defvjp(low_keep, low_pass)
low_back.defvjp(back_keep, back_low)

def matmul(left, right):
    return jnp.dot(left, right, precision=lax.Precision.HIGHEST)

def norm_rows(values, gain):
    centre = values - lax.optimization_barrier(jnp.mean(values, axis=-1, keepdims=True))
    spread = lax.optimization_barrier(jnp.mean(centre * centre, axis=-1, keepdims=True))
    return centre * lax.rsqrt(spread + 1e-05) * gain

def rotate(tensor, angles):
    half = tensor.shape[-1] // 2
    cosine = jnp.cos(angles)[:, None, :]
    sine = jnp.sin(angles)[:, None, :]
    first = tensor[..., :half]
    second = tensor[..., half:]
    return jnp.concatenate([first * cosine - second * sine, second * cosine + first * sine], axis=-1)

def forward(xval, gain_a, wqkv, wout, gain_m, wup, bup, wdown, bdown, bsize):
    rows = xval.shape[0]
    seq = rows // 2
    width = xval.shape[1]
    heads = width // HEAD
    index = jnp.arange(rows, dtype=jnp.int32)
    posit = index % seq
    clean = index >= seq
    block = posit // bsize
    half = HEAD // 2
    freq = 10000.0 ** (-jnp.arange(half).astype(jnp.float32) / half)
    angles = posit.astype(jnp.float32)[:, None] * freq[None, :]
    qblk = block[:, None]
    kblk = block[None, :]
    qcl = clean[:, None]
    kcl = clean[None, :]
    mask = ~qcl & ~kcl & (qblk == kblk) | ~qcl & kcl & (kblk < qblk) | qcl & kcl & (kblk <= qblk)
    a1 = low(norm_rows(xval, gain_a))
    qkv = low_back(matmul(a1, wqkv))
    query = low(rotate(qkv[:, :width].reshape(rows, heads, HEAD), angles))
    keys = low(rotate(qkv[:, width:2 * width].reshape(rows, heads, HEAD), angles))
    vals = low(qkv[:, 2 * width:].reshape(rows, heads, HEAD))
    scores = low_back(jnp.einsum('qhd,khd->hqk', query, keys, precision=lax.Precision.HIGHEST) * 0.125)
    scores = jnp.where(mask[None], scores, -1e+30)
    expo = jnp.exp(scores - lax.optimization_barrier(jnp.max(scores, axis=-1, keepdims=True)))
    probs = low(expo / lax.optimization_barrier(jnp.sum(expo, axis=-1, keepdims=True)))
    attended = jnp.einsum('hqk,khd->qhd', probs, vals, precision=lax.Precision.HIGHEST).reshape(rows, width)
    attended = low(low_back(attended))
    x_mid = xval + low_back(matmul(attended, wout))
    a2 = low(norm_rows(x_mid, gain_m))
    upper = low_back(matmul(a2, wup)) + bup
    hidden = low(jax.nn.gelu(upper, approximate=True))
    return x_mid + low_back(matmul(hidden, wdown)) + bdown

def reference(layer_input, cotangent, block_size, gain_attn, w_qkv, w_out, gain_mlp, w_up, b_up, w_down, b_down):
    weights = tuple((w.astype(jnp.float32) for w in (gain_attn, w_qkv, w_out, gain_mlp, w_up, b_up, w_down, b_down)))

    def step(carry, item):
        x_one, cot_one, size_one = item

        def inner(xval, gain_a, wqkv, wout, gain_m, wup, bup, wdown, bdown):
            return forward(xval, gain_a, wqkv, wout, gain_m, wup, bup, wdown, bdown, size_one)
        result, pull = jax.vjp(inner, x_one.astype(jnp.float32), *weights)
        grads = pull(cot_one.astype(jnp.float32))
        summed = tuple((a + b for a, b in zip(carry, grads[1:])))
        return (summed, (result.astype(jnp.bfloat16), grads[0].astype(jnp.bfloat16)))
    start = tuple((jnp.zeros(w.shape, jnp.float32) for w in weights))
    sums, outputs = lax.scan(step, start, (layer_input, cotangent, block_size))
    return (outputs[0], outputs[1], sums[0], sums[1], sums[2], sums[3], sums[4], sums[5], sums[6], sums[7])
```

```python
import functools
import math

import jax
import jax.numpy as jnp
from jax import lax
from jax.experimental import pallas as pl
from jax.experimental.pallas import tpu as pltpu
from jax.sharding import PartitionSpec as P

HEAD = 64
PAIR = 2 * HEAD
TILE = 128
LOG2E = 1.4426950408889634
LN2 = 0.6931471805599453
f32 = jnp.float32
bf16 = jnp.bfloat16
MIB = 1 << 20


def nn(left, right):
    return jnp.dot(left, right, preferred_element_type=f32)


def nt(left, right):
    return lax.dot_general(left, right, (((1,), (1,)), ((), ())), preferred_element_type=f32)


def norm_rows(values):
    centre = values - jnp.mean(values, axis=-1, keepdims=True)
    inverse = lax.rsqrt(jnp.mean(centre * centre, axis=-1, keepdims=True) + 1e-05)
    return centre * inverse, inverse


def norm_back(d_norm, scaled, inverse, gain):
    d_scaled = d_norm * gain
    return inverse * (
        d_scaled
        - jnp.mean(d_scaled, axis=-1, keepdims=True)
        - scaled * jnp.mean(d_scaled * scaled, axis=-1, keepdims=True)
    )


def swap_halves(tile):
    lane = lax.broadcasted_iota(jnp.int32, (1, PAIR), 1) % HEAD
    return jnp.where(
        lane < HEAD // 2,
        pltpu.roll(tile, PAIR - HEAD // 2, 1),
        pltpu.roll(tile, HEAD // 2, 1),
    )


def assemble(index, parts, whole):
    rows = parts[0].shape[0]
    for j, part in enumerate(parts):
        start = pl.multiple_of((index ^ j) * rows, math.gcd(rows, 256))
        whole[pl.ds(start, rows), :] = part[...]


def fixed(shape):
    return pl.BlockSpec(shape, lambda *_: (0,) * len(shape), pipeline_mode=pl.Buffered(1))


def call(body, name, grid, in_specs, out_specs, out_shape, scratch, limit, cost):
    return pl.pallas_call(
        body,
        name=name,
        out_shape=out_shape,
        grid_spec=pltpu.PrefetchScalarGridSpec(
            num_scalar_prefetch=1,
            grid=grid,
            in_specs=in_specs,
            out_specs=out_specs,
            scratch_shapes=scratch,
        ),
        compiler_params=pltpu.CompilerParams(
            dimension_semantics=("arbitrary",) * len(grid), vmem_limit_bytes=limit * MIB
        ),
        cost_estimate=pl.CostEstimate(
            flops=int(cost[0]), bytes_accessed=int(cost[1]), transcendentals=0
        ),
    )


def sds(shape, dtype):
    return jax.ShapeDtypeStruct(shape, dtype)


def qkv_body(n, idx_ref, x_ref, gain_ref, cos_ref, sin_ref, *refs):
    parts, (qkv_ref, a1t_ref, whole) = refs[:n], refs[n:]

    @pl.when(pl.program_id(0) == 0)
    def _():
        assemble(idx_ref[0], parts, whole)

    width = x_ref.shape[1]
    scaled, _ = norm_rows(x_ref[...].astype(f32))
    a1 = (scaled * gain_ref[...].astype(f32)).astype(bf16)
    a1t_ref[...] = a1.T
    cosine, sine = cos_ref[...], sin_ref[...]
    for part in range(3):
        y = nn(a1, whole[:, part * width : (part + 1) * width])
        if part == 2:
            qkv_ref[:, part * width :] = y.astype(bf16)
            continue
        for t in range(width // PAIR):
            tile = y[:, t * PAIR : (t + 1) * PAIR]
            tile = tile * cosine + swap_halves(tile) * sine
            if part == 0:
                tile = tile * (LOG2E / 8.0)
            at = part * width + t * PAIR
            qkv_ref[:, at : at + PAIR] = tile.astype(bf16)


def qkv_call(index, x, gain, parts, cosine, sine):
    rows, width = x.shape
    n, wide = len(parts), parts[0].shape[1]
    step = 256
    per = cosine.shape[0] // step
    return call(
        functools.partial(qkv_body, n),
        "norm_qkv",
        (rows // step,),
        [
            pl.BlockSpec((step, width), lambda i, s: (i, 0)),
            fixed((1, width)),
            pl.BlockSpec((step, PAIR), lambda i, s: (i % per, 0)),
            pl.BlockSpec((step, PAIR), lambda i, s: (i % per, 0)),
        ]
        + [fixed(parts[0].shape)] * n,
        [
            pl.BlockSpec((step, wide), lambda i, s: (i, 0)),
            pl.BlockSpec((width, step), lambda i, s: (0, i)),
        ],
        [sds((rows, wide), bf16), sds((width, rows), bf16)],
        [pltpu.VMEM((width, wide), bf16)],
        24,
        (2 * rows * width * wide, 2 * width * wide + 2 * rows * (width * 2 + wide)),
    )(index, x, gain, cosine, sine, *parts)


def head_masks():
    lane = lax.broadcasted_iota(jnp.int32, (1, PAIR), 1)
    return lane < HEAD, lane >= HEAD


def att_body(seq, idx_ref, q_ref, k_ref, v_ref, same_ref, less_ref, upto_ref, o_ref, ot_ref, lse_ref):
    first, second = head_masks()
    k_all, v_all = k_ref[...], v_ref[...]
    keys = [jnp.where(m, k_all, jnp.zeros_like(k_all)) for m in (first, second)]
    vals = [jnp.where(m, v_all, jnp.ones_like(v_all)) for m in (first, second)]

    def finish(row, tops, outs):
        total = jnp.where(first, outs[1], outs[0])
        total = pltpu.roll(total, HEAD, 1)
        out = jnp.where(first, outs[0], outs[1]) / total
        low = out.astype(bf16)
        o_ref[row : row + TILE, :] = low
        ot_ref[:, row : row + TILE] = out.T.astype(bf16)
        lse = jnp.where(first, tops[0], tops[1]) + jnp.log2(total)
        lse = lse.T
        lse_ref[0, 0:1, row : row + TILE] = lse[0:1, :]
        lse_ref[0, 1:2, row : row + TILE] = lse[HEAD : HEAD + 1, :]

    for i in range(seq // TILE):
        lo, hi = i * TILE, (i + 1) * TILE
        for clean in (False, True):
            row = lo + seq if clean else lo
            query = q_ref[row : row + TILE, :]
            tops, outs = [], []
            for h in range(2):
                scores = nt(query, keys[h][seq : seq + hi])
                edge = scores[:, lo:hi] + (upto_ref if clean else less_ref)[...]
                pieces = [edge]
                if i > 0:
                    pieces.append(scores[:, :lo])
                if not clean:
                    pieces.append(nt(query, keys[h][lo:hi]) + same_ref[...])
                top = functools.reduce(
                    jnp.maximum, [jnp.max(p, axis=-1, keepdims=True) for p in pieces]
                )
                weights = [jnp.exp2(p - top).astype(bf16) for p in pieces]
                out = nn(weights[0], vals[h][seq + lo : seq + hi])
                if i > 0:
                    out = out + nn(weights[1], vals[h][seq : seq + lo])
                if not clean:
                    out = out + nn(weights[-1], vals[h][lo:hi])
                tops.append(top)
                outs.append(out)
            finish(row, tops, outs)


def att_call(index, qkv, masks):
    rows = qkv.shape[0]
    width = qkv.shape[1] // 3
    pairs = width // PAIR

    def column(part):
        return pl.BlockSpec((rows, PAIR), lambda p, s: (0, part * pairs + p))

    return call(
        functools.partial(att_body, rows // 2),
        "attention",
        (pairs,),
        [column(0), column(1), column(2)] + [fixed((TILE, TILE))] * 3,
        [
            pl.BlockSpec((rows, PAIR), lambda p, s: (0, p)),
            pl.BlockSpec((PAIR, rows), lambda p, s: (p, 0)),
            pl.BlockSpec((1, 2, rows), lambda p, s: (p, 0, 0)),
        ],
        [sds((rows, width), bf16), sds((width, rows), bf16), sds((pairs, 2, rows), f32)],
        [],
        16,
        (4 * rows * rows * width, 2 * rows * width * 5),
    )(index, qkv, qkv, qkv, *masks)


def att_back_body(
    seq, idx_ref, q_ref, k_ref, v_ref, do_ref, o_ref, lse_ref, same_ref, less_ref, upto_ref,
    cos_ref, sin_ref, dq_ref, dk_ref, dv_ref, dqt_ref,
):
    first, second = head_masks()
    q_all, k_all, v_all, do_all = q_ref[...], k_ref[...], v_ref[...], do_ref[...]

    def split(array):
        return [jnp.where(m, array, jnp.zeros_like(array)) for m in (first, second)]

    queries, keys, vals, dos = split(q_all), split(k_all), split(v_all), split(do_all)
    keys_t = k_all.T
    product = do_all.astype(f32) * o_ref[...].astype(f32)
    picked = lax.broadcasted_iota(jnp.int32, (8, PAIR), 0)
    picked = jnp.where(picked == lax.broadcasted_iota(jnp.int32, (8, PAIR), 1) // HEAD, 1.0, 0.0)
    delta = lax.dot_general(
        picked, product, (((1,), (1,)), ((), ())),
        precision=lax.Precision.HIGHEST, preferred_element_type=f32,
    )

    def block(h, key_lo, key_hi, q_lo, q_hi, mask_ref):
        scores = nt(keys[h][key_lo:key_hi], q_all[q_lo:q_hi])
        scores = scores - lse_ref[0, h : h + 1, q_lo:q_hi]
        edge = jnp.exp2(scores[:, :TILE] + mask_ref[...])
        d_probs = nt(vals[h][key_lo:key_hi], do_all[q_lo:q_hi]) - delta[h : h + 1, q_lo:q_hi]
        if q_hi - q_lo > TILE:
            probs = jnp.concatenate([edge, jnp.exp2(scores[:, TILE:])], axis=1)
        else:
            probs = edge
        d_scores = (probs * d_probs).astype(bf16)
        probs = probs.astype(bf16)
        d_vals = nn(probs, dos[h][q_lo:q_hi])
        d_keys = nn(d_scores, queries[h][q_lo:q_hi])
        d_query = nn(keys_t[h * HEAD : (h + 1) * HEAD, key_lo:key_hi], d_scores)
        return d_vals, d_keys, d_query

    def rotate_back(tile, rows):
        at = rows % seq
        cosine, sine = cos_ref[at : at + TILE, :], sin_ref[at : at + TILE, :]
        return tile * cosine - swap_halves(tile) * sine

    for j in range(seq // TILE):
        lo, hi = j * TILE, (j + 1) * TILE
        d_vals, d_keys = 0.0, 0.0
        for h in range(2):
            dv, dk, dq = block(h, lo, hi, lo, hi, same_ref)
            d_vals, d_keys = d_vals + dv, d_keys + dk
            at = slice(h * HEAD, (h + 1) * HEAD)
            if j == 0:
                dqt_ref[at, lo:hi] = dq
            else:
                dqt_ref[at, lo:hi] += dq
        dv_ref[lo:hi, :] = d_vals.astype(bf16)
        dk_ref[lo:hi, :] = rotate_back(d_keys * LN2, lo).astype(bf16)
        d_vals, d_keys = 0.0, 0.0
        for h in range(2):
            at = slice(h * HEAD, (h + 1) * HEAD)
            for clean in (False, True):
                base = seq if clean else 0
                dv, dk, dq = block(
                    h, seq + lo, seq + hi, base + lo, base + seq, upto_ref if clean else less_ref
                )
                d_vals, d_keys = d_vals + dv, d_keys + dk
                if j == 0 and clean:
                    dqt_ref[at, base : base + seq] = dq
                elif j == 0:
                    dqt_ref[at, base : base + TILE] += dq[:, :TILE]
                    dqt_ref[at, base + TILE : base + seq] = dq[:, TILE:]
                else:
                    dqt_ref[at, base + lo : base + seq] += dq
        dv_ref[seq + lo : seq + hi, :] = d_vals.astype(bf16)
        dk_ref[seq + lo : seq + hi, :] = rotate_back(d_keys * LN2, lo).astype(bf16)
    for r in range(0, 2 * seq, TILE):
        tile = dqt_ref[:, r : r + TILE].T * 0.125
        dq_ref[r : r + TILE, :] = rotate_back(tile, r).astype(bf16)


def att_back_call(index, qkv, d_o, o, lse, masks, cosine, sine, start, count):
    rows = qkv.shape[0]
    width = qkv.shape[1] // 3
    pairs = width // PAIR
    seq = rows // 2

    def column(part):
        return pl.BlockSpec((rows, PAIR), lambda p, s: (0, part * pairs + start + p))

    out = pl.BlockSpec((rows, PAIR), lambda p, s: (0, p))
    return call(
        functools.partial(att_back_body, seq),
        "attention_back",
        (count,),
        [column(0), column(1), column(2), column(0), column(0)]
        + [pl.BlockSpec((1, 2, rows), lambda p, s: (start + p, 0, 0))]
        + [fixed((TILE, TILE))] * 3
        + [fixed((seq, PAIR))] * 2,
        [out] * 3,
        [sds((rows, count * PAIR), bf16)] * 3,
        [pltpu.VMEM((PAIR, rows), f32)],
        20,
        (12 * rows * rows * count * PAIR, 2 * rows * count * PAIR * 8),
    )(index, qkv, qkv, qkv, d_o, o, lse, *masks, cosine, sine)


def up_body(n, idx_ref, x_ref, o_ref, gain_ref, bias_ref, *refs):
    outs, ups = refs[:n], refs[n : 2 * n]
    x1_ref, a2t_ref, h_ref, g_ref, w_out, w_up = refs[2 * n :]

    @pl.when(pl.program_id(0) == 0)
    def _():
        assemble(idx_ref[0], outs, w_out)
        assemble(idx_ref[0], ups, w_up)

    x1 = x_ref[...].astype(f32) + nn(o_ref[...], w_out[...])
    x1_ref[...] = x1
    scaled, _ = norm_rows(x1)
    a2 = (scaled * gain_ref[...].astype(f32)).astype(bf16)
    a2t_ref[...] = a2.T
    c0 = math.sqrt(2.0 / math.pi)
    c1 = c0 * 0.044715
    chunk = 512
    for at in range(0, w_up.shape[1], chunk):
        u = nn(a2, w_up[:, at : at + chunk]) + bias_ref[:, at : at + chunk].astype(f32)
        square = u * u
        t = jnp.tanh(u * (c1 * square + c0))
        half = 0.5 * t + 0.5
        h_ref[:, at : at + chunk] = (u * half).astype(bf16)
        slope = u * (1.5 * c1 * square + 0.5 * c0)
        g_ref[:, at : at + chunk] = (half + slope * (1.0 - t * t)).astype(bf16)


def up_call(index, x, o, gain, bias, outs, ups):
    rows, width = x.shape
    n, ff = len(outs), ups[0].shape[1]
    step = 256

    def row(cols):
        return pl.BlockSpec((step, cols), lambda i, s: (i, 0))

    return call(
        functools.partial(up_body, n),
        "feed_up",
        (rows // step,),
        [row(width), row(width), fixed((1, width)), fixed((1, ff))]
        + [fixed(outs[0].shape)] * n
        + [fixed(ups[0].shape)] * n,
        [row(width), pl.BlockSpec((width, step), lambda i, s: (0, i)), row(ff), row(ff)],
        [sds((rows, width), f32), sds((width, rows), bf16), sds((rows, ff), bf16), sds((rows, ff), bf16)],
        [pltpu.VMEM((width, width), bf16), pltpu.VMEM((width, ff), bf16)],
        32,
        (2 * rows * width * (width + ff), 2 * width * (width + ff) + rows * (10 * width + 4 * ff)),
    )(index, x, o, gain, bias, *outs, *ups)


def down_body(n, idx_ref, dy_ref, x1_ref, g_ref, gain_ref, *refs):
    downs, ups, outs = refs[:n], refs[n : 2 * n], refs[2 * n : 3 * n]
    du_ref, dx1_ref, dx1r_ref, do_ref, gup_ref, gwide_ref, w_down, w_up, w_out = refs[3 * n :]

    @pl.when(pl.program_id(0) == 0)
    def _():
        assemble(idx_ref[0], downs, w_down)
        assemble(idx_ref[0], ups, w_up)
        assemble(idx_ref[0], outs, w_out)
        gup_ref[...] = jnp.zeros_like(gup_ref)
        gwide_ref[...] = jnp.zeros_like(gwide_ref)

    low = dy_ref[...]
    d_y = low.astype(f32)
    chunk = 512
    d_a2 = 0.0
    for at in range(0, w_up.shape[1], chunk):
        d_u = nt(low, w_down[at : at + chunk, :]) * g_ref[:, at : at + chunk].astype(f32)
        gup_ref[:, at : at + chunk] += jnp.sum(d_u, axis=0, keepdims=True)
        d_u = d_u.astype(bf16)
        du_ref[:, at : at + chunk] = d_u
        d_a2 = d_a2 + nt(d_u, w_up[:, at : at + chunk])
    scaled, inverse = norm_rows(x1_ref[...])
    gwide_ref[0:1, :] += jnp.sum(d_a2 * scaled, axis=0, keepdims=True)
    gwide_ref[1:2, :] += jnp.sum(d_y, axis=0, keepdims=True)
    d_x1 = d_y + norm_back(d_a2, scaled, inverse, gain_ref[...].astype(f32))
    dx1_ref[...] = d_x1
    d_x1 = d_x1.astype(bf16)
    dx1r_ref[...] = d_x1
    do_ref[...] = nt(d_x1, w_out[...]).astype(bf16)


def down_call(index, d_y, x1, g, gain, downs, ups, outs):
    rows, width = d_y.shape
    n, ff = len(outs), ups[0].shape[1]
    step = 256

    def row(cols):
        return pl.BlockSpec((step, cols), lambda i, s: (i, 0))

    def whole(shape):
        return pl.BlockSpec(shape, lambda i, s: (0, 0))

    return call(
        functools.partial(down_body, n),
        "feed_back",
        (rows // step,),
        [row(width), row(width), row(ff), fixed((1, width))]
        + [fixed(downs[0].shape)] * n
        + [fixed(ups[0].shape)] * n
        + [fixed(outs[0].shape)] * n,
        [row(ff), row(width), row(width), row(width), whole((1, ff)), whole((8, width))],
        [
            sds((rows, ff), bf16), sds((rows, width), f32), sds((rows, width), bf16),
            sds((rows, width), bf16), sds((1, ff), f32), sds((8, width), f32),
        ],
        [pltpu.VMEM((ff, width), bf16), pltpu.VMEM((width, ff), bf16), pltpu.VMEM((width, width), bf16)],
        40,
        (2 * rows * width * (width + 2 * ff), 2 * width * (width + 2 * ff) + rows * (14 * width + 4 * ff)),
    )(index, d_y, x1, g, gain, *downs, *ups, *outs)


def grad_down_body(idx_ref, dyt_ref, h_ref, out_ref):
    out_ref[0] = nn(dyt_ref[...], h_ref[...]).astype(bf16)


def grad_down_call(index, dyt, h, offsets, shards):
    width, rows = dyt.shape
    cols = h.shape[1] // shards
    base, step = offsets
    return call(
        grad_down_body,
        "grad_down",
        (2,),
        [fixed((width, rows)), pl.BlockSpec((rows, cols), lambda i, s: (0, s[0] ^ (base + step * i)))],
        pl.BlockSpec((1, width, cols), lambda i, s: (i, 0, 0)),
        sds((2, width, cols), bf16),
        [],
        24,
        (4 * rows * width * cols, 2 * (width * rows + 2 * rows * cols + 2 * width * cols)),
    )(index, dyt, h)


def grad_up_body(chunks, idx_ref, a0_ref, a1_ref, o0_ref, o1_ref, du_ref, dx_ref, out_ref):
    rows = a0_ref.shape[0]

    def write(top, bottom, right):
        y = nn(jnp.concatenate([top[...], bottom[...]], axis=0), right[...]).astype(bf16)
        out_ref[0] = y[:rows]
        out_ref[1] = y[rows:]

    @pl.when(pl.program_id(0) < chunks)
    def _():
        write(a0_ref, a1_ref, du_ref)

    @pl.when(pl.program_id(0) == chunks)
    def _():
        write(o0_ref, o1_ref, dx_ref)


def grad_up_call(index, a2t, ot, d_u, dx1r, offsets, shards):
    width, rows = a2t.shape
    own = width // shards
    ff = d_u.shape[1]
    chunks = ff // width
    base, step = offsets

    def shard(j):
        return pl.BlockSpec((own, rows), lambda i, s: (s[0] ^ (base + step * j), 0), pipeline_mode=pl.Buffered(1))

    return call(
        functools.partial(grad_up_body, chunks),
        "grad_up_out",
        (chunks + 1,),
        [shard(0), shard(1), shard(0), shard(1)]
        + [
            pl.BlockSpec((rows, width), lambda i, s: (0, jnp.minimum(i, chunks - 1))),
            fixed((rows, width)),
        ],
        pl.BlockSpec((2, own, width), lambda i, s: (0, 0, i)),
        sds((2, own, ff + width), bf16),
        [],
        24,
        (4 * rows * own * (ff + width), 2 * (4 * own * rows + rows * (ff + width) + 2 * own * (ff + width))),
    )(index, a2t, a2t, ot, ot, d_u, dx1r)


def grad_qkv_body(idx_ref, a0_ref, a1_ref, dq_ref, dk_ref, dv_ref, out_ref):
    rows = a0_ref.shape[0]
    cols = dq_ref.shape[1]
    left = jnp.concatenate([a0_ref[...], a1_ref[...]], axis=0)
    for j, right in enumerate((dq_ref, dk_ref, dv_ref)):
        y = nn(left, right[...]).astype(bf16)
        out_ref[0, :, j * cols : (j + 1) * cols] = y[:rows]
        out_ref[1, :, j * cols : (j + 1) * cols] = y[rows:]


def grad_qkv_call(index, a1t, d_qkv, offsets, shards):
    width, rows = a1t.shape
    own = width // shards
    cols = d_qkv[0].shape[1]
    base, step = offsets

    def shard(j):
        return pl.BlockSpec((own, rows), lambda i, s: (s[0] ^ (base + step * j), 0), pipeline_mode=pl.Buffered(1))

    return call(
        grad_qkv_body,
        "grad_qkv",
        (1,),
        [shard(0), shard(1)] + [fixed((rows, cols))] * 3,
        fixed((2, own, 3 * cols)),
        sds((2, own, 3 * cols), bf16),
        [],
        24,
        (12 * rows * own * cols, 2 * (2 * own * rows + 3 * rows * cols + 6 * own * cols)),
    )(index, a1t, a1t, *d_qkv)


def input_body(n, groups, idx_ref, x_ref, dx1_ref, gain_ref, *refs):
    grads, parts = refs[: 3 * groups], refs[3 * groups : 3 * groups + n]
    dx_ref, gain_out, whole = refs[3 * groups + n :]

    @pl.when(pl.program_id(0) == 0)
    def _():
        assemble(idx_ref[0], parts, whole)
        gain_out[...] = jnp.zeros_like(gain_out)

    width = x_ref.shape[1]
    d_a1 = 0.0
    for part in range(3):
        at = part * width
        for g in range(groups):
            ref = grads[3 * g + part]
            cols = ref.shape[1]
            d_a1 = d_a1 + nt(ref[...], whole[:, at : at + cols])
            at += cols
    scaled, inverse = norm_rows(x_ref[...].astype(f32))
    gain_out[0:1, :] += jnp.sum(d_a1 * scaled, axis=0, keepdims=True)
    d_x = dx1_ref[...] + norm_back(d_a1, scaled, inverse, gain_ref[...].astype(f32))
    dx_ref[...] = d_x.astype(bf16)


def input_call(index, x, dx1, gain, d_groups, parts):
    rows, width = x.shape
    n = len(parts)
    step = 256

    def row(cols):
        return pl.BlockSpec((step, cols), lambda i, s: (i, 0))

    flat = [array for group in d_groups for array in group]
    return call(
        functools.partial(input_body, n, len(d_groups)),
        "grad_input",
        (rows // step,),
        [row(width), row(width), fixed((1, width))]
        + [row(array.shape[1]) for array in flat]
        + [fixed(parts[0].shape)] * n,
        [row(width), pl.BlockSpec((8, width), lambda i, s: (0, 0))],
        [sds((rows, width), bf16), sds((8, width), f32)],
        [pltpu.VMEM((width, 3 * width), bf16)],
        24,
        (6 * rows * width * width, 6 * width * width + rows * width * 14),
    )(index, x, dx1, gain, *flat, *parts)


def output_body(n, idx_ref, x1_ref, h_ref, bias_ref, *refs):
    parts, (out_ref, whole) = refs[:n], refs[n:]

    @pl.when(pl.program_id(0) == 0)
    def _():
        assemble(idx_ref[0], parts, whole)

    y = x1_ref[...] + nn(h_ref[...], whole[...]) + bias_ref[...].astype(f32)
    out_ref[...] = y.astype(bf16)


def output_call(index, x1, h, bias, parts):
    rows, width = x1.shape
    n, ff = len(parts), h.shape[1]
    step = 256

    def row(cols):
        return pl.BlockSpec((step, cols), lambda i, s: (i, 0))

    return call(
        functools.partial(output_body, n),
        "layer_output",
        (rows // step,),
        [row(width), row(ff), fixed((1, width))] + [fixed(parts[0].shape)] * n,
        row(width),
        sds((rows, width), bf16),
        [pltpu.VMEM((ff, width), bf16)],
        24,
        (2 * rows * width * ff, 2 * width * ff + rows * (6 * width + 2 * ff)),
    )(index, x1, h, bias, *parts)


class Moves:
    def __init__(self, narrow, wide):
        self.narrow, self.wide = narrow, wide
        self.n = lax.axis_index("narrow")
        self.w = lax.axis_index("wide")

    def swap(self, value, axis, bit):
        size = self.narrow if axis == "narrow" else self.wide
        return lax.ppermute(value, axis, [(i, i ^ bit) for i in range(size)])

    def gather(self, shard):
        parts = [shard]
        bit = self.narrow // 2
        order = []
        while bit:
            order.append(bit)
            bit //= 2
        found = {0: shard}
        for bit in order:
            for j in list(found):
                found[j ^ bit] = self.swap(found[j], "narrow", bit)
        return [found[j] for j in range(self.narrow)]

    def canonical(self, parts):
        out = []
        for k in range(self.narrow):
            value = parts[k]
            for j in range(1, self.narrow):
                value = jnp.where(self.n == j, parts[k ^ j], value)
            out.append(value)
        return out

    def halves(self, value, bit):
        rows = value.shape[0] // 2
        mine = ((self.w // bit) % 2) * rows
        keep = lax.dynamic_slice_in_dim(value, mine, rows, 0)
        send = lax.dynamic_slice_in_dim(value, rows - mine, rows, 0)
        return keep, send

    def join(self, mine, other, bit):
        low = (self.w // bit) % 2 == 0
        return jnp.concatenate([jnp.where(low, mine, other), jnp.where(low, other, mine)], axis=0)

    def reduce(self, send, keep):
        got = self.swap(send, "narrow", 1)
        total = keep.astype(f32) + got.astype(f32)
        got = self.swap(total[1].astype(bf16), "narrow", 2)
        total = total[0] + got.astype(f32)
        split, bit = [], 1
        while bit < self.wide:
            if len(split) < 2 and total.shape[0] % 32 == 0 and 2 * bit < self.wide:
                keep, send = self.halves(total, bit)
                got = self.swap(send.astype(bf16), "wide", bit)
                total = keep + got.astype(f32)
                split.append(bit)
            else:
                mine = total.astype(bf16)
                got = self.swap(mine, "wide", bit)
                total = mine.astype(f32) + got.astype(f32)
            bit *= 2
        total = total.astype(bf16)
        for bit in reversed(split):
            total = self.join(total, self.swap(total, "wide", bit), bit)
        return total

    def everywhere(self, value):
        bit = 1
        while bit < self.narrow:
            value = value + self.swap(value, "narrow", bit)
            bit *= 2
        bit = 1
        while bit < self.wide:
            value = value + self.swap(value, "wide", bit)
            bit *= 2
        return value

    def own(self, vector):
        size = vector.shape[0] // self.narrow
        return lax.dynamic_slice_in_dim(vector, self.n * size, size, 0)


def shards(narrow, wide, layer_input, cotangent, block_size, gain_attn, w_qkv, w_out, gain_mlp, w_up, b_up, w_down, b_down):
    moves = Moves(narrow, wide)
    index = moves.n.astype(jnp.int32).reshape(1)
    x, d_y = layer_input[0], cotangent[0]
    rows, width = x.shape
    seq = rows // 2
    pairs = width // PAIR

    small = jnp.concatenate([gain_attn, gain_mlp, b_up, b_down])
    small_parts = [small] + [
        lax.ppermute(small, "narrow", [(i, i ^ j) for i in range(narrow)]) for j in range(1, narrow)
    ]
    qkv_parts = moves.gather(w_qkv)
    out_parts = moves.gather(w_out)
    up_parts = moves.gather(w_up)
    down_parts = moves.gather(w_down)
    small_parts = moves.canonical(small_parts)
    vectors, at = [], 0
    for piece in (gain_attn, gain_mlp, b_up, b_down):
        size = piece.shape[0]
        vectors.append(jnp.concatenate([part[at : at + size] for part in small_parts]).reshape(1, -1))
        at += size
    g_attn, g_mlp, up_bias, down_bias = vectors

    half = HEAD // 2
    freq = 10000.0 ** (-jnp.arange(half).astype(f32) / half)
    angles = jnp.arange(seq).astype(f32)[:, None] * freq[None, :]
    cosine, sine = jnp.cos(angles), jnp.sin(angles)
    cosine = jnp.tile(cosine, (1, 4))
    sine = jnp.concatenate([-sine, sine, -sine, sine], axis=1)
    block = jnp.arange(TILE, dtype=jnp.int32) // block_size[0]
    row_block, col_block = block[:, None], block[None, :]
    masks = [
        jnp.where(ok, 0.0, -1e30).astype(f32)
        for ok in (
            row_block == col_block, col_block < row_block, col_block <= row_block,
            row_block < col_block, row_block <= col_block,
        )
    ]
    same, less, upto, less_t, upto_t = masks
    dyt = d_y.T

    qkv, a1t = qkv_call(index, x, g_attn, qkv_parts, cosine, sine)
    o, ot, lse = att_call(index, qkv, (same, less, upto))
    x1, a2t, h, g = up_call(index, x, o, g_mlp, up_bias, out_parts, up_parts)
    send = grad_down_call(index, dyt, h, (1, 2), narrow)
    keep = grad_down_call(index, dyt, h, (0, 2), narrow)
    total_down = moves.reduce(send, keep)
    d_u, dx1, dx1r, d_o, g_up, g_wide = down_call(index, d_y, x1, g, g_mlp, down_parts, up_parts, out_parts)
    send = grad_up_call(index, a2t, ot, d_u, dx1r, (1, 2), narrow)
    keep = grad_up_call(index, a2t, ot, d_u, dx1r, (0, 2), narrow)
    total_up = moves.reduce(send, keep)
    groups, totals = [], []
    count = pairs // 2
    for start in range(0, pairs, count):
        group = att_back_call(index, qkv, d_o, o, lse, (same, less_t, upto_t), cosine, sine, start, count)
        send = grad_qkv_call(index, a1t, group, (1, 2), narrow)
        keep = grad_qkv_call(index, a1t, group, (0, 2), narrow)
        totals.append(moves.reduce(send, keep))
        groups.append(group)
    d_input, g_attn_rows = input_call(index, x, dx1, g_attn, groups, qkv_parts)
    output = output_call(index, x1, h, down_bias, down_parts)

    sums = jnp.concatenate([g_attn_rows[0], g_wide[0], g_up[0], g_wide[1]])
    sums = moves.everywhere(sums.reshape(-1, TILE)).reshape(-1)
    grads, at = [], 0
    for size in (width, width, g_up.shape[1], width):
        grads.append(moves.own(sums[at : at + size]))
        at += size
    cols = count * PAIR
    grad_qkv = jnp.concatenate(
        [total[:, j * cols : (j + 1) * cols] for j in range(3) for total in totals], axis=1
    ).astype(f32)
    ff = w_up.shape[1]
    return (
        output[None],
        d_input[None],
        grads[0],
        grad_qkv,
        total_up[:, ff:].astype(f32),
        grads[1],
        total_up[:, :ff].astype(f32),
        grads[2],
        total_down.T.astype(f32),
        grads[3],
    )


def solution(mesh):
    return jax.shard_map(
        functools.partial(shards, mesh.shape["narrow"], mesh.shape["wide"]),
        mesh=mesh,
        in_specs=(
            P(("wide", "narrow"), None, None),
            P(("wide", "narrow"), None, None),
            P(("wide", "narrow")),
            P("narrow"),
            P("narrow", None),
            P("narrow", None),
            P("narrow"),
            P("narrow", None),
            P("narrow"),
            P("narrow", None),
            P("narrow"),
        ),
        out_specs=(
            P(("wide", "narrow"), None, None),
            P(("wide", "narrow"), None, None),
            P("narrow"),
            P("narrow", None),
            P("narrow", None),
            P("narrow"),
            P("narrow", None),
            P("narrow"),
            P("narrow", None),
            P("narrow"),
        ),
        check_vma=False,
    )
```

```python
import functools
import math

import jax
import jax.numpy as jnp
from jax import lax
from jax.experimental import pallas as pl
from jax.experimental.pallas import tpu as pltpu
from jax.sharding import PartitionSpec as P

HEAD = 64
PAIR = 2 * HEAD
TILE = 128
SPAN = 256
LOG2E = 1.4426950408889634
LN2 = 0.6931471805599453
f32 = jnp.float32
bf16 = jnp.bfloat16
MIB = 1 << 20


def nn(left, right):
    return jnp.dot(left, right, preferred_element_type=f32)


def nt(left, right):
    return lax.dot_general(left, right, (((1,), (1,)), ((), ())), preferred_element_type=f32)


def norm_rows(values):
    centre = values - jnp.mean(values, axis=-1, keepdims=True)
    inverse = lax.rsqrt(jnp.mean(centre * centre, axis=-1, keepdims=True) + 1e-05)
    return centre * inverse, inverse


def norm_back(d_norm, scaled, inverse, gain):
    d_scaled = d_norm * gain
    return inverse * (
        d_scaled
        - jnp.mean(d_scaled, axis=-1, keepdims=True)
        - scaled * jnp.mean(d_scaled * scaled, axis=-1, keepdims=True)
    )


def swap_halves(tile):
    lane = lax.broadcasted_iota(jnp.int32, (1, PAIR), 1) % HEAD
    return jnp.where(
        lane < HEAD // 2,
        pltpu.roll(tile, PAIR - HEAD // 2, 1),
        pltpu.roll(tile, HEAD // 2, 1),
    )


class Weight:
    def __init__(self, pieces):
        self.arrays = [array for array, _, _ in pieces]
        self.plan = [(rows, place) for _, rows, place in pieces]
        self.rows = sum(rows for rows, _ in self.plan)
        self.cols = self.arrays[0].shape[1]

    def specs(self):
        return [pl.BlockSpec(memory_space=pltpu.HBM)] * len(self.plan)

    def whole(self):
        return pltpu.VMEM((self.rows, self.cols), bf16)

    def sems(self):
        return [pltpu.SemaphoreType.DMA((len(self.plan),))]

    def scratch(self):
        return [pltpu.VMEM((self.rows, self.cols), bf16), pltpu.SemaphoreType.DMA((len(self.plan),))]


def fetches(at_ref, plan, parts, whole, sems):
    copies = []
    for i, ((rows, place), part) in enumerate(zip(plan, parts)):
        start = pl.multiple_of(at_ref[place], math.gcd(rows, 256))
        copies.append(pltpu.make_async_copy(part.at[pl.ds(0, rows)], whole.at[pl.ds(start, rows)], sems.at[i]))
    return copies


def fetch(at_ref, *weights):
    @pl.when(pl.program_id(0) == 0)
    def _():
        for weight in weights:
            for copy in fetches(at_ref, *weight):
                copy.start()


def arrive(at_ref, weight):
    @pl.when(pl.program_id(0) == 0)
    def _():
        for copy in fetches(at_ref, *weight):
            copy.wait()


def step_rows(step):
    return pl.ds(pl.multiple_of(pl.program_id(0) * step, step), step)


def take(refs, *groups):
    out, at = [], 0
    for group in groups:
        out.append(refs[at : at + len(group)])
        at += len(group)
    return out + [refs[at:]]


def fixed(shape):
    return pl.BlockSpec(shape, lambda *_: (0,) * len(shape), pipeline_mode=pl.Buffered(1))


def call(body, name, grid, in_specs, out_specs, out_shape, scratch, limit, cost, near=(), aliases=None, moved=1 << 20):
    fun = pl.pallas_call(
        body,
        name=name,
        out_shape=out_shape,
        input_output_aliases=aliases or {},
        grid_spec=pltpu.PrefetchScalarGridSpec(
            num_scalar_prefetch=1,
            grid=grid,
            in_specs=in_specs,
            out_specs=out_specs,
            scratch_shapes=scratch,
        ),
        compiler_params=pltpu.CompilerParams(
            dimension_semantics=("arbitrary",) * len(grid), vmem_limit_bytes=limit * MIB
        ),
        cost_estimate=pl.CostEstimate(
            flops=int(cost * 1e12), bytes_accessed=moved, transcendentals=0
        ),
    )

    def run(index, *args):
        args = [
            pltpu.with_memory_space_constraint(arg, pltpu.VMEM if i in near else pltpu.HBM)
            for i, arg in enumerate(args)
        ]
        return fun(index, *args)

    return run


def hbm(shape, dtype):
    return pltpu.HBM(shape, dtype)


def vmem(shape, dtype):
    return pltpu.VMEM(shape, dtype)


def sds(shape, dtype):
    return jax.ShapeDtypeStruct(shape, dtype)


def first_body(idx_ref, w_ref, gain1_ref, gain2_ref, down_ref, up_ref, first_ref, second_ref, near_ref):
    rows, cols = w_ref.shape
    size = rows // 3

    def lanes(*refs):
        values = [ref[...].astype(f32).reshape(1, -1) for ref in refs]
        return jnp.concatenate(
            [v for v in values for _ in range(cols // (len(refs) * v.shape[1]))], axis=1
        )

    row = lax.broadcasted_iota(jnp.int32, (8, cols), 0)
    small = jnp.where(row == 0, lanes(gain1_ref, gain2_ref, down_ref), lanes(up_ref)).astype(bf16)
    start = pl.multiple_of(idx_ref[1] * size, math.gcd(size, 256))
    first_ref[:size, :] = w_ref[pl.ds(start, size), :]
    first_ref[size:, :] = small
    second_ref[...] = w_ref[2 * size :, :]
    near_ref[:rows, :] = w_ref[...]
    near_ref[rows:, :] = small


def first_call(index, w_qkv, gain1, gain2, down, up):
    rows, cols = w_qkv.shape
    size = rows // 3
    shapes = [(size + 8, cols), (size, cols), (rows + 8, cols)]
    return call(
        first_body,
        "first_messages",
        (1,),
        [fixed(array.shape) for array in (w_qkv, gain1, gain2, down, up)],
        [fixed(shape) for shape in shapes],
        [sds(shape, bf16) for shape in shapes],
        [],
        8,
        1.5,
    )(index, w_qkv, gain1, gain2, down, up)


def qkv_body(plan, n, idx_ref, x_ref, cos_ref, sin_ref, *refs):
    smalls, parts, refs = take(refs, range(n), plan)
    qkv_ref, a1t_ref, vec_ref, whole, sems = refs
    weight = (plan, parts, whole, sems)
    fetch(idx_ref, weight)
    width = x_ref.shape[1]

    @pl.when(pl.program_id(0) == 0)
    def _():
        lane = lax.broadcasted_iota(jnp.int32, (1, width), 1) // (width // n)
        values = [ref[...].astype(f32) for ref in smalls]
        vec_ref[...] = jnp.zeros_like(vec_ref)
        for i in range(3):
            vec_ref[i : i + 1, :width] = sum(
                jnp.where(lane == (idx_ref[0] ^ j), v[0:1, i * width : (i + 1) * width], 0.0)
                for j, v in enumerate(values)
            )
        size = vec_ref.shape[1] // n
        for c in range(n):
            vec_ref[3:4, c * size : (c + 1) * size] = sum(
                jnp.where((idx_ref[0] ^ j) == c, v[1:2, :size], 0.0) for j, v in enumerate(values)
            )

    scaled, _ = norm_rows(x_ref[...].astype(f32))
    a1 = (scaled * vec_ref[0:1, :width]).astype(bf16)
    a1t_ref[...] = a1.T
    cosine, sine = cos_ref[...], sin_ref[...]
    arrive(idx_ref, weight)
    for part in range(3):
        y = nn(a1, whole[:, part * width : (part + 1) * width])
        if part == 2:
            qkv_ref[:, part * width :] = y.astype(bf16)
            continue
        for t in range(width // PAIR):
            tile = y[:, t * PAIR : (t + 1) * PAIR]
            tile = tile * cosine + swap_halves(tile) * sine
            if part == 0:
                tile = tile * (LOG2E / 8.0)
            at = part * width + t * PAIR
            qkv_ref[:, at : at + PAIR] = tile.astype(bf16)


def qkv_call(index, x, weight, smalls, ff, cosine, sine):
    rows, width = x.shape
    wide = weight.cols
    step = 256
    per = cosine.shape[0] // step

    def vector(array):
        return pl.BlockSpec((8, wide), lambda i, s: (array.shape[0] // 8 - 1, 0))

    return call(
        functools.partial(qkv_body, weight.plan, len(smalls)),
        "norm_qkv",
        (rows // step,),
        [
            pl.BlockSpec((step, width), lambda i, s: (i, 0)),
            pl.BlockSpec((step, PAIR), lambda i, s: (i % per, 0)),
            pl.BlockSpec((step, PAIR), lambda i, s: (i % per, 0)),
        ]
        + [vector(array) for array in smalls]
        + weight.specs(),
        [
            pl.BlockSpec((step, wide), lambda i, s: (i, 0)),
            pl.BlockSpec((width, step), lambda i, s: (0, i)),
            pl.BlockSpec((8, ff), lambda i, s: (0, 0)),
        ],
        [hbm((rows, wide), bf16), hbm((width, rows), bf16), hbm((8, ff), f32)],
        weight.scratch(),
        14,
        7,
    )(index, x, cosine, sine, *smalls, *weight.arrays)


def head_masks():
    lane = lax.broadcasted_iota(jnp.int32, (1, PAIR), 1)
    return lane < HEAD, lane >= HEAD


def widen(tile, allowed):
    count = SPAN // TILE
    never = jnp.full(tile.shape, -1e30, f32)
    before = jnp.zeros(tile.shape, f32) if allowed else never
    return jnp.concatenate(
        [
            jnp.concatenate([tile if a == b else (before if a < b else never) for b in range(count)], axis=1)
            for a in range(count)
        ],
        axis=0,
    )


def att_body(seq, idx_ref, q_ref, k_ref, v_ref, same_ref, less_ref, upto_ref, *refs):
    o_ref, ot_ref, lse_ref = refs[-3:]
    k_all = k_ref[...]
    keys = [jnp.where(m, k_all, jnp.zeros_like(k_all)) for m in head_masks()]
    v_t = v_ref[...].T
    ones = jnp.ones((16, 2 * seq), bf16)
    vals = [jnp.concatenate([v_t[h * HEAD : (h + 1) * HEAD], ones], axis=0) for h in range(2)]
    same, less, upto = widen(same_ref[...], False), widen(less_ref[...], True), widen(upto_ref[...], True)

    def scores(lo, clean, h):
        hi = lo + SPAN
        row = lo + seq if clean else lo
        query = q_ref[row : row + SPAN, :]
        pieces = [nt(keys[h][seq + lo : seq + hi], query) + (upto if clean else less)]
        if lo > 0:
            pieces.append(nt(keys[h][seq : seq + lo], query))
        if not clean:
            pieces.append(nt(keys[h][lo:hi], query) + same)
        return pieces

    def soften(pieces):
        top = functools.reduce(jnp.maximum, [jnp.max(p, axis=0, keepdims=True) for p in pieces])
        return top, [jnp.exp2(p - top).astype(bf16) for p in pieces]

    def mix(lo, clean, h, weights):
        hi = lo + SPAN
        out = nn(vals[h][:, seq + lo : seq + hi], weights[0])
        if lo > 0:
            out = out + nn(vals[h][:, seq : seq + lo], weights[1])
        if not clean:
            out = out + nn(vals[h][:, lo:hi], weights[-1])
        return out

    def finish(lo, clean, softened):
        row = lo + seq if clean else lo
        outs = [mix(lo, clean, h, softened[h][1]) for h in range(2)]
        out = jnp.concatenate([o[:HEAD] / o[HEAD : HEAD + 1] for o in outs], axis=0)
        ot_ref[:, row : row + SPAN] = out.astype(bf16)
        o_ref[row : row + SPAN, :] = out.T.astype(bf16)
        for h in range(2):
            lse_ref[0, h : h + 1, row : row + SPAN] = softened[h][0] + jnp.log2(outs[h][HEAD : HEAD + 1])

    work = [(lo, clean) for lo in range(0, seq, SPAN) for clean in (False, True)]
    ahead = [scores(*work[0], h) for h in range(2)]
    behind = None
    for i, item in enumerate(work):
        now = ahead
        if i + 1 < len(work):
            ahead = [scores(*work[i + 1], h) for h in range(2)]
        softened = [soften(pieces) for pieces in now]
        if behind is not None:
            finish(*behind)
        behind = (*item, softened)
    finish(*behind)


def att_call(index, qkv, masks, start, count, held=()):
    rows = qkv.shape[0]
    width = qkv.shape[1] // 3
    pairs = width // PAIR

    def column(part):
        return pl.BlockSpec((rows, PAIR), lambda p, s: (0, part * pairs + start + p))

    return call(
        functools.partial(att_body, rows // 2),
        "attention",
        (count,),
        [column(0), column(1), column(2)] + [fixed((TILE, TILE))] * 3
        + [pl.BlockSpec(memory_space=pltpu.HBM)] * len(held),
        [
            pl.BlockSpec((rows, PAIR), lambda p, s: (0, start + p)),
            pl.BlockSpec((PAIR, rows), lambda p, s: (start + p, 0)),
            pl.BlockSpec((1, 2, rows), lambda p, s: (start + p, 0, 0)),
        ],
        [hbm((rows, width), bf16), hbm((width, rows), bf16), hbm((pairs, 2, rows), f32)],
        [],
        20,
        2.0 * count,
        aliases={7 + i: i for i in range(len(held))},
    )(index, qkv, qkv, qkv, *masks, *held)


def att_back_body(
    seq, idx_ref, q_ref, k_ref, v_ref, do_ref, o_ref, lse_ref, same_ref, less_ref, upto_ref,
    cos_ref, sin_ref, dq_ref, dk_ref, dv_ref, dqt_ref,
):
    first, second = head_masks()
    q_all, k_all, v_all, do_all = q_ref[...], k_ref[...], v_ref[...], do_ref[...]

    def split(array):
        return [jnp.where(m, array, jnp.zeros_like(array)) for m in (first, second)]

    queries, keys, vals, dos = split(q_all), split(k_all), split(v_all), split(do_all)
    keys_t = k_all.T
    product = do_all.astype(f32) * o_ref[...].astype(f32)
    high = product.astype(bf16)
    rest = (product - high.astype(f32)).astype(bf16)
    picked = lax.broadcasted_iota(jnp.int32, (8, PAIR), 0)
    picked = jnp.where(picked == lax.broadcasted_iota(jnp.int32, (8, PAIR), 1) // HEAD, 1.0, 0.0).astype(bf16)
    delta = nt(picked, high) + nt(picked, rest)
    same, less, upto = widen(same_ref[...], False), widen(less_ref[...], True), widen(upto_ref[...], True)
    dqt_ref[...] = jnp.zeros_like(dqt_ref)

    def products(unit):
        return [
            (nt(keys[h][k : k + SPAN], q_all[q:end]), nt(vals[h][k : k + SPAN], do_all[q:end]))
            for h, k, q, end, _ in unit[0]
        ]

    def soften(unit, values):
        out = []
        for (h, _, q, end, mask), (scores, d_probs) in zip(unit[0], values):
            scores = scores - lse_ref[0, h : h + 1, q:end]
            probs = jnp.exp2(scores[:, :SPAN] + mask)
            if end - q > SPAN:
                probs = jnp.concatenate([probs, jnp.exp2(scores[:, SPAN:])], axis=1)
            d_scores = probs * (d_probs - delta[h : h + 1, q:end])
            out.append((probs.astype(bf16), d_scores.astype(bf16)))
        return out

    def rotate_back(tile, row):
        at = row % seq
        cosine, sine = cos_ref[at : at + SPAN, :], sin_ref[at : at + SPAN, :]
        return tile * cosine - swap_halves(tile) * sine

    def gather(unit, values, sums):
        items, last = unit
        d_vals, d_keys = sums
        for (h, k, q, end, _), (probs, d_scores) in zip(items, values):
            d_vals = d_vals + nn(probs, dos[h][q:end])
            d_keys = d_keys + nn(d_scores, queries[h][q:end])
            at = slice(h * HEAD, (h + 1) * HEAD)
            dqt_ref[at, q:end] += nn(keys_t[at, k : k + SPAN], d_scores)
        if not last:
            return d_vals, d_keys
        k = items[0][1]
        dv_ref[k : k + SPAN, :] = d_vals.astype(bf16)
        dk_ref[k : k + SPAN, :] = rotate_back(d_keys * LN2, k).astype(bf16)
        return 0.0, 0.0

    units = []
    for lo in range(0, seq, SPAN):
        units.append(([(h, lo, lo, lo + SPAN, same) for h in range(2)], True))
        for base, mask in ((0, less), (seq, upto)):
            units.append(([(h, seq + lo, base + lo, base + seq, mask) for h in range(2)], base > 0))
    ahead, behind, sums = products(units[0]), None, (0.0, 0.0)
    for i, unit in enumerate(units):
        now = ahead
        if i + 1 < len(units):
            ahead = products(units[i + 1])
        values = soften(unit, now)
        if behind is not None:
            sums = gather(*behind, sums)
        behind = (unit, values)
    gather(*behind, sums)
    for r in range(0, 2 * seq, SPAN):
        tile = dqt_ref[:, r : r + SPAN].T * 0.125
        dq_ref[r : r + SPAN, :] = rotate_back(tile, r).astype(bf16)


def att_back_call(index, qkv, d_o, o, lse, masks, cosine, sine, start, count):
    rows = qkv.shape[0]
    width = qkv.shape[1] // 3
    pairs = width // PAIR
    seq = rows // 2

    def column(part):
        return pl.BlockSpec((rows, PAIR), lambda p, s: (0, part * pairs + start + p))

    out = pl.BlockSpec((rows, PAIR), lambda p, s: (0, p))
    return call(
        functools.partial(att_back_body, seq),
        "attention_back",
        (count,),
        [column(0), column(1), column(2), column(0), column(0)]
        + [pl.BlockSpec((1, 2, rows), lambda p, s: (start + p, 0, 0))]
        + [fixed((TILE, TILE))] * 3
        + [fixed((seq, PAIR))] * 2,
        [out] * 3,
        [vmem((rows, count * PAIR), bf16)] * 3,
        [pltpu.VMEM((PAIR, rows), f32)],
        20,
        3.6 * count,
    )(index, qkv, qkv, qkv, d_o, o, lse, *masks, cosine, sine)


def up_body(out_at, up_at, idx_ref, x_ref, o_ref, vec_ref, *refs):
    outs, ups, refs = take(refs, out_at, up_at)
    x1_ref, a2t_ref, h_ref, g_ref, w_out, w_up, out_sems, up_sems = refs
    out_weight, up_weight = (out_at, outs, w_out, out_sems), (up_at, ups, w_up, up_sems)
    fetch(idx_ref, out_weight, up_weight)
    arrive(idx_ref, out_weight)
    width = x_ref.shape[1]
    here = step_rows(x_ref.shape[0])
    x1 = x_ref[...].astype(f32) + nn(o_ref[...], w_out[...])
    x1_ref[here, :] = x1
    scaled, _ = norm_rows(x1)
    a2 = (scaled * vec_ref[1:2, :width]).astype(bf16)
    a2t_ref[:, here] = a2.T
    arrive(idx_ref, up_weight)
    c0 = math.sqrt(2.0 / math.pi)
    c1 = c0 * 0.044715
    chunk = 512
    for at in range(0, w_up.shape[1], chunk):
        u = nn(a2, w_up[:, at : at + chunk]) + vec_ref[3:4, at : at + chunk]
        square = u * u
        t = jnp.tanh(u * (c1 * square + c0))
        half = 0.5 * t + 0.5
        h_ref[here, at : at + chunk] = (u * half).astype(bf16)
        slope = u * (1.5 * c1 * square + 0.5 * c0)
        g_ref[here, at : at + chunk] = (half + slope * (1.0 - t * t)).astype(bf16)


def up_call(index, x, o, vec, w_out, w_up):
    rows, width = x.shape
    ff = w_up.cols
    step = 256

    def row(cols):
        return pl.BlockSpec((step, cols), lambda i, s: (i, 0))

    outs = [
        vmem((rows, width), f32), vmem((width, rows), bf16), vmem((rows, ff), bf16), vmem((rows, ff), bf16),
        w_out.whole(), w_up.whole(),
    ]
    return call(
        functools.partial(up_body, w_out.plan, w_up.plan),
        "feed_up",
        (rows // step,),
        [row(width), row(width), fixed(vec.shape)] + w_out.specs() + w_up.specs(),
        [fixed(out.shape) for out in outs],
        outs,
        w_out.sems() + w_up.sems(),
        8,
        18,
    )(index, x, o, vec, *w_out.arrays, *w_up.arrays)


def down_body(down_at, idx_ref, dy_ref, x1_ref, g_ref, vec_ref, w_up, w_out, *refs):
    downs, refs = take(refs, down_at)
    du_ref, dx1_ref, dx1r_ref, do_ref, bias_ref, w_down, down_sems = refs
    weight = (down_at, downs, w_down, down_sems)
    fetch(idx_ref, weight)

    @pl.when(pl.program_id(0) == 0)
    def _():
        bias_ref[...] = jnp.zeros_like(bias_ref)

    width = dy_ref.shape[1]
    here = step_rows(dy_ref.shape[0])
    low = dy_ref[...]
    d_y = low.astype(f32)
    bias_ref[1:2, :width] += jnp.sum(d_y, axis=0, keepdims=True)
    arrive(idx_ref, weight)
    chunk = 512
    d_a2 = 0.0
    for at in range(0, w_up.shape[1], chunk):
        d_u = nt(low, w_down[at : at + chunk, :]) * g_ref[here, at : at + chunk].astype(f32)
        bias_ref[0:1, at : at + chunk] += jnp.sum(d_u, axis=0, keepdims=True)
        d_u = d_u.astype(bf16)
        du_ref[here, at : at + chunk] = d_u
        d_a2 = d_a2 + nt(d_u, w_up[:, at : at + chunk])
    scaled, inverse = norm_rows(x1_ref[here, :])
    d_x1 = d_y + norm_back(d_a2, scaled, inverse, vec_ref[1:2, :width])
    dx1_ref[here, :] = d_x1
    d_x1 = d_x1.astype(bf16)
    dx1r_ref[here, :] = d_x1
    do_ref[...] = nt(d_x1, w_out[...]).astype(bf16)


def down_call(index, d_y, x1, g, vec, w_up, w_out, w_down):
    rows, width = d_y.shape
    ff = w_up.shape[1]
    step = 256

    def row(cols):
        return pl.BlockSpec((step, cols), lambda i, s: (i, 0))

    return call(
        functools.partial(down_body, w_down.plan),
        "feed_back",
        (rows // step,),
        [row(width)] + [fixed(array.shape) for array in (x1, g, vec, w_up, w_out)] + w_down.specs(),
        [fixed((rows, ff)), fixed((rows, width)), fixed((rows, width)), row(width), fixed((2, ff)),
         fixed((ff, width))],
        [
            vmem((rows, ff), bf16), vmem((rows, width), f32), vmem((rows, width), bf16),
            hbm((rows, width), bf16), vmem((2, ff), f32), w_down.whole(),
        ],
        w_down.sems(),
        10,
        20,
        near=(1, 2, 4, 5),
    )(index, d_y, x1, g, vec, w_up, w_out, *w_down.arrays)


def grad_down_body(offsets, idx_ref, dyt_ref, h_ref, out_ref):
    base, step = offsets
    cols = out_ref.shape[2]
    shard = idx_ref[0] ^ (base + step * pl.program_id(0))
    columns = pl.ds(pl.multiple_of(shard * cols, cols), cols)
    out_ref[pl.program_id(0)] = nn(dyt_ref[...], h_ref[:, columns]).astype(bf16)


def grad_down_call(index, dyt, h, offsets, shards):
    width, rows = dyt.shape
    cols = h.shape[1] // shards
    return call(
        functools.partial(grad_down_body, offsets),
        "grad_down",
        (2,),
        [fixed(dyt.shape), fixed(h.shape)],
        fixed((2, width, cols)),
        vmem((2, width, cols), bf16),
        [],
        6,
        3,
        near=(0, 1),
    )(index, dyt, h)


def shard_rows(idx_ref, offsets, rows):
    base, step = offsets
    return [
        pl.ds(pl.multiple_of((idx_ref[0] ^ (base + step * j)) * rows, math.gcd(rows, 256)), rows) for j in range(2)
    ]


def grad_up_body(chunks, offsets, idx_ref, a_ref, o_ref, du_ref, dx_ref, bias_ref, out_ref):
    rows = out_ref.shape[1]
    width = dx_ref.shape[1]
    i = pl.program_id(0)
    columns = pl.ds(pl.multiple_of(i * width, width), width)
    shards_at = shard_rows(idx_ref, offsets, rows)

    def write(left, right):
        y = nn(jnp.concatenate([left[at, :] for at in shards_at], axis=0), right).astype(bf16)
        out_ref[0, :, columns] = y[:rows]
        out_ref[1, :, columns] = y[rows:]

    @pl.when(i < chunks)
    def _():
        write(a_ref, du_ref[:, columns])

    @pl.when(i == chunks)
    def _():
        write(o_ref, dx_ref[...])
        at = (chunks + 1) * width
        lanes = out_ref.shape[2] - at
        base, step = offsets
        shards = width // rows
        pad = jnp.zeros((1, 2 * lanes - rows), f32)
        for j in range(2):
            shard = idx_ref[0] ^ (base + step * j)
            tiles = [
                bias_ref[0:1, pl.ds(pl.multiple_of(shard * width + k * lanes, lanes), lanes)]
                for k in range(width // lanes)
            ]
            own = sum(
                jnp.where(shard == k, bias_ref[1:2, k * rows : (k + 1) * rows], 0.0) for k in range(shards)
            )
            own = jnp.concatenate([own, pad], axis=1)
            tiles += [own[:, :lanes], own[:, lanes:]]
            block = jnp.concatenate(tiles + [jnp.zeros((16 - len(tiles), lanes), f32)], axis=0)
            out_ref[j, :16, at:] = block.astype(bf16)
            out_ref[j, 16:, at:] = jnp.zeros((rows - 16, lanes), bf16)


def grad_up_call(index, a2t, ot, d_u, dx1r, biases, offsets, shards):
    width, rows = a2t.shape
    own = width // shards
    ff = d_u.shape[1]
    chunks = ff // width
    cols = ff + width + TILE
    return call(
        functools.partial(grad_up_body, chunks, offsets),
        "grad_up_out",
        (chunks + 1,),
        [fixed(array.shape) for array in (a2t, ot, d_u, dx1r, biases)],
        fixed((2, own, cols)),
        vmem((2, own, cols), bf16),
        [],
        8,
        4.7,
        near=range(5),
    )(index, a2t, ot, d_u, dx1r, biases)


def grad_qkv_body(offsets, idx_ref, a_ref, *refs):
    rights, out_ref = refs[:-1], refs[-1]
    rows = out_ref.shape[1]
    left = jnp.concatenate([a_ref[at, :] for at in shard_rows(idx_ref, offsets, rows)], axis=0)
    at = 0
    for right in rights:
        cols = right.shape[1]
        y = nn(left, right[...]).astype(bf16)
        out_ref[0, :, at : at + cols] = y[:rows]
        out_ref[1, :, at : at + cols] = y[rows:]
        at += cols


def grad_qkv_call(index, a1t, rights, offsets, shards):
    own = a1t.shape[0] // shards
    cols = sum(right.shape[1] for right in rights)
    return call(
        functools.partial(grad_qkv_body, offsets),
        "grad_qkv",
        (1,),
        [fixed(array.shape) for array in (a1t, *rights)],
        fixed((2, own, cols)),
        vmem((2, own, cols), bf16),
        [],
        8,
        1.0 + cols / 1000.0,
        near=range(1 + len(rights)),
    )(index, a1t, *rights)


def input_body(plan, groups, idx_ref, x_ref, dx1_ref, vec_ref, *refs):
    grads, parts, refs = take(refs, range(3 * groups), plan)
    dx_ref, whole, sems = refs
    weight = (plan, parts, whole, sems)
    fetch(idx_ref, weight)
    width = x_ref.shape[1]
    here = step_rows(x_ref.shape[0])
    scaled, inverse = norm_rows(x_ref[...].astype(f32))
    arrive(idx_ref, weight)
    d_a1 = 0.0
    for part in range(3):
        at = part * width
        for g in range(groups):
            ref = grads[3 * g + part]
            cols = ref.shape[1]
            d_a1 = d_a1 + nt(ref[here, :], whole[:, at : at + cols])
            at += cols
    d_x = dx1_ref[here, :] + norm_back(d_a1, scaled, inverse, vec_ref[0:1, :width])
    dx_ref[...] = d_x.astype(bf16)


def input_call(index, x, dx1, vec, d_groups, weight):
    rows, width = x.shape
    step = 256

    def row(cols):
        return pl.BlockSpec((step, cols), lambda i, s: (i, 0))

    flat = [array for group in d_groups for array in group]
    return call(
        functools.partial(input_body, weight.plan, len(d_groups)),
        "grad_input",
        (rows // step,),
        [row(width), fixed(dx1.shape), fixed(vec.shape)] + [fixed(array.shape) for array in flat] + weight.specs(),
        row(width),
        hbm((rows, width), bf16),
        weight.scratch(),
        12,
        9,
        near=(1, *range(3, 3 + len(flat))),
    )(index, x, dx1, vec, *flat, *weight.arrays)


def output_body(idx_ref, x1_ref, h_ref, vec_ref, w_ref, out_ref):
    here = step_rows(out_ref.shape[0])
    y = x1_ref[here, :] + nn(h_ref[here, :], w_ref[...]) + vec_ref[2:3, : x1_ref.shape[1]]
    out_ref[...] = y.astype(bf16)


def output_call(index, x1, h, vec, weight):
    rows, width = x1.shape
    step = 256
    return call(
        output_body,
        "layer_output",
        (rows // step,),
        [fixed(array.shape) for array in (x1, h, vec, weight)],
        pl.BlockSpec((step, width), lambda i, s: (i, 0)),
        hbm((rows, width), bf16),
        [],
        6,
        8,
        near=(0, 1, 3),
    )(index, x1, h, vec, weight)


def whole_call(name, body, arrays, outs, place=None):
    def run(*refs):
        body(refs[: len(arrays)], refs[len(arrays) :])

    return pl.pallas_call(
        run,
        name=name,
        in_specs=[pl.BlockSpec(memory_space=pltpu.VMEM)] * len(arrays),
        out_specs=[pl.BlockSpec(memory_space=pltpu.VMEM)] * len(outs),
        out_shape=[(place or vmem)(shape, dtype) for shape, dtype in outs],
        compiler_params=pltpu.CompilerParams(vmem_limit_bytes=8 * MIB),
        cost_estimate=pl.CostEstimate(
            flops=0,
            bytes_accessed=sum(array.size * array.dtype.itemsize for array in arrays),
            transcendentals=0,
        ),
    )(*(pltpu.with_memory_space_constraint(array, pltpu.VMEM) for array in arrays))


def half_of(bit, flip, rows):
    mine = (lax.axis_index("wide") // bit) % 2
    return pl.ds(pl.multiple_of((1 - mine if flip else mine) * rows, math.gcd(rows, 256)), rows)


def add_call(terms, rows, cols):
    def body(ins, outs):
        outs[0][...] = sum(
            (ref[...] if lead is None else ref[lead]).astype(f32) for ref, (_, lead) in zip(ins, terms)
        ).astype(bf16)

    return whole_call("add_terms", body, [a for a, _ in terms], [((rows, cols), bf16)])[0]


def halve_call(terms, rows, cols, bit):
    def body(ins, outs):
        for flip, out in ((1, outs[0]), (0, outs[1])):
            half = half_of(bit, flip, rows)
            out[...] = sum(
                (ref[half, :] if lead is None else ref[lead, half, :]).astype(f32)
                for ref, (_, lead) in zip(ins, terms)
            ).astype(out.dtype)

    return whole_call(
        "add_halves", body, [a for a, _ in terms], [((rows, cols), bf16), ((rows, cols), f32)]
    )


def fork_call(keep, core, rows, cols, left):
    def body(ins, outs):
        kept, got = ins
        outs[0][...] = (kept[1, :, :left].astype(f32) + got[1, :, :left].astype(f32)).astype(bf16)
        half = half_of(1, 1, rows // 2)
        for j in range(2):
            outs[1][j] = (kept[j, half, left:].astype(f32) + got[j, half, left:].astype(f32)).astype(bf16)

    return whole_call(
        "add_fork", body, [keep, core], [((rows, left), bf16), ((2, rows // 2, cols - left), bf16)]
    )


def cross_call(keep, core, got_left, got_right, rows, cols, left):
    rows //= 2

    def body(ins, outs):
        kept, got, from_left, from_right = ins
        mine, other = half_of(1, 0, rows), half_of(1, 1, rows)
        for half, out in ((other, outs[0]), (mine, outs[2])):
            out[...] = (
                kept[0, half, :left].astype(f32) + got[0, half, :left].astype(f32) + from_left[half, :].astype(f32)
            ).astype(out.dtype)
        for j, out in ((1, outs[1]), (0, outs[3])):
            out[...] = (
                kept[j, mine, left:].astype(f32) + got[j, mine, left:].astype(f32) + from_right[j].astype(f32)
            ).astype(out.dtype)

    shapes = [(rows, left), (rows, cols - left)]
    return whole_call(
        "add_cross", body, [keep, core, got_left, got_right],
        [(shape, dtype) for dtype in (bf16, f32) for shape in shapes],
    )


def merge_call(lefts, rights, rows, cols, left, bit):
    def body(ins, outs):
        for flip, out in ((1, outs[0]), (0, outs[1])):
            half = half_of(bit, flip, rows)
            out[:, :left] = (ins[0][half, :].astype(f32) + ins[1][half, :].astype(f32)).astype(out.dtype)
            out[:, left:] = (ins[2][half, :].astype(f32) + ins[3][half, :].astype(f32)).astype(out.dtype)

    return whole_call(
        "add_merge", body, [*lefts, *rights], [((rows, cols), bf16), ((rows, cols), f32)]
    )


def join_call(mine, other, bit):
    rows, cols = mine.shape

    def body(ins, outs):
        for flip in (0, 1):
            outs[0][half_of(bit, flip, rows), :] = ins[flip][...]

    return whole_call("join_halves", body, [mine, other], [((2 * rows, cols), bf16)])[0]


def turn_call(mine, other, bit):
    rows, cols = mine.shape

    def body(ins, outs):
        for flip in (0, 1):
            outs[0][:, half_of(bit, flip, rows)] = ins[flip][...].astype(f32).T

    return whole_call("last_down", body, [mine, other], [((cols, 2 * rows), f32)], hbm)[0]


def spread_body(plans, w_ref, gain_ref, *refs):
    ins, outs = refs[: 2 * len(plans)], refs[2 * len(plans) :]
    for c, plan in enumerate(plans):
        mine_ref, other_ref = ins[2 * c], ins[2 * c + 1]
        rows = mine_ref.shape[0]
        for flip, ref in ((0, mine_ref), (1, other_ref)):
            for begin, length, out, to in plan:
                outs[out][half_of(1, flip, rows), to : to + length] = ref[:, begin : begin + length].astype(f32)
    share = jnp.sum(outs[0][...] * w_ref[...].astype(f32), axis=1, keepdims=True)
    share = jnp.broadcast_to(share, (share.shape[0], PAIR)).T[0:1]
    outs[-1][...] = (share / gain_ref[...].astype(f32).reshape(1, -1)).reshape(-1)


def spread_call(weight, gain, sums, plans, shapes):
    arrays = [array for pair in sums for array in pair]
    return whole_call(
        "last_grads",
        lambda ins, outs: spread_body(plans, *ins, *outs),
        [weight, gain, *arrays],
        [(shape, f32) for shape in (*shapes, gain.shape)],
        hbm,
    )


def after(value, *deps):
    return lax.optimization_barrier((value, *deps))[0] if deps else value


class Moves:
    def __init__(self, narrow, wide):
        self.narrow, self.wide = narrow, wide
        self.n = lax.axis_index("narrow")
        self.w = lax.axis_index("wide")
        self.starts = [self.n, self.w % 2, (self.w // 2) % 2]

    def swap(self, value, axis, bit):
        size = self.narrow if axis == "narrow" else self.wide
        return lax.ppermute(value, axis, [(i, i ^ bit) for i in range(size)])

    def place(self, start):
        self.starts.append(start)
        return len(self.starts) - 1

    def reduce(self, send, keep, left):
        rows, cols = send.shape[1:]
        core = self.swap(send, "narrow", 1)
        deps = yield (send,)
        core = after(core, *deps)
        to_left, to_right = fork_call(keep, core, rows, cols, left)
        got_left, got_right = self.swap(to_left, "narrow", 2), self.swap(to_right, "wide", 1)
        deps = yield to_left, to_right
        to_left, to_right, mine_left, mine_right = cross_call(
            keep, core, after(got_left, *deps), after(got_right, *deps), rows, cols, left
        )
        got_left, got_right = self.swap(to_left, "wide", 1), self.swap(to_right, "narrow", 2)
        deps = yield to_left, to_right
        rows //= 4
        total, mine = merge_call(
            (mine_left, after(got_left, *deps)), (mine_right, after(got_right, *deps)), rows, cols, left, 2
        )
        got = self.swap(total, "wide", 2)
        deps = yield (total,)
        terms = [(mine, None), (after(got, *deps), None)]
        bit = 4
        while bit < self.wide:
            total = add_call(terms, rows, cols)
            got = self.swap(total, "wide", bit)
            deps = (yield (total,)) if bit == 4 else ()
            terms = [(total, None), (after(got, *deps), None)]
            bit *= 2
        total = add_call(terms, rows, cols)
        got = self.swap(total, "wide", 2)
        deps = yield (total,)
        total = join_call(total, after(got, *deps), 2)
        got = self.swap(total, "wide", 1)
        deps = yield (total,)
        yield total, after(got, *deps)


def begin(steps):
    return next(steps)


def step(steps, *deps):
    return steps.send(deps)


def advance(chains, *deps):
    return [array for chain in chains for array in step(chain, *deps)]


def shards(narrow, wide, layer_input, cotangent, block_size, gain_attn, w_qkv, w_out, gain_mlp, w_up, b_up, w_down, b_down):
    moves = Moves(narrow, wide)
    x, d_y = layer_input[0], cotangent[0]
    rows, width = x.shape
    seq = rows // 2
    pairs = width // PAIR
    ff = w_up.shape[1]
    n, bit = moves.n, moves.w % 2

    size = w_qkv.shape[0] // 3
    at_qkv = [
        moves.place((n ^ j) * w_qkv.shape[0] + extra)
        for j, extra in (
            (0, 0), (1, 0), (2, bit * size), (2, 2 * size), (2, (1 - bit) * size),
            (3, bit * size), (3, 2 * size), (3, (1 - bit) * size),
        )
    ]
    at_row = [moves.place((n ^ j) * w_out.shape[0]) for j in range(4)]

    def half_places(shard):
        half = shard.shape[0] // 2
        return [
            moves.place((n ^ j) * shard.shape[0] + extra)
            for j, extra in (
                (0, 0), (1, 0), (2, bit * half), (2, (1 - bit) * half), (3, bit * half), (3, (1 - bit) * half)
            )
        ]

    def own_half(shard):
        half = shard.shape[0] // 2
        return lax.dynamic_slice_in_dim(shard, bit * half, half, 0)

    def by_halves(shard, near, pieces, places):
        rows = shard.shape[0]
        return Weight(
            [(a, r, p) for a, r, p in zip((shard, near, *pieces), (rows, rows) + (rows // 2,) * 4, places)]
        )

    at_up = half_places(w_up)
    at_down = [moves.place((n ^ j) * w_down.shape[0]) for j in range(4)]
    index = jnp.stack(moves.starts).astype(jnp.int32)

    def ready(*deps):
        return after(index, *deps)

    first, second, near = first_call(index, w_qkv, gain_attn, gain_mlp, b_down, b_up)
    got_first = moves.swap(first, "narrow", 2)
    got_near = moves.swap(near, "narrow", 1)
    got_cross = moves.swap(got_first, "wide", 1)
    got_second = moves.swap(after(second, got_first), "narrow", 2)
    far_first, far_second, far_cross = (moves.swap(v, "narrow", 1) for v in (got_first, got_second, got_cross))
    count = w_qkv.shape[0]
    qkv_w = Weight(
        [
            (array, rows_of, place)
            for (array, rows_of), place in zip(
                (
                    (w_qkv, count), (got_near, count), (got_first, size), (got_second, size), (got_cross, size),
                    (far_first, size), (far_second, size), (far_cross, size),
                ),
                at_qkv,
            )
        ]
    )
    smalls = [near, got_near, got_first, far_first]
    up_far = moves.swap(after(own_half(w_up), got_second), "narrow", 2)
    out_near, up_near, down_near = (moves.swap(v, "narrow", 1) for v in (w_out, w_up, w_down))

    freq = 10000.0 ** (-jnp.arange(HEAD // 2).astype(f32) / (HEAD // 2))
    angles = jnp.arange(seq).astype(f32)[:, None] * freq[None, :]
    cosine, sine = jnp.cos(angles), jnp.sin(angles)
    cosine = jnp.tile(cosine, (1, 4))
    sine = jnp.concatenate([-sine, sine, -sine, sine], axis=1)
    block = jnp.arange(TILE, dtype=jnp.int32) // block_size[0]
    row_block, col_block = block[:, None], block[None, :]
    same, less, upto, less_t, upto_t = (
        jnp.where(ok, 0.0, -1e30).astype(f32)
        for ok in (
            row_block == col_block, col_block < row_block, col_block <= row_block,
            row_block < col_block, row_block <= col_block,
        )
    )
    dyt = d_y.T

    qkv, a1t, vec = qkv_call(index, x, qkv_w, smalls, ff, cosine, sine)
    up_far = after(up_far, vec)
    up_cross = moves.swap(up_far, "wide", 1)
    out_far = moves.swap(after(w_out, up_far), "narrow", 2)
    down_far = moves.swap(after(w_down, up_far), "narrow", 2)
    o, ot, lse = att_call(ready(up_far), qkv, (same, less_t, upto_t), 0, pairs)
    up_cross, out_far = after(up_cross, lse), after(out_far, lse)
    up_last = [moves.swap(v, "narrow", 1) for v in (after(up_far, lse), up_cross)]
    out_last = moves.swap(out_far, "narrow", 1)
    out_w = Weight([(a, w_out.shape[0], p) for a, p in zip((w_out, out_near, out_far, out_last), at_row)])
    up_w = by_halves(w_up, up_near, (up_far, up_cross, *up_last), at_up)
    x1, a2t, h, g, out_full, up_full = up_call(ready(lse), x, o, vec, out_w, up_w)
    send = grad_down_call(index, dyt, h, (1, 2), narrow)
    down_far = after(down_far, send)
    down_last = moves.swap(down_far, "narrow", 1)
    down_w = Weight([(a, w_down.shape[0], p) for a, p in zip((w_down, down_near, down_far, down_last), at_down)])
    keep = grad_down_call(ready(send, down_far), dyt, h, (0, 2), narrow)
    chain_a = moves.reduce(send, keep, width // 2)
    begin(chain_a)
    d_u, dx1, dx1r, d_o, biases, down_full = down_call(
        ready(keep, *advance([chain_a], keep)), d_y, x1, g, vec, up_full, out_full, down_w
    )
    send = grad_up_call(index, a2t, ot, d_u, dx1r, biases, (1, 2), narrow)
    keep = grad_up_call(ready(send), a2t, ot, d_u, dx1r, biases, (0, 2), narrow)
    chain_b = moves.reduce(send, keep, 2048)
    begin(chain_b)

    def back(start, count, *deps):
        return att_back_call(
            ready(*deps), qkv, d_o, o, lse, (same, less_t, upto_t), cosine, sine, start, count
        )

    g0 = back(0, 2, keep, *advance([chain_a, chain_b], keep))
    g1 = back(2, 2, g0[0], *advance([chain_a], g0[0]))
    g2 = back(4, 2, g1[0], *advance([chain_a, chain_b], g1[0]))
    groups = [g0, g1, g2]
    rights = [array for group in groups for array in group]
    send = grad_qkv_call(ready(*advance([chain_a, chain_b], g2[0])), a1t, rights, (1, 2), narrow)
    keep = grad_qkv_call(ready(send), a1t, rights, (0, 2), narrow)
    chain_c = moves.reduce(send, keep, 1152)
    begin(chain_c)
    sent = advance([chain_a, chain_b, chain_c], keep)
    output = output_call(ready(keep, *sent), x1, h, vec, down_full)
    sum_a = step(chain_a, output)
    sent = advance([chain_b, chain_c], output)
    d_input = input_call(ready(output, *sum_a, *sent), x, dx1, vec, groups, qkv_w)
    grad_down = turn_call(*sum_a, 1)
    sent = advance([chain_b, chain_c], d_input)
    sent = advance([chain_c], *sent)
    sum_b = step(chain_b, *sent)
    sent = advance([chain_c], *sent)
    sent = advance([chain_c], *sent)
    sum_c = step(chain_c)

    own = width // narrow
    grad_up, grad_out, biases, grad_gain_mlp = spread_call(
        w_up, gain_mlp, [sum_b], [[(0, ff, 0, 0), (ff, width, 1, 0), (ff + width, TILE, 2, 0)]],
        [(own, ff), (own, width), (own, TILE)],
    )
    biases = biases[:8].reshape(-1)
    cols = 2 * PAIR
    columns = [((3 * g + part) * cols, cols, 0, part * width + g * cols) for g in range(3) for part in range(3)]
    grad_qkv, grad_gain_attn = spread_call(w_qkv, gain_attn, [sum_c], [columns], [(own, 3 * width)])
    return (
        output[None],
        d_input[None],
        grad_gain_attn,
        grad_qkv,
        grad_out,
        grad_gain_mlp,
        grad_up,
        biases[:width],
        grad_down,
        biases[width : width + own],
    )


def solution(mesh):
    return jax.shard_map(
        functools.partial(shards, mesh.shape["narrow"], mesh.shape["wide"]),
        mesh=mesh,
        in_specs=(
            P(("wide", "narrow"), None, None),
            P(("wide", "narrow"), None, None),
            P(("wide", "narrow")),
            P("narrow"),
            P("narrow", None),
            P("narrow", None),
            P("narrow"),
            P("narrow", None),
            P("narrow"),
            P("narrow", None),
            P("narrow"),
        ),
        out_specs=(
            P(("wide", "narrow"), None, None),
            P(("wide", "narrow"), None, None),
            P("narrow"),
            P("narrow", None),
            P("narrow", None),
            P("narrow"),
            P("narrow", None),
            P("narrow"),
            P("narrow", None),
            P("narrow"),
        ),
        check_vma=False,
    )
```

```python
import functools
import math

import jax
import jax.numpy as jnp
from jax import lax
from jax.experimental import pallas as pl
from jax.experimental.pallas import tpu as pltpu
from jax.sharding import PartitionSpec as P

HEAD = 64
PAIR = 2 * HEAD
TILE = 128
ORDER = (1, 3, 0, 2)
SPAN = 256
LOG2E = 1.4426950408889634
LN2 = 0.6931471805599453
f32 = jnp.float32
bf16 = jnp.bfloat16
MIB = 1 << 20


def nn(left, right):
    return jnp.dot(left, right, preferred_element_type=f32)


def nt(left, right):
    return lax.dot_general(left, right, (((1,), (1,)), ((), ())), preferred_element_type=f32)


def norm_rows(values):
    centre = values - jnp.mean(values, axis=-1, keepdims=True)
    inverse = lax.rsqrt(jnp.mean(centre * centre, axis=-1, keepdims=True) + 1e-05)
    return centre * inverse, inverse


def norm_back(d_norm, scaled, inverse, gain):
    d_scaled = d_norm * gain
    return inverse * (
        d_scaled
        - jnp.mean(d_scaled, axis=-1, keepdims=True)
        - scaled * jnp.mean(d_scaled * scaled, axis=-1, keepdims=True)
    )


def swap_halves(tile):
    lane = lax.broadcasted_iota(jnp.int32, (1, PAIR), 1) % HEAD
    return jnp.where(
        lane < HEAD // 2,
        pltpu.roll(tile, PAIR - HEAD // 2, 1),
        pltpu.roll(tile, HEAD // 2, 1),
    )


class Weight:
    def __init__(self, pieces):
        self.arrays = [array for array, _, _ in pieces]
        self.plan = [(rows, place) for _, rows, place in pieces]
        self.rows = sum(rows for rows, _ in self.plan)
        self.cols = self.arrays[0].shape[1]

    def specs(self, near=True):
        space = pltpu.VMEM if near else pltpu.HBM
        return [pl.BlockSpec(memory_space=pltpu.HBM)] + [pl.BlockSpec(memory_space=space)] * (len(self.plan) - 1)

    def near(self, at):
        return list(range(at + 1, at + len(self.plan)))

    def whole(self):
        return pltpu.VMEM((self.rows, self.cols), bf16)

    def sems(self):
        return [pltpu.SemaphoreType.DMA((len(self.plan),))]

    def scratch(self):
        return [pltpu.VMEM((self.rows, self.cols), bf16), pltpu.SemaphoreType.DMA((len(self.plan),))]


def fetches(at_ref, plan, parts, whole, sems):
    copies = []
    for i, ((rows, place), part) in enumerate(zip(plan, parts)):
        start = pl.multiple_of(at_ref[place], math.gcd(rows, 256))
        copies.append(pltpu.make_async_copy(part.at[pl.ds(0, rows)], whole.at[pl.ds(start, rows)], sems.at[i]))
    return copies


def fetch(at_ref, *weights):
    @pl.when(pl.program_id(0) == 0)
    def _():
        for weight in weights:
            for copy in fetches(at_ref, *weight):
                copy.start()


def arrive(at_ref, weight):
    @pl.when(pl.program_id(0) == 0)
    def _():
        for copy in fetches(at_ref, *weight):
            copy.wait()


def step_rows(step):
    return pl.ds(pl.multiple_of(pl.program_id(0) * step, step), step)


def take(refs, *groups):
    out, at = [], 0
    for group in groups:
        out.append(refs[at : at + len(group)])
        at += len(group)
    return out + [refs[at:]]


def fixed(shape):
    return pl.BlockSpec(shape, lambda *_: (0,) * len(shape), pipeline_mode=pl.Buffered(1))


def call(body, name, grid, in_specs, out_specs, out_shape, scratch, limit, cost, near=(), aliases=None, moved=1 << 20):
    fun = pl.pallas_call(
        body,
        name=name,
        out_shape=out_shape,
        input_output_aliases=aliases or {},
        grid_spec=pltpu.PrefetchScalarGridSpec(
            num_scalar_prefetch=1,
            grid=grid,
            in_specs=in_specs,
            out_specs=out_specs,
            scratch_shapes=scratch,
        ),
        compiler_params=pltpu.CompilerParams(
            dimension_semantics=("arbitrary",) * len(grid), vmem_limit_bytes=limit * MIB
        ),
        cost_estimate=pl.CostEstimate(
            flops=int(cost * 1e12), bytes_accessed=moved, transcendentals=0
        ),
    )

    def run(index, *args):
        args = [
            pltpu.with_memory_space_constraint(arg, pltpu.VMEM if i in near else pltpu.HBM)
            for i, arg in enumerate(args)
        ]
        return fun(index, *args)

    return run


def hbm(shape, dtype):
    return pltpu.HBM(shape, dtype)


def vmem(shape, dtype):
    return pltpu.VMEM(shape, dtype)


def sds(shape, dtype):
    return jax.ShapeDtypeStruct(shape, dtype)


def small_rows(cols, gain1_ref, gain2_ref, down_ref, up_ref):
    def lanes(*refs):
        values = [ref[...].astype(f32).reshape(1, -1) for ref in refs]
        return jnp.concatenate(
            [v for v in values for _ in range(cols // (len(refs) * v.shape[1]))], axis=1
        )

    row = lax.broadcasted_iota(jnp.int32, (8, cols), 0)
    return jnp.where(row == 0, lanes(gain1_ref, gain2_ref, down_ref), lanes(up_ref)).astype(bf16)


def first_body(idx_ref, w_ref, gain1_ref, gain2_ref, down_ref, up_ref, out_ref, small_ref):
    size = w_ref.shape[0]
    small = small_rows(w_ref.shape[1], gain1_ref, gain2_ref, down_ref, up_ref)
    out_ref[:size, :] = w_ref[...]
    out_ref[size:, :] = small
    small_ref[...] = small


def first_call(index, weight, *vectors):
    size, cols = weight.shape[0] // 3, weight.shape[1]
    shapes = [(size + 8, cols), (8, cols)]
    return call(
        first_body,
        "first_message",
        (1,),
        [pl.BlockSpec((size, cols), lambda i, s: (s[1], 0))] + [fixed(v.shape) for v in vectors],
        [fixed(shape) for shape in shapes],
        [vmem(shape, bf16) for shape in shapes],
        [],
        6,
        1.5,
    )(index, weight, *vectors)


def thirds_body(idx_ref, *refs):
    count = len(refs) // 2
    for ref, out_ref in zip(refs[:count], refs[count:]):
        out_ref[...] = ref[...]


def thirds_call(index, weight, places):
    size, cols = weight.shape[0] // 3, weight.shape[1]
    return call(
        thirds_body,
        "next_message",
        (1,),
        [pl.BlockSpec((size, cols), lambda i, s, p=p: (2 if p is None else s[p], 0)) for p in places],
        [fixed((size, cols))] * len(places),
        [vmem((size, cols), bf16)] * len(places),
        [],
        6,
        1.5,
    )(index, *[weight] * len(places))


def qkv_body(plan, n, idx_ref, x_ref, cos_ref, sin_ref, *refs):
    smalls, parts, refs = take(refs, range(n), plan)
    qkv_ref, a1t_ref, vec_ref, whole, sems = refs
    weight = (plan, parts, whole, sems)
    fetch(idx_ref, weight)
    width = x_ref.shape[1]

    @pl.when(pl.program_id(0) == 0)
    def _():
        lane = lax.broadcasted_iota(jnp.int32, (1, width), 1) // (width // n)
        values = [ref[...].astype(f32) for ref in smalls]
        vec_ref[...] = jnp.zeros_like(vec_ref)
        for i in range(3):
            vec_ref[i : i + 1, :width] = sum(
                jnp.where(lane == (idx_ref[0] ^ j), v[0:1, i * width : (i + 1) * width], 0.0)
                for j, v in enumerate(values)
            )
        size = vec_ref.shape[1] // n
        for c in range(n):
            vec_ref[3:4, c * size : (c + 1) * size] = sum(
                jnp.where((idx_ref[0] ^ j) == c, v[1:2, :size], 0.0) for j, v in enumerate(values)
            )

    scaled, _ = norm_rows(x_ref[...].astype(f32))
    a1 = (scaled * vec_ref[0:1, :width]).astype(bf16)
    a1t_ref[...] = a1.T
    cosine, sine = cos_ref[...], sin_ref[...]
    arrive(idx_ref, weight)
    for part in range(3):
        y = nn(a1, whole[:, part * width : (part + 1) * width])
        if part == 2:
            qkv_ref[:, part * width :] = y.astype(bf16)
            continue
        for t in range(width // PAIR):
            tile = y[:, t * PAIR : (t + 1) * PAIR]
            tile = tile * cosine + swap_halves(tile) * sine
            if part == 0:
                tile = tile * (LOG2E / 8.0)
            at = part * width + t * PAIR
            qkv_ref[:, at : at + PAIR] = tile.astype(bf16)


def qkv_call(index, x, weight, smalls, ff, cosine, sine):
    rows, width = x.shape
    wide = weight.cols
    step = 256
    per = cosine.shape[0] // step

    def vector(array):
        return pl.BlockSpec((8, wide), lambda i, s: (array.shape[0] // 8 - 1, 0))

    return call(
        functools.partial(qkv_body, weight.plan, len(smalls)),
        "norm_qkv",
        (rows // step,),
        [
            pl.BlockSpec((step, width), lambda i, s: (i, 0)),
            pl.BlockSpec((step, PAIR), lambda i, s: (i % per, 0)),
            pl.BlockSpec((step, PAIR), lambda i, s: (i % per, 0)),
        ]
        + [vector(array) for array in smalls]
        + weight.specs(),
        [
            pl.BlockSpec((step, wide), lambda i, s: (i, 0)),
            pl.BlockSpec((width, step), lambda i, s: (0, i)),
            pl.BlockSpec((8, ff), lambda i, s: (0, 0)),
            fixed((weight.rows, wide)),
        ],
        [hbm((rows, wide), bf16), hbm((width, rows), bf16), hbm((8, ff), f32), hbm((weight.rows, wide), bf16)],
        weight.sems(),
        16,
        7,
        near=(*range(3, 3 + len(smalls)), *weight.near(3 + len(smalls))),
    )(index, x, cosine, sine, *smalls, *weight.arrays)


def head_masks():
    lane = lax.broadcasted_iota(jnp.int32, (1, PAIR), 1)
    return lane < HEAD, lane >= HEAD


def widen(tile, allowed):
    count = SPAN // TILE
    never = jnp.full(tile.shape, -1e30, f32)
    before = jnp.zeros(tile.shape, f32) if allowed else never
    return jnp.concatenate(
        [
            jnp.concatenate([tile if a == b else (before if a < b else never) for b in range(count)], axis=1)
            for a in range(count)
        ],
        axis=0,
    )


def att_body(seq, idx_ref, q_ref, k_ref, v_ref, same_ref, less_ref, upto_ref, *refs):
    o_ref, ot_ref, lse_ref = refs[-3:]
    k_all = k_ref[...]
    keys = [jnp.where(m, k_all, jnp.zeros_like(k_all)) for m in head_masks()]
    v_t = v_ref[...].T
    ones = jnp.ones((16, 2 * seq), bf16)
    vals = [jnp.concatenate([v_t[h * HEAD : (h + 1) * HEAD], ones], axis=0) for h in range(2)]
    same, less, upto = widen(same_ref[...], False), widen(less_ref[...], True), widen(upto_ref[...], True)

    def scores(lo, clean, h):
        hi = lo + SPAN
        row = lo + seq if clean else lo
        query = q_ref[row : row + SPAN, :]
        pieces = [nt(keys[h][seq + lo : seq + hi], query) + (upto if clean else less)]
        if lo > 0:
            pieces.append(nt(keys[h][seq : seq + lo], query))
        if not clean:
            pieces.append(nt(keys[h][lo:hi], query) + same)
        return pieces

    def soften(pieces):
        top = functools.reduce(jnp.maximum, [jnp.max(p, axis=0, keepdims=True) for p in pieces])
        return top, [jnp.exp2(p - top).astype(bf16) for p in pieces]

    def mix(lo, clean, h, weights):
        hi = lo + SPAN
        out = nn(vals[h][:, seq + lo : seq + hi], weights[0])
        if lo > 0:
            out = out + nn(vals[h][:, seq : seq + lo], weights[1])
        if not clean:
            out = out + nn(vals[h][:, lo:hi], weights[-1])
        return out

    def finish(lo, clean, softened):
        row = lo + seq if clean else lo
        outs = [mix(lo, clean, h, softened[h][1]) for h in range(2)]
        out = jnp.concatenate([o[:HEAD] / o[HEAD : HEAD + 1] for o in outs], axis=0)
        ot_ref[:, row : row + SPAN] = out.astype(bf16)
        o_ref[row : row + SPAN, :] = out.T.astype(bf16)
        for h in range(2):
            lse_ref[0, h : h + 1, row : row + SPAN] = softened[h][0] + jnp.log2(outs[h][HEAD : HEAD + 1])

    work = [(lo, clean) for lo in range(0, seq, SPAN) for clean in (False, True)]
    ahead = [scores(*work[0], h) for h in range(2)]
    behind = None
    for i, item in enumerate(work):
        now = ahead
        if i + 1 < len(work):
            ahead = [scores(*work[i + 1], h) for h in range(2)]
        softened = [soften(pieces) for pieces in now]
        if behind is not None:
            finish(*behind)
        behind = (*item, softened)
    finish(*behind)


def att_call(index, qkv, masks, start, count, held=()):
    rows = qkv.shape[0]
    width = qkv.shape[1] // 3
    pairs = width // PAIR

    def column(part):
        return pl.BlockSpec((rows, PAIR), lambda p, s: (0, part * pairs + start + p))

    return call(
        functools.partial(att_body, rows // 2),
        "attention",
        (count,),
        [column(0), column(1), column(2)] + [fixed((TILE, TILE))] * 3
        + [pl.BlockSpec(memory_space=pltpu.HBM)] * len(held),
        [
            pl.BlockSpec((rows, PAIR), lambda p, s: (0, start + p)),
            pl.BlockSpec((PAIR, rows), lambda p, s: (start + p, 0)),
            pl.BlockSpec((1, 2, rows), lambda p, s: (start + p, 0, 0)),
        ],
        [hbm((rows, width), bf16), hbm((width, rows), bf16), hbm((pairs, 2, rows), f32)],
        [],
        16,
        2.0 * count,
        aliases={7 + i: i for i in range(len(held))},
    )(index, qkv, qkv, qkv, *masks, *held)


def att_back_body(
    seq, idx_ref, q_ref, k_ref, v_ref, do_ref, o_ref, lse_ref, same_ref, less_ref, upto_ref,
    cos_ref, sin_ref, dq_ref, dk_ref, dv_ref, dqt_ref,
):
    first, second = head_masks()
    q_all, k_all, v_all, do_all = q_ref[...], k_ref[...], v_ref[...], do_ref[...]

    def split(array):
        return [jnp.where(m, array, jnp.zeros_like(array)) for m in (first, second)]

    queries, keys, vals, dos = split(q_all), split(k_all), split(v_all), split(do_all)
    keys_t = k_all.T
    product = do_all.astype(f32) * o_ref[...].astype(f32)
    high = product.astype(bf16)
    rest = (product - high.astype(f32)).astype(bf16)
    picked = lax.broadcasted_iota(jnp.int32, (8, PAIR), 0)
    picked = jnp.where(picked == lax.broadcasted_iota(jnp.int32, (8, PAIR), 1) // HEAD, 1.0, 0.0).astype(bf16)
    delta = nt(picked, high) + nt(picked, rest)
    same, less, upto = widen(same_ref[...], False), widen(less_ref[...], True), widen(upto_ref[...], True)
    dqt_ref[...] = jnp.zeros_like(dqt_ref)

    def products(unit):
        return [
            (nt(keys[h][k : k + SPAN], q_all[q:end]), nt(vals[h][k : k + SPAN], do_all[q:end]))
            for h, k, q, end, _ in unit[0]
        ]

    def soften(unit, values):
        out = []
        for (h, _, q, end, mask), (scores, d_probs) in zip(unit[0], values):
            scores = scores - lse_ref[0, h : h + 1, q:end]
            probs = jnp.exp2(scores[:, :SPAN] + mask)
            if end - q > SPAN:
                probs = jnp.concatenate([probs, jnp.exp2(scores[:, SPAN:])], axis=1)
            d_scores = probs * (d_probs - delta[h : h + 1, q:end])
            out.append((probs.astype(bf16), d_scores.astype(bf16)))
        return out

    def rotate_back(tile, row):
        at = row % seq
        cosine, sine = cos_ref[at : at + SPAN, :], sin_ref[at : at + SPAN, :]
        return tile * cosine - swap_halves(tile) * sine

    def gather(unit, values, sums):
        items, last = unit
        d_vals, d_keys = sums
        for (h, k, q, end, _), (probs, d_scores) in zip(items, values):
            d_vals = d_vals + nn(probs, dos[h][q:end])
            d_keys = d_keys + nn(d_scores, queries[h][q:end])
            at = slice(h * HEAD, (h + 1) * HEAD)
            dqt_ref[at, q:end] += nn(keys_t[at, k : k + SPAN], d_scores)
        if not last:
            return d_vals, d_keys
        k = items[0][1]
        dv_ref[k : k + SPAN, :] = d_vals.astype(bf16)
        dk_ref[k : k + SPAN, :] = rotate_back(d_keys * LN2, k).astype(bf16)
        return 0.0, 0.0

    units = []
    for lo in range(0, seq, SPAN):
        units.append(([(h, lo, lo, lo + SPAN, same) for h in range(2)], True))
        for base, mask in ((0, less), (seq, upto)):
            units.append(([(h, seq + lo, base + lo, base + seq, mask) for h in range(2)], base > 0))
    ahead, behind, sums = products(units[0]), None, (0.0, 0.0)
    for i, unit in enumerate(units):
        now = ahead
        if i + 1 < len(units):
            ahead = products(units[i + 1])
        values = soften(unit, now)
        if behind is not None:
            sums = gather(*behind, sums)
        behind = (unit, values)
    gather(*behind, sums)
    for r in range(0, 2 * seq, SPAN):
        tile = dqt_ref[:, r : r + SPAN].T * 0.125
        dq_ref[r : r + SPAN, :] = rotate_back(tile, r).astype(bf16)


def att_back_call(index, qkv, d_o, o, lse, masks, cosine, sine, start, count):
    rows = qkv.shape[0]
    width = qkv.shape[1] // 3
    pairs = width // PAIR
    seq = rows // 2

    def column(part):
        return pl.BlockSpec((rows, PAIR), lambda p, s: (0, part * pairs + start + p))

    out = pl.BlockSpec((rows, PAIR), lambda p, s: (0, p))
    return call(
        functools.partial(att_back_body, seq),
        "attention_back",
        (count,),
        [column(0), column(1), column(2), column(0), column(0)]
        + [pl.BlockSpec((1, 2, rows), lambda p, s: (start + p, 0, 0))]
        + [fixed((TILE, TILE))] * 3
        + [fixed((seq, PAIR))] * 2,
        [out] * 3,
        [vmem((rows, count * PAIR), bf16)] * 3,
        [pltpu.VMEM((PAIR, rows), f32)],
        16,
        3.6 * count,
    )(index, qkv, qkv, qkv, d_o, o, lse, *masks, cosine, sine)


def up_body(out_at, up_at, idx_ref, x_ref, o_ref, vec_ref, *refs):
    outs, ups, refs = take(refs, out_at, up_at)
    x1_ref, a2t_ref, h_ref, g_ref, w_out, w_up, out_sems, up_sems = refs
    out_weight, up_weight = (out_at, outs, w_out, out_sems), (up_at, ups, w_up, up_sems)
    fetch(idx_ref, out_weight, up_weight)
    arrive(idx_ref, out_weight)
    width = x_ref.shape[1]
    here = step_rows(x_ref.shape[0])
    x1 = x_ref[...].astype(f32) + nn(o_ref[...], w_out[...])
    x1_ref[...] = x1
    scaled, _ = norm_rows(x1)
    a2 = (scaled * vec_ref[1:2, :width]).astype(bf16)
    a2t_ref[:, here] = a2.T
    arrive(idx_ref, up_weight)
    c0 = math.sqrt(2.0 / math.pi)
    c1 = c0 * 0.044715
    chunk = 512
    for at in range(0, w_up.shape[1], chunk):
        u = nn(a2, w_up[:, at : at + chunk]) + vec_ref[3:4, at : at + chunk]
        square = u * u
        t = jnp.tanh(u * (c1 * square + c0))
        half = 0.5 * t + 0.5
        h_ref[here, at : at + chunk] = (u * half).astype(bf16)
        slope = u * (1.5 * c1 * square + 0.5 * c0)
        g_ref[here, at : at + chunk] = (half + slope * (1.0 - t * t)).astype(bf16)


def up_call(index, x, o, vec, w_out, w_up):
    rows, width = x.shape
    ff = w_up.cols
    step = 256

    def row(cols):
        return pl.BlockSpec((step, cols), lambda i, s: (i, 0))

    outs = [
        hbm((rows, width), f32), vmem((width, rows), bf16), vmem((rows, ff), bf16), vmem((rows, ff), bf16),
        w_out.whole(), w_up.whole(),
    ]
    return call(
        functools.partial(up_body, w_out.plan, w_up.plan),
        "feed_up",
        (rows // step,),
        [row(width), row(width), fixed(vec.shape)] + w_out.specs() + w_up.specs(),
        [row(width)] + [fixed(out.shape) for out in outs[1:]],
        outs,
        w_out.sems() + w_up.sems(),
        12,
        18,
        near=w_out.near(3) + w_up.near(3 + len(w_out.plan)),
    )(index, x, o, vec, *w_out.arrays, *w_up.arrays)


def down_body(down_at, idx_ref, dy_ref, x1_ref, g_ref, vec_ref, w_up, w_out, *refs):
    downs, refs = take(refs, down_at)
    du_ref, dx1_ref, dx1r_ref, do_ref, bias_ref, w_down, down_sems = refs
    weight = (down_at, downs, w_down, down_sems)
    fetch(idx_ref, weight)

    @pl.when(pl.program_id(0) == 0)
    def _():
        bias_ref[...] = jnp.zeros_like(bias_ref)

    width = dy_ref.shape[1]
    here = step_rows(dy_ref.shape[0])
    low = dy_ref[...]
    d_y = low.astype(f32)
    bias_ref[1:2, :width] += jnp.sum(d_y, axis=0, keepdims=True)
    arrive(idx_ref, weight)
    chunk = 512
    d_a2 = 0.0
    for at in range(0, w_up.shape[1], chunk):
        d_u = nt(low, w_down[at : at + chunk, :]) * g_ref[here, at : at + chunk].astype(f32)
        bias_ref[0:1, at : at + chunk] += jnp.sum(d_u, axis=0, keepdims=True)
        d_u = d_u.astype(bf16)
        du_ref[here, at : at + chunk] = d_u
        d_a2 = d_a2 + nt(d_u, w_up[:, at : at + chunk])
    scaled, inverse = norm_rows(x1_ref[...])
    d_x1 = d_y + norm_back(d_a2, scaled, inverse, vec_ref[1:2, :width])
    dx1_ref[...] = d_x1
    d_x1 = d_x1.astype(bf16)
    dx1r_ref[here, :] = d_x1
    do_ref[...] = nt(d_x1, w_out[...]).astype(bf16)


def down_call(index, d_y, x1, g, vec, w_up, w_out, w_down):
    rows, width = d_y.shape
    ff = w_up.shape[1]
    step = 256

    def row(cols):
        return pl.BlockSpec((step, cols), lambda i, s: (i, 0))

    return call(
        functools.partial(down_body, w_down.plan),
        "feed_back",
        (rows // step,),
        [row(width), row(width)] + [fixed(array.shape) for array in (g, vec, w_up, w_out)] + w_down.specs(),
        [fixed((rows, ff)), row(width), fixed((rows, width)), row(width), fixed((2, ff)),
         fixed((ff, width))],
        [
            vmem((rows, ff), bf16), hbm((rows, width), f32), vmem((rows, width), bf16),
            hbm((rows, width), bf16), vmem((2, ff), f32), w_down.whole(),
        ],
        w_down.sems(),
        14,
        20,
        near=(2, 4, 5, *w_down.near(6)),
    )(index, d_y, x1, g, vec, w_up, w_out, *w_down.arrays)


def grad_down_body(offsets, idx_ref, dyt_ref, h_ref, out_ref):
    base, step = offsets
    cols = out_ref.shape[2]
    shard = idx_ref[0] ^ (base + step * pl.program_id(0))
    columns = pl.ds(pl.multiple_of(shard * cols, cols), cols)
    out_ref[pl.program_id(0)] = nn(dyt_ref[...], h_ref[:, columns]).astype(bf16)


def grad_down_call(index, dyt, h, offsets, shards):
    width, rows = dyt.shape
    cols = h.shape[1] // shards
    return call(
        functools.partial(grad_down_body, offsets),
        "grad_down",
        (2,),
        [fixed(dyt.shape), fixed(h.shape)],
        fixed((2, width, cols)),
        vmem((2, width, cols), bf16),
        [],
        8,
        3,
        near=(0, 1),
    )(index, dyt, h)


def shard_rows(idx_ref, rows):
    return [pl.ds(pl.multiple_of((idx_ref[0] ^ j) * rows, math.gcd(rows, 256)), rows) for j in ORDER]


def grad_up_body(chunks, idx_ref, a_ref, o_ref, du_ref, dx_ref, bias_ref, send_ref, keep_ref):
    rows = send_ref.shape[1]
    width = dx_ref.shape[1]
    i = pl.program_id(0)
    columns = pl.ds(pl.multiple_of(i * width, width), width)
    shards_at = shard_rows(idx_ref, rows)

    def write(left, right):
        y = nn(jnp.concatenate([left[at, :] for at in shards_at], axis=0), right).astype(bf16)
        for k in range(4):
            (send_ref if k < 2 else keep_ref)[k % 2, :, columns] = y[k * rows : (k + 1) * rows]

    @pl.when(i < chunks)
    def _():
        write(a_ref, du_ref[:, columns])

    @pl.when(i == chunks)
    def _():
        write(o_ref, dx_ref[...])
        at = (chunks + 1) * width
        lanes = send_ref.shape[2] - at
        shards = width // rows
        pad = jnp.zeros((1, 2 * lanes - rows), f32)
        for k, j in enumerate(ORDER):
            shard = idx_ref[0] ^ j
            out_ref = send_ref if k < 2 else keep_ref
            tiles = [
                bias_ref[0:1, pl.ds(pl.multiple_of(shard * width + t * lanes, lanes), lanes)]
                for t in range(width // lanes)
            ]
            own = sum(
                jnp.where(shard == t, bias_ref[1:2, t * rows : (t + 1) * rows], 0.0) for t in range(shards)
            )
            own = jnp.concatenate([own, pad], axis=1)
            tiles += [own[:, :lanes], own[:, lanes:]]
            block = jnp.concatenate(tiles + [jnp.zeros((16 - len(tiles), lanes), f32)], axis=0)
            out_ref[k % 2, :16, at:] = block.astype(bf16)
            out_ref[k % 2, 16:, at:] = jnp.zeros((rows - 16, lanes), bf16)


def grad_up_call(index, a2t, ot, d_u, dx1r, biases, shards):
    width, rows = a2t.shape
    own = width // shards
    ff = d_u.shape[1]
    chunks = ff // width
    cols = ff + width + TILE
    return call(
        functools.partial(grad_up_body, chunks),
        "grad_up_out",
        (chunks + 1,),
        [fixed(array.shape) for array in (a2t, ot, d_u, dx1r, biases)],
        [fixed((2, own, cols))] * 2,
        [vmem((2, own, cols), bf16)] * 2,
        [],
        10,
        4.7,
        near=range(5),
    )(index, a2t, ot, d_u, dx1r, biases)


def grad_qkv_body(idx_ref, a_ref, *refs):
    rights, send_ref, keep_ref = refs[:-2], refs[-2], refs[-1]
    rows = send_ref.shape[1]
    left = jnp.concatenate([a_ref[at, :] for at in shard_rows(idx_ref, rows)], axis=0)
    at = 0
    for right in rights:
        cols = right.shape[1]
        y = nn(left, right[...]).astype(bf16)
        for k in range(4):
            (send_ref if k < 2 else keep_ref)[k % 2, :, at : at + cols] = y[k * rows : (k + 1) * rows]
        at += cols


def grad_qkv_call(index, a1t, rights, shards):
    own = a1t.shape[0] // shards
    cols = sum(right.shape[1] for right in rights)
    return call(
        grad_qkv_body,
        "grad_qkv",
        (1,),
        [fixed(array.shape) for array in (a1t, *rights)],
        [fixed((2, own, cols))] * 2,
        [vmem((2, own, cols), bf16)] * 2,
        [],
        10,
        1.0 + cols / 1000.0,
        near=range(1 + len(rights)),
    )(index, a1t, *rights)


def input_body(groups, idx_ref, x_ref, dx1_ref, vec_ref, w_ref, *refs):
    grads, (dx_ref,) = refs[: 3 * groups], refs[3 * groups :]
    width = x_ref.shape[1]
    here = step_rows(x_ref.shape[0])
    scaled, inverse = norm_rows(x_ref[...].astype(f32))
    d_a1 = 0.0
    for part in range(3):
        at = part * width
        for g in range(groups):
            ref = grads[3 * g + part]
            cols = ref.shape[1]
            d_a1 = d_a1 + nt(ref[here, :], w_ref[:, at : at + cols])
            at += cols
    d_x = dx1_ref[...] + norm_back(d_a1, scaled, inverse, vec_ref[0:1, :width])
    dx_ref[...] = d_x.astype(bf16)


def input_call(index, x, dx1, vec, d_groups, weight):
    rows, width = x.shape
    step = 256

    def row(cols):
        return pl.BlockSpec((step, cols), lambda i, s: (i, 0))

    flat = [array for group in d_groups for array in group]
    return call(
        functools.partial(input_body, len(d_groups)),
        "grad_input",
        (rows // step,),
        [row(width), row(width)] + [fixed(array.shape) for array in (vec, weight, *flat)],
        row(width),
        hbm((rows, width), bf16),
        [],
        14,
        9,
        near=range(4, 4 + len(flat)),
    )(index, x, dx1, vec, weight, *flat)


def output_body(idx_ref, x1_ref, h_ref, vec_ref, w_ref, out_ref):
    y = x1_ref[...] + nn(h_ref[...], w_ref[...]) + vec_ref[2:3, : x1_ref.shape[1]]
    out_ref[...] = y.astype(bf16)


def output_call(index, x1, h, vec, weight):
    rows, width = x1.shape

    def row(cols):
        return pl.BlockSpec((256, cols), lambda i, s: (i, 0))

    return call(
        output_body,
        "layer_output",
        (rows // 256,),
        [row(width), row(h.shape[1]), fixed(vec.shape), fixed(weight.shape)],
        row(width),
        hbm((rows, width), bf16),
        [],
        14,
        8,
        near=(3,),
    )(index, x1, h, vec, weight)


def pace_body(idx_ref, tile_ref, out_ref):
    out_ref[...] = tile_ref[:8, :]


def pace_call(index, tile):
    return call(
        pace_body,
        "pace",
        (1,),
        [fixed(tile.shape)],
        fixed((8, tile.shape[1])),
        vmem((8, tile.shape[1]), f32),
        [],
        2,
        5,
        near=(0,),
    )(index, tile)


def whole_call(name, jobs):
    arrays = [array for _, ins, _, _ in jobs for array in ins]
    results = [place(shape, dtype) for _, _, outs, place in jobs for shape, dtype in outs]

    def run(*refs):
        ins, outs = refs[: len(arrays)], refs[len(arrays) :]
        at, to = 0, 0
        for body, job_ins, job_outs, _ in jobs:
            body(ins[at : at + len(job_ins)], outs[to : to + len(job_outs)])
            at, to = at + len(job_ins), to + len(job_outs)

    flat = pl.pallas_call(
        run,
        name=name,
        in_specs=[pl.BlockSpec(memory_space=pltpu.VMEM)] * len(arrays),
        out_specs=[pl.BlockSpec(memory_space=pltpu.VMEM)] * len(results),
        out_shape=results,
        compiler_params=pltpu.CompilerParams(vmem_limit_bytes=10 * MIB),
        cost_estimate=pl.CostEstimate(
            flops=0,
            bytes_accessed=sum(array.size * array.dtype.itemsize for array in arrays),
            transcendentals=0,
        ),
    )(*(pltpu.with_memory_space_constraint(array, pltpu.VMEM) for array in arrays))
    groups, at = [], 0
    for _, _, outs, _ in jobs:
        groups.append(flat[at : at + len(outs)])
        at += len(outs)
    return groups


def half_of(bit, flip, rows):
    mine = (lax.axis_index("wide") // bit) % 2
    return pl.ds(pl.multiple_of((1 - mine if flip else mine) * rows, math.gcd(rows, 256)), rows)


def add_job(terms, rows, cols):
    def body(ins, outs):
        outs[0][...] = sum(
            (ref[...] if lead is None else ref[lead]).astype(f32) for ref, (_, lead) in zip(ins, terms)
        ).astype(bf16)

    return body, [a for a, _ in terms], [((rows, cols), bf16)], vmem


def halve_job(terms, rows, cols, bit):
    def body(ins, outs):
        for flip, out in ((1, outs[0]), (0, outs[1])):
            half = half_of(bit, flip, rows)
            out[...] = sum(
                (ref[half, :] if lead is None else ref[lead, half, :]).astype(f32)
                for ref, (_, lead) in zip(ins, terms)
            ).astype(out.dtype)

    return body, [a for a, _ in terms], [((rows, cols), bf16), ((rows, cols), f32)], vmem


def part_job(keep, core, rows, cols):
    def body(ins, outs):
        kept, got = ins
        for j, out in ((1, outs[0]), (0, outs[1])):
            out[...] = (kept[j].astype(f32) + got[j].astype(f32)).astype(out.dtype)

    return body, [keep, core], [((rows, cols), bf16), ((rows, cols), f32)], vmem


def fork_job(keep, core, rows, cols, left):
    rest = cols - left

    def body(ins, outs):
        kept, got = ins
        for j, out in ((1, outs[0]), (0, outs[2])):
            out[...] = (kept[j, :, :left].astype(f32) + got[j, :, :left].astype(f32)).astype(out.dtype)
        for flip, out in ((1, outs[1]), (0, outs[3])):
            half = half_of(1, flip, rows // 2)
            for j in range(2):
                out[j] = (kept[j, half, left:].astype(f32) + got[j, half, left:].astype(f32)).astype(out.dtype)

    shapes = [(rows, left), (2, rows // 2, rest)]
    return body, [keep, core], [(shape, dtype) for dtype in (bf16, f32) for shape in shapes], vmem


def cross_job(own_left, own_right, got_left, got_right, rows, cols, left):
    rows //= 2

    def body(ins, outs):
        lefts, rights, from_left, from_right = ins
        for flip, out in ((1, outs[0]), (0, outs[2])):
            half = half_of(1, flip, rows)
            out[...] = (lefts[half, :] + from_left[half, :].astype(f32)).astype(out.dtype)
        for j, out in ((1, outs[1]), (0, outs[3])):
            out[...] = (rights[j] + from_right[j].astype(f32)).astype(out.dtype)

    shapes = [(rows, left), (rows, cols - left)]
    return (
        body, [own_left, own_right, got_left, got_right], [(shape, dtype) for dtype in (bf16, f32) for shape in shapes],
        vmem,
    )


def merge_job(lefts, rights, rows, cols, left, bit):
    def body(ins, outs):
        for flip, out in ((1, outs[0]), (0, outs[1])):
            half = half_of(bit, flip, rows)
            out[:, :left] = (ins[0][half, :].astype(f32) + ins[1][half, :].astype(f32)).astype(out.dtype)
            out[:, left:] = (ins[2][half, :].astype(f32) + ins[3][half, :].astype(f32)).astype(out.dtype)

    return body, [*lefts, *rights], [((rows, cols), bf16), ((rows, cols), f32)], vmem


def join_job(mine, other, bit):
    rows, cols = mine.shape

    def body(ins, outs):
        for flip in (0, 1):
            outs[0][half_of(bit, flip, rows), :] = ins[flip][...]

    return body, [mine, other], [((2 * rows, cols), bf16)], vmem


def turn_job(mine, other, bit):
    rows, cols = mine.shape

    def body(ins, outs):
        for flip in (0, 1):
            outs[0][:, half_of(bit, flip, rows)] = ins[flip][...].astype(f32).T

    return body, [mine, other], [((cols, 2 * rows), f32)], hbm


def spread_body(plans, w_ref, gain_ref, *refs):
    ins, outs = refs[: 2 * len(plans)], refs[2 * len(plans) :]
    for c, plan in enumerate(plans):
        mine_ref, other_ref = ins[2 * c], ins[2 * c + 1]
        rows = mine_ref.shape[0]
        for flip, ref in ((0, mine_ref), (1, other_ref)):
            for begin, length, out, to in plan:
                outs[out][half_of(1, flip, rows), to : to + length] = ref[:, begin : begin + length].astype(f32)
    share = jnp.sum(outs[0][...] * w_ref[...].astype(f32), axis=1, keepdims=True)
    share = jnp.broadcast_to(share, (share.shape[0], PAIR)).T[0:1]
    outs[-1][...] = (share / gain_ref[...].astype(f32).reshape(1, -1)).reshape(-1)


def spread_job(weight, gain, sums, plans, shapes):
    arrays = [array for pair in sums for array in pair]
    outs = [(shape, f32) for shape in (*shapes, gain.shape)]
    return lambda ins, outs: spread_body(plans, *ins, *outs), [weight, gain, *arrays], outs, hbm


def after(value, *deps):
    return lax.optimization_barrier((value, *deps))[0] if deps else value


class Moves:
    def __init__(self, narrow, wide):
        self.narrow, self.wide = narrow, wide
        self.n = lax.axis_index("narrow")
        self.w = lax.axis_index("wide")
        self.starts = [self.n, self.w % 2, (self.w // 2) % 2]

    def swap(self, value, axis, bit):
        size = self.narrow if axis == "narrow" else self.wide
        return lax.ppermute(value, axis, [(i, i ^ bit) for i in range(size)])

    def place(self, start):
        self.starts.append(start)
        return len(self.starts) - 1

    def reduce(self, send, keep, left=0):
        rows, cols = send.shape[1:]
        core = self.swap(send, "narrow", 1)
        deps = yield (send,)
        core = after(core, *deps)
        if left:
            to_left, to_right, mine_left, mine_right = yield fork_job(keep, core, rows, cols, left)
            got_left, got_right = self.swap(to_left, "narrow", 2), self.swap(to_right, "wide", 1)
            deps = yield to_left, to_right
            to_left, to_right, mine_left, mine_right = yield cross_job(
                mine_left, mine_right, after(got_left, *deps), after(got_right, *deps), rows, cols, left
            )
            got_left, got_right = self.swap(to_left, "wide", 1), self.swap(to_right, "narrow", 2)
            deps = yield to_left, to_right
            rows //= 4
            total, mine = yield merge_job(
                (mine_left, after(got_left, *deps)), (mine_right, after(got_right, *deps)), rows, cols, left, 2
            )
        else:
            total, mine = yield part_job(keep, core, rows, cols)
            got = self.swap(total, "narrow", 2)
            deps = yield (total,)
            total, mine = yield halve_job([(mine, None), (after(got, *deps), None)], rows // 2, cols, 1)
            got = self.swap(total, "wide", 1)
            deps = yield (total,)
            rows //= 4
            total, mine = yield halve_job([(mine, None), (after(got, *deps), None)], rows, cols, 2)
        got = self.swap(total, "wide", 2)
        deps = yield (total,)
        terms = [(mine, None), (after(got, *deps), None)]
        bit = 4
        while bit < self.wide:
            if bit == 4:
                (total,) = yield add_job(terms, rows, cols)
            else:
                total = whole_call("add_terms", [add_job(terms, rows, cols)])[0][0]
            got = self.swap(total, "wide", bit)
            deps = (yield (total,)) if bit == 4 else ()
            terms = [(total, None), (after(got, *deps), None)]
            bit *= 2
        (total,) = yield add_job(terms, rows, cols)
        got = self.swap(total, "wide", 2)
        deps = yield (total,)
        (total,) = yield join_job(total, after(got, *deps), 2)
        got = self.swap(total, "wide", 1)
        deps = yield (total,)
        yield total, after(got, *deps)


def begin(chain):
    return next(chain)


def close(chain, *deps):
    return chain.send(deps)


def advance(chains, *deps):
    jobs = [chain.send(deps) for chain in chains]
    results = whole_call("gradient_sums", jobs)
    return [array for chain, result in zip(chains, results) for array in chain.send(result)]


def shards(narrow, wide, layer_input, cotangent, block_size, gain_attn, w_qkv, w_out, gain_mlp, w_up, b_up, w_down, b_down):
    moves = Moves(narrow, wide)
    x, d_y = layer_input[0], cotangent[0]
    rows, width = x.shape
    seq = rows // 2
    pairs = width // PAIR
    ff = w_up.shape[1]
    n, bit = moves.n, moves.w % 2

    size = w_qkv.shape[0] // 3
    at_qkv = [
        moves.place((n ^ j) * w_qkv.shape[0] + extra)
        for j, extra in (
            (0, 0), (1, 0), (2, bit * size), (2, 2 * size), (2, (1 - bit) * size),
            (3, bit * size), (3, 2 * size), (3, (1 - bit) * size),
        )
    ]
    at_row = [moves.place((n ^ j) * w_out.shape[0]) for j in range(4)]

    at_down = [moves.place((n ^ j) * w_down.shape[0]) for j in range(4)]
    size_up = w_up.shape[0] // 3
    at_up = [
        moves.place((n ^ j) * w_up.shape[0] + extra)
        for j, extra in (
            (0, 0), (1, 0), (2, bit * size_up), (2, 2 * size_up), (2, (1 - bit) * size_up),
            (3, bit * size_up), (3, 2 * size_up), (3, (1 - bit) * size_up),
        )
    ]
    index = jnp.stack(moves.starts).astype(jnp.int32)

    def ready(*deps):
        return after(index, *deps)

    freq = 10000.0 ** (-jnp.arange(HEAD // 2).astype(f32) / (HEAD // 2))
    angles = jnp.arange(seq).astype(f32)[:, None] * freq[None, :]
    cosine, sine = jnp.cos(angles), jnp.sin(angles)
    cosine = jnp.tile(cosine, (1, 4))
    sine = jnp.concatenate([-sine, sine, -sine, sine], axis=1)

    first, small = first_call(index, w_qkv, gain_attn, gain_mlp, b_down, b_up)
    got_first = moves.swap(first, "narrow", 2)
    (second,) = thirds_call(ready(first), w_qkv, (None,))
    got_second = moves.swap(second, "narrow", 2)
    up_first, up_second = thirds_call(ready(second), w_up, (1, None))
    got_near, got_small, up_near, out_near = (
        moves.swap(after(v, first), "narrow", 1) for v in (w_qkv, small, w_up, w_out)
    )
    up_far, up_more = moves.swap(up_first, "narrow", 2), moves.swap(up_second, "narrow", 2)
    paced = pace_call(ready(up_first), cosine)
    got_first, got_near, got_small, up_near, out_near, _ = lax.optimization_barrier(
        (got_first, got_near, got_small, up_near, out_near, paced)
    )
    got_cross = moves.swap(got_first, "wide", 1)
    far_first = moves.swap(got_first, "narrow", 1)
    out_far = moves.swap(after(w_out, got_first), "narrow", 2)
    far_second, far_cross = (moves.swap(v, "narrow", 1) for v in (got_second, got_cross))
    count = w_qkv.shape[0]
    qkv_w = Weight(
        [
            (array, rows_of, place)
            for (array, rows_of), place in zip(
                (
                    (w_qkv, count), (got_near, count), (got_first, size), (got_second, size), (got_cross, size),
                    (far_first, size), (far_second, size), (far_cross, size),
                ),
                at_qkv,
            )
        ]
    )
    smalls = [small, got_small, got_first, far_first]

    block = jnp.arange(TILE, dtype=jnp.int32) // block_size[0]
    row_block, col_block = block[:, None], block[None, :]
    same, less, upto, less_t, upto_t = (
        jnp.where(ok, 0.0, -1e30).astype(f32)
        for ok in (
            row_block == col_block, col_block < row_block, col_block <= row_block,
            row_block < col_block, row_block <= col_block,
        )
    )
    dyt = d_y.T

    qkv, a1t, vec, qkv_full = qkv_call(index, x, qkv_w, smalls, ff, cosine, sine)
    up_far = after(up_far, vec)
    up_cross = moves.swap(up_far, "wide", 1)
    down_far = moves.swap(after(w_down, up_far), "narrow", 2)
    o, ot, lse = att_call(ready(up_far), qkv, (same, less_t, upto_t), 0, pairs)
    up_pieces = [after(v, lse) for v in (up_far, up_more, up_cross)]
    up_last = [moves.swap(v, "narrow", 1) for v in up_pieces]
    out_far = after(out_far, lse)
    out_last = moves.swap(out_far, "narrow", 1)
    out_w = Weight([(a, w_out.shape[0], p) for a, p in zip((w_out, out_near, out_far, out_last), at_row)])
    up_w = Weight(
        [
            (a, r, p)
            for a, r, p in zip(
                (w_up, up_near, *up_pieces, *up_last), (w_up.shape[0],) * 2 + (size_up,) * 6, at_up
            )
        ]
    )
    x1, a2t, h, g, out_full, up_full = up_call(ready(lse), x, o, vec, out_w, up_w)
    send = grad_down_call(index, dyt, h, (1, 2), narrow)
    keep = grad_down_call(ready(send), dyt, h, (0, 2), narrow)
    down_far = after(down_far, keep)
    down_last = moves.swap(down_far, "narrow", 1)
    down_near = moves.swap(after(w_down, send), "narrow", 1)
    down_w = Weight([(a, w_down.shape[0], p) for a, p in zip((w_down, down_near, down_far, down_last), at_down)])
    chain_a = moves.reduce(send, keep, width // 2)
    begin(chain_a)
    d_u, dx1, dx1r, d_o, biases, down_full = down_call(
        ready(keep, *advance([chain_a], keep)), d_y, x1, g, vec, up_full, out_full, down_w
    )
    send, keep = grad_up_call(ready(*advance([chain_a], dx1r)), a2t, ot, d_u, dx1r, biases, narrow)
    chain_b = moves.reduce(send, keep, 2048)
    begin(chain_b)

    def back(start, count, *deps):
        return att_back_call(
            ready(*deps), qkv, d_o, o, lse, (same, less_t, upto_t), cosine, sine, start, count
        )

    paced = pace_call(ready(send), same)
    g0 = back(0, 2, keep, *advance([chain_a, chain_b], keep, paced))
    g1 = back(2, 2, g0[0], *advance([chain_a], g0[0]))
    g2 = back(4, 2, g1[0], *advance([chain_b], g1[0]))
    groups = [g0, g1, g2]
    rights = [array for group in groups for array in group]
    send, keep = grad_qkv_call(ready(*advance([chain_a, chain_b], g2[0])), a1t, rights, narrow)
    chain_c = moves.reduce(send, keep, 1152)
    begin(chain_c)
    paced = pace_call(ready(send), same)
    sent = advance([chain_b, chain_c], keep, paced)
    output = output_call(ready(keep, *sent), x1, h, vec, down_full)
    sent = advance([chain_a, chain_b, chain_c], output)
    d_input = input_call(ready(output, *sent), x, dx1, vec, groups, qkv_full)
    sent = advance([chain_b, chain_c], d_input)
    sum_a = close(chain_a, *sent)
    (grad_down,) = whole_call("last_down", [turn_job(*sum_a, 1)])[0]
    sent = advance([chain_c], *sent, grad_down)
    sent = advance([chain_c], *sent)
    sum_b = close(chain_b, *sent)
    sent = advance([chain_c], *sent)
    sum_c = close(chain_c)

    own = width // narrow
    grad_up, grad_out, biases, grad_gain_mlp = whole_call(
        "last_up",
        [
            spread_job(
                w_up, gain_mlp, [sum_b], [[(0, ff, 0, 0), (ff, width, 1, 0), (ff + width, TILE, 2, 0)]],
                [(own, ff), (own, width), (own, TILE)],
            )
        ],
    )[0]
    biases = biases[:8].reshape(-1)
    plan, begin_at, to = [], 0, 0
    for group in groups:
        cols = group[0].shape[1]
        for part in range(3):
            plan.append((begin_at, cols, 0, part * width + to))
            begin_at += cols
        to += cols
    grad_qkv, grad_gain_attn = whole_call("last_qkv", [spread_job(w_qkv, gain_attn, [sum_c], [plan], [(own, 3 * width)])])[0]
    return (
        output[None],
        d_input[None],
        grad_gain_attn,
        grad_qkv,
        grad_out,
        grad_gain_mlp,
        grad_up,
        biases[:width],
        grad_down,
        biases[width : width + own],
    )


def solution(mesh):
    return jax.shard_map(
        functools.partial(shards, mesh.shape["narrow"], mesh.shape["wide"]),
        mesh=mesh,
        in_specs=(
            P(("wide", "narrow"), None, None),
            P(("wide", "narrow"), None, None),
            P(("wide", "narrow")),
            P("narrow"),
            P("narrow", None),
            P("narrow", None),
            P("narrow"),
            P("narrow", None),
            P("narrow"),
            P("narrow", None),
            P("narrow"),
        ),
        out_specs=(
            P(("wide", "narrow"), None, None),
            P(("wide", "narrow"), None, None),
            P("narrow"),
            P("narrow", None),
            P("narrow", None),
            P("narrow"),
            P("narrow", None),
            P("narrow"),
            P("narrow", None),
            P("narrow"),
        ),
        check_vma=False,
    )
```

```python
import functools
import math

import jax
import jax.numpy as jnp
from jax import lax
from jax.experimental import pallas as pl
from jax.experimental.pallas import tpu as pltpu
from jax.sharding import PartitionSpec as P

HEAD = 64
PAIR = 2 * HEAD
TILE = 128
ORDER = (1, 3, 0, 2)
SPAN = 256
LOG2E = 1.4426950408889634
LN2 = 0.6931471805599453
f32 = jnp.float32
bf16 = jnp.bfloat16
MIB = 1 << 20


def nn(left, right):
    return jnp.dot(left, right, preferred_element_type=f32)


def nt(left, right):
    return lax.dot_general(left, right, (((1,), (1,)), ((), ())), preferred_element_type=f32)


def norm_rows(values):
    centre = values - jnp.mean(values, axis=-1, keepdims=True)
    inverse = lax.rsqrt(jnp.mean(centre * centre, axis=-1, keepdims=True) + 1e-05)
    return centre * inverse, inverse


def norm_back(d_norm, scaled, inverse, gain):
    d_scaled = d_norm * gain
    return inverse * (
        d_scaled
        - jnp.mean(d_scaled, axis=-1, keepdims=True)
        - scaled * jnp.mean(d_scaled * scaled, axis=-1, keepdims=True)
    )


def swap_halves(tile):
    lane = lax.broadcasted_iota(jnp.int32, (1, PAIR), 1) % HEAD
    return jnp.where(
        lane < HEAD // 2,
        pltpu.roll(tile, PAIR - HEAD // 2, 1),
        pltpu.roll(tile, HEAD // 2, 1),
    )


class Weight:
    def __init__(self, pieces):
        self.arrays = [array for array, _, _ in pieces]
        self.plan = [(rows, place) for _, rows, place in pieces]
        self.rows = sum(rows for rows, _ in self.plan)
        self.cols = self.arrays[0].shape[1]

    def specs(self, near=True):
        space = pltpu.VMEM if near else pltpu.HBM
        return [pl.BlockSpec(memory_space=pltpu.HBM)] + [pl.BlockSpec(memory_space=space)] * (len(self.plan) - 1)

    def near(self, at):
        return list(range(at + 1, at + len(self.plan)))

    def whole(self):
        return pltpu.VMEM((self.rows, self.cols), bf16)

    def sems(self):
        return [pltpu.SemaphoreType.DMA((len(self.plan),))]

    def scratch(self):
        return [self.whole(), *self.sems()]


def fetches(at_ref, plan, parts, whole, sems):
    copies = []
    for i, ((rows, place), part) in enumerate(zip(plan, parts)):
        start = pl.multiple_of(at_ref[place], math.gcd(rows, 256))
        copies.append(pltpu.make_async_copy(part.at[pl.ds(0, rows)], whole.at[pl.ds(start, rows)], sems.at[i]))
    return copies


def fetch(at_ref, *weights):
    @pl.when(pl.program_id(0) == 0)
    def _():
        for weight in weights:
            for copy in fetches(at_ref, *weight):
                copy.start()


def arrive(at_ref, weight):
    @pl.when(pl.program_id(0) == 0)
    def _():
        for copy in fetches(at_ref, *weight):
            copy.wait()


def step_rows(step):
    return pl.ds(pl.multiple_of(pl.program_id(0) * step, step), step)


def take(refs, *groups):
    out, at = [], 0
    for group in groups:
        out.append(refs[at : at + len(group)])
        at += len(group)
    return out + [refs[at:]]


def fixed(shape):
    return pl.BlockSpec(shape, lambda *_: (0,) * len(shape), pipeline_mode=pl.Buffered(1))


def call(body, name, grid, in_specs, out_specs, out_shape, scratch, limit, cost, near=(), aliases=None, moved=1 << 20):
    fun = pl.pallas_call(
        body,
        name=name,
        out_shape=out_shape,
        input_output_aliases=aliases or {},
        grid_spec=pltpu.PrefetchScalarGridSpec(
            num_scalar_prefetch=1,
            grid=grid,
            in_specs=in_specs,
            out_specs=out_specs,
            scratch_shapes=scratch,
        ),
        compiler_params=pltpu.CompilerParams(
            dimension_semantics=("arbitrary",) * len(grid), vmem_limit_bytes=limit * MIB
        ),
        cost_estimate=pl.CostEstimate(
            flops=int(cost * 1e12), bytes_accessed=moved, transcendentals=0
        ),
    )

    def run(index, *args):
        args = [
            pltpu.with_memory_space_constraint(arg, pltpu.VMEM if i in near else pltpu.HBM)
            for i, arg in enumerate(args)
        ]
        return fun(index, *args)

    return run


def hbm(shape, dtype):
    return pltpu.HBM(shape, dtype)


def vmem(shape, dtype):
    return pltpu.VMEM(shape, dtype)


def sds(shape, dtype):
    return jax.ShapeDtypeStruct(shape, dtype)


def small_rows(cols, gain1_ref, gain2_ref, down_ref, up_ref):
    def lanes(*refs):
        values = [ref[...].astype(f32).reshape(1, -1) for ref in refs]
        return jnp.concatenate(
            [v for v in values for _ in range(cols // (len(refs) * v.shape[1]))], axis=1
        )

    row = lax.broadcasted_iota(jnp.int32, (8, cols), 0)
    return jnp.where(row == 0, lanes(gain1_ref, gain2_ref, down_ref), lanes(up_ref)).astype(bf16)


def vector_body(idx_ref, w_ref, gain1_ref, gain2_ref, down_ref, up_ref, out_ref, small_ref):
    size = w_ref.shape[0]
    small = small_rows(w_ref.shape[1], gain1_ref, gain2_ref, down_ref, up_ref)
    out_ref[:size, :] = w_ref[...]
    out_ref[size:, :] = small
    small_ref[...] = small


def vector_call(index, weight, *vectors):
    size, cols = weight.shape[0] // 3, weight.shape[1]
    shapes = [(size + 8, cols), (8, cols)]
    return call(
        vector_body,
        "vector_message",
        (1,),
        [pl.BlockSpec((size, cols), lambda i, s: (2, 0))] + [fixed(v.shape) for v in vectors],
        [fixed(shape) for shape in shapes],
        [vmem(shape, bf16) for shape in shapes],
        [],
        6,
        1.5,
    )(index, weight, *vectors)


def thirds_body(idx_ref, *refs):
    count = len(refs) // 2
    for ref, out_ref in zip(refs[:count], refs[count:]):
        out_ref[...] = ref[...]


def thirds_call(index, weight, places):
    size, cols = weight.shape[0] // 3, weight.shape[1]
    return call(
        thirds_body,
        "next_message",
        (1,),
        [pl.BlockSpec((size, cols), lambda i, s, p=p: (2 if p is None else s[p], 0)) for p in places],
        [fixed((size, cols))] * len(places),
        [vmem((size, cols), bf16)] * len(places),
        [],
        6,
        1.5,
    )(index, *[weight] * len(places))


def qkv_body(plan, n, idx_ref, x_ref, cos_ref, sin_ref, *refs):
    smalls, parts, refs = take(refs, range(n), plan)
    qkv_ref, a1t_ref, vec_ref, whole, sems = refs
    weight = (plan, parts, whole, sems)
    fetch(idx_ref, weight)
    width = x_ref.shape[1]
    here = step_rows(x_ref.shape[0])

    @pl.when(pl.program_id(0) == 0)
    def _():
        lane = lax.broadcasted_iota(jnp.int32, (1, width), 1) // (width // n)
        values = [ref[...].astype(f32) for ref in smalls]
        vec_ref[...] = jnp.zeros_like(vec_ref)
        for i in range(3):
            vec_ref[i : i + 1, :width] = sum(
                jnp.where(lane == (idx_ref[0] ^ j), v[0:1, i * width : (i + 1) * width], 0.0)
                for j, v in enumerate(values)
            )
        size = vec_ref.shape[1] // n
        for c in range(n):
            vec_ref[3:4, c * size : (c + 1) * size] = sum(
                jnp.where((idx_ref[0] ^ j) == c, v[1:2, :size], 0.0) for j, v in enumerate(values)
            )

    scaled, _ = norm_rows(x_ref[...].astype(f32))
    a1 = (scaled * vec_ref[0:1, :width]).astype(bf16)
    a1t_ref[...] = a1.T
    cosine, sine = cos_ref[...], sin_ref[...]
    arrive(idx_ref, weight)
    for part in range(3):
        y = nn(a1, whole[:, part * width : (part + 1) * width])
        if part == 2:
            qkv_ref[here, part * width :] = y.astype(bf16)
            continue
        for t in range(width // PAIR):
            tile = y[:, t * PAIR : (t + 1) * PAIR]
            tile = tile * cosine + swap_halves(tile) * sine
            if part == 0:
                tile = tile * (LOG2E / 8.0)
            at = part * width + t * PAIR
            qkv_ref[here, at : at + PAIR] = tile.astype(bf16)


def qkv_call(index, x, weight, smalls, ff, cosine, sine):
    rows, width = x.shape
    wide = weight.cols
    step = 256
    per = cosine.shape[0] // step

    def vector(array):
        return pl.BlockSpec((8, wide), lambda i, s: (array.shape[0] // 8 - 1, 0))

    return call(
        functools.partial(qkv_body, weight.plan, len(smalls)),
        "norm_qkv",
        (rows // step,),
        [
            pl.BlockSpec((step, width), lambda i, s: (i, 0)),
            pl.BlockSpec((step, PAIR), lambda i, s: (i % per, 0)),
            pl.BlockSpec((step, PAIR), lambda i, s: (i % per, 0)),
        ]
        + [vector(array) for array in smalls]
        + weight.specs(),
        [
            fixed((rows, wide)),
            pl.BlockSpec((width, step), lambda i, s: (0, i)),
            pl.BlockSpec((8, ff), lambda i, s: (0, 0)),
            fixed((weight.rows, wide)),
        ],
        [vmem((rows, wide), bf16), hbm((width, rows), bf16), hbm((8, ff), f32), hbm((weight.rows, wide), bf16)],
        weight.sems(),
        16,
        7,
        near=(*range(3, 3 + len(smalls)), *weight.near(3 + len(smalls))),
    )(index, x, cosine, sine, *smalls, *weight.arrays)


def head_masks():
    lane = lax.broadcasted_iota(jnp.int32, (1, PAIR), 1)
    return lane < HEAD, lane >= HEAD


def widen(tile, allowed):
    count = SPAN // TILE
    never = jnp.full(tile.shape, -1e30, f32)
    before = jnp.zeros(tile.shape, f32) if allowed else never
    return jnp.concatenate(
        [
            jnp.concatenate([tile if a == b else (before if a < b else never) for b in range(count)], axis=1)
            for a in range(count)
        ],
        axis=0,
    )


def att_body(seq, idx_ref, qkv_ref, same_ref, less_ref, upto_ref, o_ref, ot_ref, lse_ref):
    def columns(part):
        start = part * (qkv_ref.shape[1] // 3) + pl.program_id(0) * PAIR
        return pl.ds(pl.multiple_of(start, PAIR), PAIR)

    queries, k_all = columns(0), qkv_ref[:, columns(1)]
    keys = [jnp.where(m, k_all, jnp.zeros_like(k_all)) for m in head_masks()]
    v_t = qkv_ref[:, columns(2)].T
    ones = jnp.ones((16, 2 * seq), bf16)
    vals = [jnp.concatenate([v_t[h * HEAD : (h + 1) * HEAD], ones], axis=0) for h in range(2)]
    same, less, upto = widen(same_ref[...], False), widen(less_ref[...], True), widen(upto_ref[...], True)

    def scores(lo, clean, h):
        hi = lo + SPAN
        row = lo + seq if clean else lo
        query = qkv_ref[row : row + SPAN, queries]
        pieces = [nt(keys[h][seq + lo : seq + hi], query) + (upto if clean else less)]
        if lo > 0:
            pieces.append(nt(keys[h][seq : seq + lo], query))
        if not clean:
            pieces.append(nt(keys[h][lo:hi], query) + same)
        return pieces

    def soften(pieces):
        top = functools.reduce(jnp.maximum, [jnp.max(p, axis=0, keepdims=True) for p in pieces])
        return top, [jnp.exp2(p - top).astype(bf16) for p in pieces]

    def mix(lo, clean, h, weights):
        hi = lo + SPAN
        out = nn(vals[h][:, seq + lo : seq + hi], weights[0])
        if lo > 0:
            out = out + nn(vals[h][:, seq : seq + lo], weights[1])
        if not clean:
            out = out + nn(vals[h][:, lo:hi], weights[-1])
        return out

    def finish(lo, clean, softened):
        row = lo + seq if clean else lo
        outs = [mix(lo, clean, h, softened[h][1]) for h in range(2)]
        out = jnp.concatenate([o[:HEAD] / o[HEAD : HEAD + 1] for o in outs], axis=0)
        ot_ref[:, row : row + SPAN] = out.astype(bf16)
        o_ref[row : row + SPAN, :] = out.T.astype(bf16)
        for h in range(2):
            lse_ref[0, h : h + 1, row : row + SPAN] = softened[h][0] + jnp.log2(outs[h][HEAD : HEAD + 1])

    work = [(lo, clean) for lo in range(0, seq, SPAN) for clean in (False, True)]
    ahead = [scores(*work[0], h) for h in range(2)]
    behind = None
    for i, item in enumerate(work):
        now = ahead
        if i + 1 < len(work):
            ahead = [scores(*work[i + 1], h) for h in range(2)]
        softened = [soften(pieces) for pieces in now]
        if behind is not None:
            finish(*behind)
        behind = (*item, softened)
    finish(*behind)


def att_call(index, qkv, masks):
    rows = qkv.shape[0]
    width = qkv.shape[1] // 3
    pairs = width // PAIR
    return call(
        functools.partial(att_body, rows // 2),
        "attention",
        (pairs,),
        [fixed(qkv.shape)] + [fixed((TILE, TILE))] * 3,
        [
            pl.BlockSpec((rows, PAIR), lambda p, s: (0, p)),
            pl.BlockSpec((PAIR, rows), lambda p, s: (p, 0)),
            pl.BlockSpec((1, 2, rows), lambda p, s: (p, 0, 0)),
        ],
        [hbm((rows, width), bf16), hbm((width, rows), bf16), hbm((pairs, 2, rows), f32)],
        [],
        16,
        12.0,
        near=(0,),
    )(index, qkv, *masks)


def att_back_body(
    seq, idx_ref, q_ref, k_ref, v_ref, do_ref, o_ref, lse_ref, same_ref, less_ref, upto_ref,
    cos_ref, sin_ref, dq_ref, dk_ref, dv_ref, dqt_ref,
):
    first, second = head_masks()
    q_all, k_all, v_all, do_all = q_ref[...], k_ref[...], v_ref[...], do_ref[...]

    def split(array):
        return [jnp.where(m, array, jnp.zeros_like(array)) for m in (first, second)]

    queries, keys, vals, dos = split(q_all), split(k_all), split(v_all), split(do_all)
    keys_t = k_all.T
    product = do_all.astype(f32) * o_ref[...].astype(f32)
    high = product.astype(bf16)
    rest = (product - high.astype(f32)).astype(bf16)
    picked = lax.broadcasted_iota(jnp.int32, (8, PAIR), 0)
    picked = jnp.where(picked == lax.broadcasted_iota(jnp.int32, (8, PAIR), 1) // HEAD, 1.0, 0.0).astype(bf16)
    delta = nt(picked, high) + nt(picked, rest)
    same, less, upto = widen(same_ref[...], False), widen(less_ref[...], True), widen(upto_ref[...], True)
    dqt_ref[...] = jnp.zeros_like(dqt_ref)

    def products(unit):
        return [
            (nt(keys[h][k : k + SPAN], q_all[q:end]), nt(vals[h][k : k + SPAN], do_all[q:end]))
            for h, k, q, end, _ in unit[0]
        ]

    def soften(unit, values):
        out = []
        for (h, _, q, end, mask), (scores, d_probs) in zip(unit[0], values):
            scores = scores - lse_ref[0, h : h + 1, q:end]
            probs = jnp.exp2(scores[:, :SPAN] + mask)
            if end - q > SPAN:
                probs = jnp.concatenate([probs, jnp.exp2(scores[:, SPAN:])], axis=1)
            d_scores = probs * (d_probs - delta[h : h + 1, q:end])
            out.append((probs.astype(bf16), d_scores.astype(bf16)))
        return out

    def rotate_back(tile, row):
        at = row % seq
        cosine, sine = cos_ref[at : at + SPAN, :], sin_ref[at : at + SPAN, :]
        return tile * cosine - swap_halves(tile) * sine

    def gather(unit, values, sums):
        items, last = unit
        d_vals, d_keys = sums
        for (h, k, q, end, _), (probs, d_scores) in zip(items, values):
            d_vals = d_vals + nn(probs, dos[h][q:end])
            d_keys = d_keys + nn(d_scores, queries[h][q:end])
            at = slice(h * HEAD, (h + 1) * HEAD)
            dqt_ref[at, q:end] += nn(keys_t[at, k : k + SPAN], d_scores)
        if not last:
            return d_vals, d_keys
        k = items[0][1]
        dv_ref[k : k + SPAN, :] = d_vals.astype(bf16)
        dk_ref[k : k + SPAN, :] = rotate_back(d_keys * LN2, k).astype(bf16)
        return 0.0, 0.0

    units = []
    for lo in range(0, seq, SPAN):
        units.append(([(h, lo, lo, lo + SPAN, same) for h in range(2)], True))
        for base, mask in ((0, less), (seq, upto)):
            units.append(([(h, seq + lo, base + lo, base + seq, mask) for h in range(2)], base > 0))
    ahead, behind, sums = products(units[0]), None, (0.0, 0.0)
    for i, unit in enumerate(units):
        now = ahead
        if i + 1 < len(units):
            ahead = products(units[i + 1])
        values = soften(unit, now)
        if behind is not None:
            sums = gather(*behind, sums)
        behind = (unit, values)
    gather(*behind, sums)
    for r in range(0, 2 * seq, SPAN):
        tile = dqt_ref[:, r : r + SPAN].T * 0.125
        dq_ref[r : r + SPAN, :] = rotate_back(tile, r).astype(bf16)


def att_back_call(index, qkv, d_o, o, lse, masks, cosine, sine, start, count):
    rows = qkv.shape[0]
    width = qkv.shape[1] // 3
    pairs = width // PAIR
    seq = rows // 2

    def column(part):
        return pl.BlockSpec((rows, PAIR), lambda p, s: (0, part * pairs + start + p))

    out = pl.BlockSpec((rows, PAIR), lambda p, s: (0, p))
    return call(
        functools.partial(att_back_body, seq),
        "attention_back",
        (count,),
        [column(0), column(1), column(2), column(0), column(0)]
        + [pl.BlockSpec((1, 2, rows), lambda p, s: (start + p, 0, 0))]
        + [fixed((TILE, TILE))] * 3
        + [fixed((seq, PAIR))] * 2,
        [out] * 3,
        [vmem((rows, count * PAIR), bf16)] * 3,
        [pltpu.VMEM((PAIR, rows), f32)],
        16,
        3.6 * count,
    )(index, qkv, qkv, qkv, d_o, o, lse, *masks, cosine, sine)


def up_body(out_at, up_at, idx_ref, x_ref, o_ref, vec_ref, *refs):
    outs, ups, refs = take(refs, out_at, up_at)
    x1_ref, a2t_ref, h_ref, g_ref, w_out, w_up, out_sems, up_sems = refs
    out_weight, up_weight = (out_at, outs, w_out, out_sems), (up_at, ups, w_up, up_sems)
    fetch(idx_ref, out_weight, up_weight)
    arrive(idx_ref, out_weight)
    width = x_ref.shape[1]
    here = step_rows(x_ref.shape[0])
    x1 = x_ref[...].astype(f32) + nn(o_ref[...], w_out[...])
    x1_ref[...] = x1
    scaled, _ = norm_rows(x1)
    a2 = (scaled * vec_ref[1:2, :width]).astype(bf16)
    a2t_ref[:, here] = a2.T
    arrive(idx_ref, up_weight)
    c0 = math.sqrt(2.0 / math.pi)
    c1 = c0 * 0.044715
    chunk = 512
    for at in range(0, w_up.shape[1], chunk):
        u = nn(a2, w_up[:, at : at + chunk]) + vec_ref[3:4, at : at + chunk]
        square = u * u
        t = jnp.tanh(u * (c1 * square + c0))
        half = 0.5 * t + 0.5
        h_ref[here, at : at + chunk] = (u * half).astype(bf16)
        slope = u * (1.5 * c1 * square + 0.5 * c0)
        g_ref[here, at : at + chunk] = (half + slope * (1.0 - t * t)).astype(bf16)


def up_call(index, x, o, vec, w_out, w_up):
    rows, width = x.shape
    ff = w_up.cols
    step = 256

    def row(cols):
        return pl.BlockSpec((step, cols), lambda i, s: (i, 0))

    outs = [
        hbm((rows, width), f32), vmem((width, rows), bf16), vmem((rows, ff), bf16), vmem((rows, ff), bf16),
        w_out.whole(), w_up.whole(),
    ]
    return call(
        functools.partial(up_body, w_out.plan, w_up.plan),
        "feed_up",
        (rows // step,),
        [row(width), row(width), fixed(vec.shape)] + w_out.specs() + w_up.specs(),
        [row(width)] + [fixed(out.shape) for out in outs[1:]],
        outs,
        w_out.sems() + w_up.sems(),
        12,
        18,
        near=w_out.near(3) + w_up.near(3 + len(w_out.plan)),
    )(index, x, o, vec, *w_out.arrays, *w_up.arrays)


def down_body(down_at, idx_ref, dy_ref, x1_ref, g_ref, vec_ref, w_up, w_out, *refs):
    downs, refs = take(refs, down_at)
    du_ref, dx1_ref, dx1r_ref, do_ref, bias_ref, w_down, down_sems = refs
    weight = (down_at, downs, w_down, down_sems)
    fetch(idx_ref, weight)

    @pl.when(pl.program_id(0) == 0)
    def _():
        bias_ref[...] = jnp.zeros_like(bias_ref)

    width = dy_ref.shape[1]
    here = step_rows(dy_ref.shape[0])
    low = dy_ref[...]
    d_y = low.astype(f32)
    bias_ref[1:2, :width] += jnp.sum(d_y, axis=0, keepdims=True)
    arrive(idx_ref, weight)
    chunk = 512
    d_a2 = 0.0
    for at in range(0, w_up.shape[1], chunk):
        d_u = nt(low, w_down[at : at + chunk, :]) * g_ref[here, at : at + chunk].astype(f32)
        bias_ref[0:1, at : at + chunk] += jnp.sum(d_u, axis=0, keepdims=True)
        d_u = d_u.astype(bf16)
        du_ref[here, at : at + chunk] = d_u
        d_a2 = d_a2 + nt(d_u, w_up[:, at : at + chunk])
    scaled, inverse = norm_rows(x1_ref[...])
    d_x1 = d_y + norm_back(d_a2, scaled, inverse, vec_ref[1:2, :width])
    dx1_ref[...] = d_x1
    d_x1 = d_x1.astype(bf16)
    dx1r_ref[here, :] = d_x1
    do_ref[...] = nt(d_x1, w_out[...]).astype(bf16)


def down_call(index, d_y, x1, g, vec, w_up, w_out, w_down):
    rows, width = d_y.shape
    ff = w_up.shape[1]
    step = 256

    def row(cols):
        return pl.BlockSpec((step, cols), lambda i, s: (i, 0))

    return call(
        functools.partial(down_body, w_down.plan),
        "feed_back",
        (rows // step,),
        [row(width), row(width)] + [fixed(array.shape) for array in (g, vec, w_up, w_out)] + w_down.specs(),
        [fixed((rows, ff)), row(width), fixed((rows, width)), row(width), fixed((2, ff)),
         fixed((ff, width))],
        [
            vmem((rows, ff), bf16), hbm((rows, width), f32), vmem((rows, width), bf16),
            hbm((rows, width), bf16), vmem((2, ff), f32), w_down.whole(),
        ],
        w_down.sems(),
        14,
        20,
        near=(2, 4, 5, *w_down.near(6)),
    )(index, d_y, x1, g, vec, w_up, w_out, *w_down.arrays)


def grad_down_body(offsets, idx_ref, dyt_ref, h_ref, out_ref):
    base, step = offsets
    cols = out_ref.shape[2]
    shard = idx_ref[0] ^ (base + step * pl.program_id(0))
    columns = pl.ds(pl.multiple_of(shard * cols, cols), cols)
    out_ref[pl.program_id(0)] = nn(dyt_ref[...], h_ref[:, columns]).astype(bf16)


def grad_down_call(index, dyt, h, offsets, shards):
    width, rows = dyt.shape
    cols = h.shape[1] // shards
    return call(
        functools.partial(grad_down_body, offsets),
        "grad_down",
        (2,),
        [fixed(dyt.shape), fixed(h.shape)],
        fixed((2, width, cols)),
        vmem((2, width, cols), bf16),
        [],
        8,
        3,
        near=(0, 1),
    )(index, dyt, h)


def shard_rows(idx_ref, rows):
    return [pl.ds(pl.multiple_of((idx_ref[0] ^ j) * rows, math.gcd(rows, 256)), rows) for j in ORDER]


def grad_up_body(chunks, idx_ref, a_ref, o_ref, du_ref, dx_ref, bias_ref, send_ref, keep_ref):
    rows = send_ref.shape[1]
    width = dx_ref.shape[1]
    i = pl.program_id(0)
    columns = pl.ds(pl.multiple_of(i * width, width), width)
    shards_at = shard_rows(idx_ref, rows)

    def write(left, right):
        y = nn(jnp.concatenate([left[at, :] for at in shards_at], axis=0), right).astype(bf16)
        for k in range(4):
            (send_ref if k < 2 else keep_ref)[k % 2, :, columns] = y[k * rows : (k + 1) * rows]

    @pl.when(i < chunks)
    def _():
        write(a_ref, du_ref[:, columns])

    @pl.when(i == chunks)
    def _():
        write(o_ref, dx_ref[...])
        at = (chunks + 1) * width
        lanes = send_ref.shape[2] - at
        shards = width // rows
        pad = jnp.zeros((1, 2 * lanes - rows), f32)
        for k, j in enumerate(ORDER):
            shard = idx_ref[0] ^ j
            out_ref = send_ref if k < 2 else keep_ref
            tiles = [
                bias_ref[0:1, pl.ds(pl.multiple_of(shard * width + t * lanes, lanes), lanes)]
                for t in range(width // lanes)
            ]
            own = sum(
                jnp.where(shard == t, bias_ref[1:2, t * rows : (t + 1) * rows], 0.0) for t in range(shards)
            )
            own = jnp.concatenate([own, pad], axis=1)
            tiles += [own[:, :lanes], own[:, lanes:]]
            block = jnp.concatenate(tiles + [jnp.zeros((16 - len(tiles), lanes), f32)], axis=0)
            out_ref[k % 2, :16, at:] = block.astype(bf16)
            out_ref[k % 2, 16:, at:] = jnp.zeros((rows - 16, lanes), bf16)


def grad_up_call(index, a2t, ot, d_u, dx1r, biases, shards):
    width, rows = a2t.shape
    own = width // shards
    ff = d_u.shape[1]
    chunks = ff // width
    cols = ff + width + TILE
    return call(
        functools.partial(grad_up_body, chunks),
        "grad_up_out",
        (chunks + 1,),
        [fixed(array.shape) for array in (a2t, ot, d_u, dx1r, biases)],
        [fixed((2, own, cols))] * 2,
        [vmem((2, own, cols), bf16)] * 2,
        [],
        10,
        4.7,
        near=range(5),
    )(index, a2t, ot, d_u, dx1r, biases)


def grad_qkv_body(idx_ref, a_ref, *refs):
    rights, send_ref, keep_ref = refs[:-2], refs[-2], refs[-1]
    rows = send_ref.shape[1]
    left = jnp.concatenate([a_ref[at, :] for at in shard_rows(idx_ref, rows)], axis=0)
    at = 0
    for right in rights:
        cols = right.shape[1]
        y = nn(left, right[...]).astype(bf16)
        for k in range(4):
            (send_ref if k < 2 else keep_ref)[k % 2, :, at : at + cols] = y[k * rows : (k + 1) * rows]
        at += cols


def grad_qkv_call(index, a1t, rights, shards):
    own = a1t.shape[0] // shards
    cols = sum(right.shape[1] for right in rights)
    return call(
        grad_qkv_body,
        "grad_qkv",
        (1,),
        [fixed(array.shape) for array in (a1t, *rights)],
        [fixed((2, own, cols))] * 2,
        [vmem((2, own, cols), bf16)] * 2,
        [],
        10,
        1.0 + cols / 1000.0,
        near=range(1 + len(rights)),
    )(index, a1t, *rights)


def input_body(groups, idx_ref, x_ref, dx1_ref, vec_ref, w_ref, *refs):
    grads, (dx_ref,) = refs[: 3 * groups], refs[3 * groups :]
    width = x_ref.shape[1]
    here = step_rows(x_ref.shape[0])
    scaled, inverse = norm_rows(x_ref[...].astype(f32))
    d_a1 = 0.0
    for part in range(3):
        at = part * width
        for g in range(groups):
            ref = grads[3 * g + part]
            cols = ref.shape[1]
            d_a1 = d_a1 + nt(ref[here, :], w_ref[:, at : at + cols])
            at += cols
    d_x = dx1_ref[...] + norm_back(d_a1, scaled, inverse, vec_ref[0:1, :width])
    dx_ref[...] = d_x.astype(bf16)


def input_call(index, x, dx1, vec, d_groups, weight):
    rows, width = x.shape
    step = 256

    def row(cols):
        return pl.BlockSpec((step, cols), lambda i, s: (i, 0))

    flat = [array for group in d_groups for array in group]
    return call(
        functools.partial(input_body, len(d_groups)),
        "grad_input",
        (rows // step,),
        [row(width), row(width)] + [fixed(array.shape) for array in (vec, weight, *flat)],
        row(width),
        hbm((rows, width), bf16),
        [],
        14,
        9,
        near=range(4, 4 + len(flat)),
    )(index, x, dx1, vec, weight, *flat)


def output_body(idx_ref, x1_ref, h_ref, vec_ref, w_ref, out_ref):
    y = x1_ref[...] + nn(h_ref[...], w_ref[...]) + vec_ref[2:3, : x1_ref.shape[1]]
    out_ref[...] = y.astype(bf16)


def output_call(index, x1, h, vec, weight):
    rows, width = x1.shape

    def row(cols):
        return pl.BlockSpec((256, cols), lambda i, s: (i, 0))

    return call(
        output_body,
        "layer_output",
        (rows // 256,),
        [row(width), row(h.shape[1]), fixed(vec.shape), fixed(weight.shape)],
        row(width),
        hbm((rows, width), bf16),
        [],
        14,
        8,
        near=(3,),
    )(index, x1, h, vec, weight)


def pace_body(idx_ref, tile_ref, out_ref):
    out_ref[...] = tile_ref[:8, :]


def pace_call(index, tile):
    return call(
        pace_body,
        "pace",
        (1,),
        [fixed(tile.shape)],
        fixed((8, tile.shape[1])),
        vmem((8, tile.shape[1]), f32),
        [],
        2,
        5,
        near=(0,),
    )(index, tile)


def whole_call(name, jobs):
    arrays = [array for _, ins, _, _ in jobs for array in ins]
    results = [place(shape, dtype) for _, _, outs, place in jobs for shape, dtype in outs]

    def run(*refs):
        ins, outs = refs[: len(arrays)], refs[len(arrays) :]
        at, to = 0, 0
        for body, job_ins, job_outs, _ in jobs:
            body(ins[at : at + len(job_ins)], outs[to : to + len(job_outs)])
            at, to = at + len(job_ins), to + len(job_outs)

    flat = pl.pallas_call(
        run,
        name=name,
        in_specs=[pl.BlockSpec(memory_space=pltpu.VMEM)] * len(arrays),
        out_specs=[pl.BlockSpec(memory_space=pltpu.VMEM)] * len(results),
        out_shape=results,
        compiler_params=pltpu.CompilerParams(vmem_limit_bytes=10 * MIB),
        cost_estimate=pl.CostEstimate(
            flops=0,
            bytes_accessed=sum(array.size * array.dtype.itemsize for array in arrays),
            transcendentals=0,
        ),
    )(*(pltpu.with_memory_space_constraint(array, pltpu.VMEM) for array in arrays))
    groups, at = [], 0
    for _, _, outs, _ in jobs:
        groups.append(flat[at : at + len(outs)])
        at += len(outs)
    return groups


def half_of(bit, flip, rows):
    mine = (lax.axis_index("wide") // bit) % 2
    return pl.ds(pl.multiple_of((1 - mine if flip else mine) * rows, math.gcd(rows, 256)), rows)


def add_job(terms, rows, cols):
    def body(ins, outs):
        outs[0][...] = sum(
            (ref[...] if lead is None else ref[lead]).astype(f32) for ref, (_, lead) in zip(ins, terms)
        ).astype(bf16)

    return body, [a for a, _ in terms], [((rows, cols), bf16)], vmem


def halve_job(terms, rows, cols, bit):
    def body(ins, outs):
        for flip, out in ((1, outs[0]), (0, outs[1])):
            half = half_of(bit, flip, rows)
            out[...] = sum(
                (ref[half, :] if lead is None else ref[lead, half, :]).astype(f32)
                for ref, (_, lead) in zip(ins, terms)
            ).astype(out.dtype)

    return body, [a for a, _ in terms], [((rows, cols), bf16), ((rows, cols), f32)], vmem


def part_job(keep, core, rows, cols):
    def body(ins, outs):
        kept, got = ins
        for j, out in ((1, outs[0]), (0, outs[1])):
            out[...] = (kept[j].astype(f32) + got[j].astype(f32)).astype(out.dtype)

    return body, [keep, core], [((rows, cols), bf16), ((rows, cols), f32)], vmem


def fork_job(keep, core, rows, cols, left):
    rest = cols - left

    def body(ins, outs):
        kept, got = ins
        for j, out in ((1, outs[0]), (0, outs[2])):
            out[...] = (kept[j, :, :left].astype(f32) + got[j, :, :left].astype(f32)).astype(out.dtype)
        for flip, out in ((1, outs[1]), (0, outs[3])):
            half = half_of(1, flip, rows // 2)
            for j in range(2):
                out[j] = (kept[j, half, left:].astype(f32) + got[j, half, left:].astype(f32)).astype(out.dtype)

    shapes = [(rows, left), (2, rows // 2, rest)]
    return body, [keep, core], [(shape, dtype) for dtype in (bf16, f32) for shape in shapes], vmem


def cross_job(own_left, own_right, got_left, got_right, rows, cols, left):
    rows //= 2

    def body(ins, outs):
        lefts, rights, from_left, from_right = ins
        for flip, out in ((1, outs[0]), (0, outs[2])):
            half = half_of(1, flip, rows)
            out[...] = (lefts[half, :] + from_left[half, :].astype(f32)).astype(out.dtype)
        for j, out in ((1, outs[1]), (0, outs[3])):
            out[...] = (rights[j] + from_right[j].astype(f32)).astype(out.dtype)

    shapes = [(rows, left), (rows, cols - left)]
    return (
        body, [own_left, own_right, got_left, got_right], [(shape, dtype) for dtype in (bf16, f32) for shape in shapes],
        vmem,
    )


def merge_job(lefts, rights, rows, cols, left, bit):
    def body(ins, outs):
        for flip, out in ((1, outs[0]), (0, outs[1])):
            half = half_of(bit, flip, rows)
            out[:, :left] = (ins[0][half, :].astype(f32) + ins[1][half, :].astype(f32)).astype(out.dtype)
            out[:, left:] = (ins[2][half, :].astype(f32) + ins[3][half, :].astype(f32)).astype(out.dtype)

    return body, [*lefts, *rights], [((rows, cols), bf16), ((rows, cols), f32)], vmem


def join_job(mine, other, bit):
    rows, cols = mine.shape

    def body(ins, outs):
        for flip in (0, 1):
            outs[0][half_of(bit, flip, rows), :] = ins[flip][...]

    return body, [mine, other], [((2 * rows, cols), bf16)], vmem


def turn_job(mine, other, bit):
    rows, cols = mine.shape

    def body(ins, outs):
        for flip in (0, 1):
            outs[0][:, half_of(bit, flip, rows)] = ins[flip][...].astype(f32).T

    return body, [mine, other], [((cols, 2 * rows), f32)], hbm


def spread_body(plans, w_ref, gain_ref, *refs):
    ins, outs = refs[: 2 * len(plans)], refs[2 * len(plans) :]
    for c, plan in enumerate(plans):
        mine_ref, other_ref = ins[2 * c], ins[2 * c + 1]
        rows = mine_ref.shape[0]
        for flip, ref in ((0, mine_ref), (1, other_ref)):
            for begin, length, out, to in plan:
                outs[out][half_of(1, flip, rows), to : to + length] = ref[:, begin : begin + length].astype(f32)
    share = jnp.sum(outs[0][...] * w_ref[...].astype(f32), axis=1, keepdims=True)
    share = jnp.broadcast_to(share, (share.shape[0], PAIR)).T[0:1]
    outs[-1][...] = (share / gain_ref[...].astype(f32).reshape(1, -1)).reshape(-1)


def spread_job(weight, gain, sums, plans, shapes):
    arrays = [array for pair in sums for array in pair]
    outs = [(shape, f32) for shape in (*shapes, gain.shape)]
    return lambda ins, outs: spread_body(plans, *ins, *outs), [weight, gain, *arrays], outs, hbm


def after(value, *deps):
    return lax.optimization_barrier((value, *deps))[0] if deps else value


class Moves:
    def __init__(self, narrow, wide):
        self.narrow, self.wide = narrow, wide
        self.n = lax.axis_index("narrow")
        self.w = lax.axis_index("wide")
        self.starts = [self.n, self.w % 2, (self.w // 2) % 2]

    def swap(self, value, axis, bit):
        size = self.narrow if axis == "narrow" else self.wide
        return lax.ppermute(value, axis, [(i, i ^ bit) for i in range(size)])

    def place(self, start):
        self.starts.append(start)
        return len(self.starts) - 1

    def reduce(self, send, keep, left=0):
        rows, cols = send.shape[1:]
        core = self.swap(send, "narrow", 1)
        deps = yield (send,)
        core = after(core, *deps)
        if left:
            to_left, to_right, mine_left, mine_right = yield fork_job(keep, core, rows, cols, left)
            got_left, got_right = self.swap(to_left, "narrow", 2), self.swap(to_right, "wide", 1)
            deps = yield to_left, to_right
            to_left, to_right, mine_left, mine_right = yield cross_job(
                mine_left, mine_right, after(got_left, *deps), after(got_right, *deps), rows, cols, left
            )
            got_left, got_right = self.swap(to_left, "wide", 1), self.swap(to_right, "narrow", 2)
            deps = yield to_left, to_right
            rows //= 4
            total, mine = yield merge_job(
                (mine_left, after(got_left, *deps)), (mine_right, after(got_right, *deps)), rows, cols, left, 2
            )
        else:
            total, mine = yield part_job(keep, core, rows, cols)
            got = self.swap(total, "narrow", 2)
            deps = yield (total,)
            total, mine = yield halve_job([(mine, None), (after(got, *deps), None)], rows // 2, cols, 1)
            got = self.swap(total, "wide", 1)
            deps = yield (total,)
            rows //= 4
            total, mine = yield halve_job([(mine, None), (after(got, *deps), None)], rows, cols, 2)
        got = self.swap(total, "wide", 2)
        deps = yield (total,)
        terms = [(mine, None), (after(got, *deps), None)]
        bit = 4
        while bit < self.wide:
            if bit == 4:
                (total,) = yield add_job(terms, rows, cols)
            else:
                total = whole_call("add_terms", [add_job(terms, rows, cols)])[0][0]
            got = self.swap(total, "wide", bit)
            deps = (yield (total,)) if bit == 4 else ()
            terms = [(total, None), (after(got, *deps), None)]
            bit *= 2
        (total,) = yield add_job(terms, rows, cols)
        got = self.swap(total, "wide", 2)
        deps = yield (total,)
        (total,) = yield join_job(total, after(got, *deps), 2)
        got = self.swap(total, "wide", 1)
        deps = yield (total,)
        yield total, after(got, *deps)


def begin(chain):
    return next(chain)


def close(chain, *deps):
    return chain.send(deps)


def advance(chains, *deps):
    jobs = [chain.send(deps) for chain in chains]
    results = whole_call("gradient_sums", jobs)
    return [array for chain, result in zip(chains, results) for array in chain.send(result)]


def shards(narrow, wide, layer_input, cotangent, block_size, gain_attn, w_qkv, w_out, gain_mlp, w_up, b_up, w_down, b_down):
    moves = Moves(narrow, wide)
    x, d_y = layer_input[0], cotangent[0]
    rows, width = x.shape
    seq = rows // 2
    pairs = width // PAIR
    ff = w_up.shape[1]
    n, bit = moves.n, moves.w % 2

    size = w_qkv.shape[0] // 3
    at_qkv = [
        moves.place((n ^ j) * w_qkv.shape[0] + extra)
        for j, extra in (
            (0, 0), (1, 0), (2, bit * size), (2, 2 * size), (2, (1 - bit) * size),
            (3, bit * size), (3, 2 * size), (3, (1 - bit) * size),
        )
    ]
    at_row = [moves.place((n ^ j) * w_out.shape[0]) for j in range(4)]

    at_down = [moves.place((n ^ j) * w_down.shape[0]) for j in range(4)]
    size_up = w_up.shape[0] // 3
    at_up = [
        moves.place((n ^ j) * w_up.shape[0] + extra)
        for j, extra in (
            (0, 0), (1, 0), (2, bit * size_up), (2, 2 * size_up), (2, (1 - bit) * size_up),
            (3, bit * size_up), (3, 2 * size_up), (3, (1 - bit) * size_up),
        )
    ]
    index = jnp.stack(moves.starts).astype(jnp.int32)

    def ready(*deps):
        return after(index, *deps)

    freq = 10000.0 ** (-jnp.arange(HEAD // 2).astype(f32) / (HEAD // 2))
    angles = jnp.arange(seq).astype(f32)[:, None] * freq[None, :]
    cosine, sine = jnp.cos(angles), jnp.sin(angles)
    cosine = jnp.tile(cosine, (1, 4))
    sine = jnp.concatenate([-sine, sine, -sine, sine], axis=1)

    first = lax.dynamic_slice_in_dim(w_qkv, bit * size, size, 0)
    got_first = moves.swap(first, "narrow", 2)
    second, small = vector_call(ready(first), w_qkv, gain_attn, gain_mlp, b_down, b_up)
    got_second = moves.swap(second, "narrow", 2)
    up_first, up_second = thirds_call(ready(second), w_up, (1, None))
    got_near, got_small, up_near, out_near = (
        moves.swap(after(v, first), "narrow", 1) for v in (w_qkv, small, w_up, w_out)
    )
    up_far, up_more = moves.swap(up_first, "narrow", 2), moves.swap(up_second, "narrow", 2)
    paced = pace_call(ready(up_first), cosine)
    got_first, got_near, got_small, up_near, out_near, _ = lax.optimization_barrier(
        (got_first, got_near, got_small, up_near, out_near, paced)
    )
    got_cross = moves.swap(got_first, "wide", 1)
    far_first = moves.swap(got_first, "narrow", 1)
    out_far = moves.swap(after(w_out, got_first), "narrow", 2)
    far_second, far_cross = (moves.swap(v, "narrow", 1) for v in (got_second, got_cross))
    count = w_qkv.shape[0]
    qkv_w = Weight(
        [
            (array, rows_of, place)
            for (array, rows_of), place in zip(
                (
                    (w_qkv, count), (got_near, count), (got_first, size), (got_second, size), (got_cross, size),
                    (far_first, size), (far_second, size), (far_cross, size),
                ),
                at_qkv,
            )
        ]
    )
    smalls = [small, got_small, got_second, far_second]

    block = jnp.arange(TILE, dtype=jnp.int32) // block_size[0]
    row_block, col_block = block[:, None], block[None, :]
    same, less, upto, less_t, upto_t = (
        jnp.where(ok, 0.0, -1e30).astype(f32)
        for ok in (
            row_block == col_block, col_block < row_block, col_block <= row_block,
            row_block < col_block, row_block <= col_block,
        )
    )
    dyt = d_y.T

    qkv, a1t, vec, qkv_full = qkv_call(index, x, qkv_w, smalls, ff, cosine, sine)
    up_far = after(up_far, vec)
    up_cross = moves.swap(up_far, "wide", 1)
    down_far = moves.swap(after(w_down, up_far), "narrow", 2)
    o, ot, lse = att_call(ready(up_far), qkv, (same, less_t, upto_t))
    up_pieces = [after(v, lse) for v in (up_far, up_more, up_cross)]
    up_last = [moves.swap(v, "narrow", 1) for v in up_pieces]
    out_far = after(out_far, lse)
    out_last = moves.swap(out_far, "narrow", 1)
    out_w = Weight([(a, w_out.shape[0], p) for a, p in zip((w_out, out_near, out_far, out_last), at_row)])
    up_w = Weight(
        [
            (a, r, p)
            for a, r, p in zip(
                (w_up, up_near, *up_pieces, *up_last), (w_up.shape[0],) * 2 + (size_up,) * 6, at_up
            )
        ]
    )
    x1, a2t, h, g, out_full, up_full = up_call(ready(lse), x, o, vec, out_w, up_w)
    send = grad_down_call(index, dyt, h, (1, 2), narrow)
    keep = grad_down_call(ready(send), dyt, h, (0, 2), narrow)
    down_far = after(down_far, keep)
    down_last = moves.swap(down_far, "narrow", 1)
    down_near = moves.swap(after(w_down, send), "narrow", 1)
    down_w = Weight([(a, w_down.shape[0], p) for a, p in zip((w_down, down_near, down_far, down_last), at_down)])
    chain_a = moves.reduce(send, keep, width // 2)
    begin(chain_a)
    d_u, dx1, dx1r, d_o, biases, down_full = down_call(
        ready(keep, *advance([chain_a], keep)), d_y, x1, g, vec, up_full, out_full, down_w
    )
    send, keep = grad_up_call(ready(*advance([chain_a], dx1r)), a2t, ot, d_u, dx1r, biases, narrow)
    chain_b = moves.reduce(send, keep, 2048)
    begin(chain_b)

    def back(start, count, *deps):
        return att_back_call(
            ready(*deps), qkv, d_o, o, lse, (same, less_t, upto_t), cosine, sine, start, count
        )

    paced = pace_call(ready(send), same)
    g0 = back(0, 2, keep, *advance([chain_a, chain_b], keep, paced))
    g1 = back(2, 2, g0[0], *advance([chain_a], g0[0]))
    g2 = back(4, 2, g1[0], *advance([chain_b], g1[0]))
    groups = [g0, g1, g2]
    rights = [array for group in groups for array in group]
    send, keep = grad_qkv_call(ready(*advance([chain_b], g2[0])), a1t, rights, narrow)
    chain_c = moves.reduce(send, keep, 1152)
    begin(chain_c)
    paced = pace_call(ready(send), same)
    sent = advance([chain_a], keep)
    sent = advance([chain_b, chain_c], keep, paced, *sent)
    output = output_call(ready(keep, *sent), x1, h, vec, down_full)
    sent = advance([chain_a, chain_c], output)
    d_input = input_call(ready(output, *sent), x, dx1, vec, groups, qkv_full)
    sent = advance([chain_b, chain_c], d_input)
    sent = advance([chain_b, chain_c], *sent)
    sum_a = close(chain_a, *sent)
    (grad_down,) = whole_call("last_down", [turn_job(*sum_a, 1)])[0]
    sent = advance([chain_c], *sent, grad_down)
    sent = advance([chain_c], *sent)
    sum_b = close(chain_b, *sent)
    sum_c = close(chain_c)

    own = width // narrow
    grad_up, grad_out, biases, grad_gain_mlp = whole_call(
        "last_up",
        [
            spread_job(
                w_up, gain_mlp, [sum_b], [[(0, ff, 0, 0), (ff, width, 1, 0), (ff + width, TILE, 2, 0)]],
                [(own, ff), (own, width), (own, TILE)],
            )
        ],
    )[0]
    biases = biases[:8].reshape(-1)
    plan, begin_at, to = [], 0, 0
    for group in groups:
        cols = group[0].shape[1]
        for part in range(3):
            plan.append((begin_at, cols, 0, part * width + to))
            begin_at += cols
        to += cols
    grad_qkv, grad_gain_attn = whole_call("last_qkv", [spread_job(w_qkv, gain_attn, [sum_c], [plan], [(own, 3 * width)])])[0]
    return (
        output[None],
        d_input[None],
        grad_gain_attn,
        grad_qkv,
        grad_out,
        grad_gain_mlp,
        grad_up,
        biases[:width],
        grad_down,
        biases[width : width + own],
    )


def solution(mesh):
    return jax.shard_map(
        functools.partial(shards, mesh.shape["narrow"], mesh.shape["wide"]),
        mesh=mesh,
        in_specs=(
            P(("wide", "narrow"), None, None),
            P(("wide", "narrow"), None, None),
            P(("wide", "narrow")),
            P("narrow"),
            P("narrow", None),
            P("narrow", None),
            P("narrow"),
            P("narrow", None),
            P("narrow"),
            P("narrow", None),
            P("narrow"),
        ),
        out_specs=(
            P(("wide", "narrow"), None, None),
            P(("wide", "narrow"), None, None),
            P("narrow"),
            P("narrow", None),
            P("narrow", None),
            P("narrow"),
            P("narrow", None),
            P("narrow"),
            P("narrow", None),
            P("narrow"),
        ),
        check_vma=False,
    )
```

```python
import functools
import math

import jax
import jax.numpy as jnp
from jax import lax
from jax.experimental import pallas as pl
from jax.experimental.pallas import tpu as pltpu
from jax.sharding import PartitionSpec as P

HEAD = 64
PAIR = 2 * HEAD
TILE = 128
ORDER = (1, 3, 0, 2)
SPAN = 256
LOG2E = 1.4426950408889634
LN2 = 0.6931471805599453
f32 = jnp.float32
bf16 = jnp.bfloat16
MIB = 1 << 20


def nn(left, right):
    return jnp.dot(left, right, preferred_element_type=f32)


def nt(left, right):
    return lax.dot_general(left, right, (((1,), (1,)), ((), ())), preferred_element_type=f32)


def norm_rows(values):
    centre = values - jnp.mean(values, axis=-1, keepdims=True)
    inverse = lax.rsqrt(jnp.mean(centre * centre, axis=-1, keepdims=True) + 1e-05)
    return centre * inverse, inverse


def norm_back(d_norm, scaled, inverse, gain):
    d_scaled = d_norm * gain
    return inverse * (
        d_scaled
        - jnp.mean(d_scaled, axis=-1, keepdims=True)
        - scaled * jnp.mean(d_scaled * scaled, axis=-1, keepdims=True)
    )


def swap_halves(tile):
    lane = lax.broadcasted_iota(jnp.int32, (1, PAIR), 1) % HEAD
    return jnp.where(
        lane < HEAD // 2,
        pltpu.roll(tile, PAIR - HEAD // 2, 1),
        pltpu.roll(tile, HEAD // 2, 1),
    )


class Weight:
    def __init__(self, pieces):
        self.arrays = [array for array, _, _ in pieces]
        self.plan = [(rows, place) for _, rows, place in pieces]
        self.rows = sum(rows for rows, _ in self.plan)
        self.cols = self.arrays[0].shape[1]

    def specs(self, near=True):
        space = pltpu.VMEM if near else pltpu.HBM
        return [pl.BlockSpec(memory_space=pltpu.HBM)] + [pl.BlockSpec(memory_space=space)] * (len(self.plan) - 1)

    def near(self, at):
        return list(range(at + 1, at + len(self.plan)))

    def whole(self):
        return pltpu.VMEM((self.rows, self.cols), bf16)

    def sems(self):
        return [pltpu.SemaphoreType.DMA((len(self.plan),))]

    def scratch(self):
        return [self.whole(), *self.sems()]


def fetches(at_ref, plan, parts, whole, sems):
    copies = []
    for i, ((rows, place), part) in enumerate(zip(plan, parts)):
        start = pl.multiple_of(at_ref[place], math.gcd(rows, 256))
        copies.append(pltpu.make_async_copy(part.at[pl.ds(0, rows)], whole.at[pl.ds(start, rows)], sems.at[i]))
    return copies


def fetch(at_ref, *weights):
    @pl.when(pl.program_id(0) == 0)
    def _():
        for weight in weights:
            for copy in fetches(at_ref, *weight):
                copy.start()


def arrive(at_ref, weight):
    @pl.when(pl.program_id(0) == 0)
    def _():
        for copy in fetches(at_ref, *weight):
            copy.wait()


def step_rows(step):
    return pl.ds(pl.multiple_of(pl.program_id(0) * step, step), step)


def take(refs, *groups):
    out, at = [], 0
    for group in groups:
        out.append(refs[at : at + len(group)])
        at += len(group)
    return out + [refs[at:]]


def fixed(shape):
    return pl.BlockSpec(shape, lambda *_: (0,) * len(shape), pipeline_mode=pl.Buffered(1))


def call(body, name, grid, in_specs, out_specs, out_shape, scratch, limit, cost, near=(), aliases=None, moved=1 << 20):
    fun = pl.pallas_call(
        body,
        name=name,
        out_shape=out_shape,
        input_output_aliases=aliases or {},
        grid_spec=pltpu.PrefetchScalarGridSpec(
            num_scalar_prefetch=1,
            grid=grid,
            in_specs=in_specs,
            out_specs=out_specs,
            scratch_shapes=scratch,
        ),
        compiler_params=pltpu.CompilerParams(
            dimension_semantics=("arbitrary",) * len(grid), vmem_limit_bytes=limit * MIB
        ),
        cost_estimate=pl.CostEstimate(
            flops=int(cost * 1e12), bytes_accessed=moved, transcendentals=0
        ),
    )

    def run(index, *args):
        args = [
            pltpu.with_memory_space_constraint(arg, pltpu.VMEM if i in near else pltpu.HBM)
            for i, arg in enumerate(args)
        ]
        return fun(index, *args)

    return run


def hbm(shape, dtype):
    return pltpu.HBM(shape, dtype)


def vmem(shape, dtype):
    return pltpu.VMEM(shape, dtype)


def sds(shape, dtype):
    return jax.ShapeDtypeStruct(shape, dtype)


def small_rows(cols, gain1_ref, gain2_ref, down_ref, up_ref):
    def lanes(*refs):
        values = [ref[...].astype(f32).reshape(1, -1) for ref in refs]
        return jnp.concatenate(
            [v for v in values for _ in range(cols // (len(refs) * v.shape[1]))], axis=1
        )

    row = lax.broadcasted_iota(jnp.int32, (8, cols), 0)
    return jnp.where(row == 0, lanes(gain1_ref, gain2_ref, down_ref), lanes(up_ref)).astype(bf16)


def vector_body(idx_ref, w_ref, gain1_ref, gain2_ref, down_ref, up_ref, out_ref, small_ref):
    size = w_ref.shape[0]
    small = small_rows(w_ref.shape[1], gain1_ref, gain2_ref, down_ref, up_ref)
    out_ref[:size, :] = w_ref[...]
    out_ref[size:, :] = small
    small_ref[...] = small


def vector_call(index, weight, *vectors):
    size, cols = weight.shape[0] // 3, weight.shape[1]
    shapes = [(size + 8, cols), (8, cols)]
    return call(
        vector_body,
        "vector_message",
        (1,),
        [pl.BlockSpec((size, cols), lambda i, s: (2, 0))] + [fixed(v.shape) for v in vectors],
        [fixed(shape) for shape in shapes],
        [vmem(shape, bf16) for shape in shapes],
        [],
        6,
        1.5,
    )(index, weight, *vectors)


def thirds_body(idx_ref, *refs):
    count = len(refs) // 2
    for ref, out_ref in zip(refs[:count], refs[count:]):
        out_ref[...] = ref[...]


def thirds_call(index, weight, places):
    size, cols = weight.shape[0] // 3, weight.shape[1]
    return call(
        thirds_body,
        "next_message",
        (1,),
        [pl.BlockSpec((size, cols), lambda i, s, p=p: (2 if p is None else s[p], 0)) for p in places],
        [fixed((size, cols))] * len(places),
        [vmem((size, cols), bf16)] * len(places),
        [],
        6,
        1.5,
    )(index, *[weight] * len(places))


def qkv_body(plan, n, idx_ref, x_ref, cos_ref, sin_ref, *refs):
    smalls, parts, refs = take(refs, range(n), plan)
    qkv_ref, a1t_ref, vec_ref, whole, sems = refs
    weight = (plan, parts, whole, sems)
    fetch(idx_ref, weight)
    width = x_ref.shape[1]
    here = step_rows(x_ref.shape[0])

    @pl.when(pl.program_id(0) == 0)
    def _():
        lane = lax.broadcasted_iota(jnp.int32, (1, width), 1) // (width // n)
        values = [ref[...].astype(f32) for ref in smalls]
        vec_ref[...] = jnp.zeros_like(vec_ref)
        for i in range(3):
            vec_ref[i : i + 1, :width] = sum(
                jnp.where(lane == (idx_ref[0] ^ j), v[0:1, i * width : (i + 1) * width], 0.0)
                for j, v in enumerate(values)
            )
        size = vec_ref.shape[1] // n
        for c in range(n):
            vec_ref[3:4, c * size : (c + 1) * size] = sum(
                jnp.where((idx_ref[0] ^ j) == c, v[1:2, :size], 0.0) for j, v in enumerate(values)
            )

    scaled, _ = norm_rows(x_ref[...].astype(f32))
    a1 = (scaled * vec_ref[0:1, :width]).astype(bf16)
    a1t_ref[...] = a1.T
    cosine, sine = cos_ref[...], sin_ref[...]
    arrive(idx_ref, weight)
    for part in range(3):
        y = nn(a1, whole[:, part * width : (part + 1) * width])
        if part == 2:
            qkv_ref[here, part * width :] = y.astype(bf16)
            continue
        for t in range(width // PAIR):
            tile = y[:, t * PAIR : (t + 1) * PAIR]
            tile = tile * cosine + swap_halves(tile) * sine
            if part == 0:
                tile = tile * (LOG2E / 8.0)
            at = part * width + t * PAIR
            qkv_ref[here, at : at + PAIR] = tile.astype(bf16)


def qkv_call(index, x, weight, smalls, ff, cosine, sine):
    rows, width = x.shape
    wide = weight.cols
    step = 256
    per = cosine.shape[0] // step

    def vector(array):
        return pl.BlockSpec((8, wide), lambda i, s: (array.shape[0] // 8 - 1, 0))

    return call(
        functools.partial(qkv_body, weight.plan, len(smalls)),
        "norm_qkv",
        (rows // step,),
        [
            pl.BlockSpec((step, width), lambda i, s: (i, 0)),
            pl.BlockSpec((step, PAIR), lambda i, s: (i % per, 0)),
            pl.BlockSpec((step, PAIR), lambda i, s: (i % per, 0)),
        ]
        + [vector(array) for array in smalls]
        + weight.specs(),
        [
            fixed((rows, wide)),
            pl.BlockSpec((width, step), lambda i, s: (0, i)),
            pl.BlockSpec((8, ff), lambda i, s: (0, 0)),
            fixed((weight.rows, wide)),
        ],
        [vmem((rows, wide), bf16), hbm((width, rows), bf16), hbm((8, ff), f32), hbm((weight.rows, wide), bf16)],
        weight.sems(),
        16,
        7,
        near=(*range(3, 3 + len(smalls)), *weight.near(3 + len(smalls))),
    )(index, x, cosine, sine, *smalls, *weight.arrays)


def head_masks():
    lane = lax.broadcasted_iota(jnp.int32, (1, PAIR), 1)
    return lane < HEAD, lane >= HEAD


def widen(tile, allowed):
    count = SPAN // TILE
    never = jnp.full(tile.shape, -1e30, f32)
    before = jnp.zeros(tile.shape, f32) if allowed else never
    return jnp.concatenate(
        [
            jnp.concatenate([tile if a == b else (before if a < b else never) for b in range(count)], axis=1)
            for a in range(count)
        ],
        axis=0,
    )


def att_body(seq, idx_ref, qkv_ref, same_ref, less_ref, upto_ref, o_ref, ot_ref, lse_ref):
    def columns(part):
        start = part * (qkv_ref.shape[1] // 3) + pl.program_id(0) * PAIR
        return pl.ds(pl.multiple_of(start, PAIR), PAIR)

    queries, k_all = columns(0), qkv_ref[:, columns(1)]
    keys = [jnp.where(m, k_all, jnp.zeros_like(k_all)) for m in head_masks()]
    v_t = qkv_ref[:, columns(2)].T
    ones = jnp.ones((16, 2 * seq), bf16)
    vals = [jnp.concatenate([v_t[h * HEAD : (h + 1) * HEAD], ones], axis=0) for h in range(2)]
    same, less, upto = widen(same_ref[...], False), widen(less_ref[...], True), widen(upto_ref[...], True)

    def scores(lo, clean, h):
        hi = lo + SPAN
        row = lo + seq if clean else lo
        query = qkv_ref[row : row + SPAN, queries]
        pieces = [nt(keys[h][seq + lo : seq + hi], query) + (upto if clean else less)]
        if lo > 0:
            pieces.append(nt(keys[h][seq : seq + lo], query))
        if not clean:
            pieces.append(nt(keys[h][lo:hi], query) + same)
        return pieces

    def soften(pieces):
        top = functools.reduce(jnp.maximum, [jnp.max(p, axis=0, keepdims=True) for p in pieces])
        return top, [jnp.exp2(p - top).astype(bf16) for p in pieces]

    def mix(lo, clean, h, weights):
        hi = lo + SPAN
        out = nn(vals[h][:, seq + lo : seq + hi], weights[0])
        if lo > 0:
            out = out + nn(vals[h][:, seq : seq + lo], weights[1])
        if not clean:
            out = out + nn(vals[h][:, lo:hi], weights[-1])
        return out

    def finish(lo, clean, softened):
        row = lo + seq if clean else lo
        outs = [mix(lo, clean, h, softened[h][1]) for h in range(2)]
        out = jnp.concatenate([o[:HEAD] / o[HEAD : HEAD + 1] for o in outs], axis=0)
        ot_ref[:, row : row + SPAN] = out.astype(bf16)
        o_ref[row : row + SPAN, :] = out.T.astype(bf16)
        for h in range(2):
            lse_ref[0, h : h + 1, row : row + SPAN] = softened[h][0] + jnp.log2(outs[h][HEAD : HEAD + 1])

    work = [(lo, clean) for lo in range(0, seq, SPAN) for clean in (False, True)]
    ahead = [scores(*work[0], h) for h in range(2)]
    behind = None
    for i, item in enumerate(work):
        now = ahead
        if i + 1 < len(work):
            ahead = [scores(*work[i + 1], h) for h in range(2)]
        softened = [soften(pieces) for pieces in now]
        if behind is not None:
            finish(*behind)
        behind = (*item, softened)
    finish(*behind)


def att_call(index, qkv, masks):
    rows = qkv.shape[0]
    width = qkv.shape[1] // 3
    pairs = width // PAIR
    return call(
        functools.partial(att_body, rows // 2),
        "attention",
        (pairs,),
        [fixed(qkv.shape)] + [fixed((TILE, TILE))] * 3,
        [
            pl.BlockSpec((rows, PAIR), lambda p, s: (0, p)),
            pl.BlockSpec((PAIR, rows), lambda p, s: (p, 0)),
            pl.BlockSpec((1, 2, rows), lambda p, s: (p, 0, 0)),
        ],
        [hbm((rows, width), bf16), hbm((width, rows), bf16), hbm((pairs, 2, rows), f32)],
        [],
        16,
        12.0,
        near=(0,),
    )(index, qkv, *masks)


def att_back_body(
    seq, idx_ref, q_ref, k_ref, v_ref, do_ref, o_ref, lse_ref, same_ref, less_ref, upto_ref,
    cos_ref, sin_ref, dq_ref, dk_ref, dv_ref, dqt_ref,
):
    first, second = head_masks()
    q_all, k_all, v_all, do_all = q_ref[...], k_ref[...], v_ref[...], do_ref[...]

    def split(array):
        return [jnp.where(m, array, jnp.zeros_like(array)) for m in (first, second)]

    queries, keys, vals, dos = split(q_all), split(k_all), split(v_all), split(do_all)
    keys_t = k_all.T
    product = do_all.astype(f32) * o_ref[...].astype(f32)
    high = product.astype(bf16)
    rest = (product - high.astype(f32)).astype(bf16)
    picked = lax.broadcasted_iota(jnp.int32, (8, PAIR), 0)
    picked = jnp.where(picked == lax.broadcasted_iota(jnp.int32, (8, PAIR), 1) // HEAD, 1.0, 0.0).astype(bf16)
    delta = nt(picked, high) + nt(picked, rest)
    same, less, upto = widen(same_ref[...], False), widen(less_ref[...], True), widen(upto_ref[...], True)
    dqt_ref[...] = jnp.zeros_like(dqt_ref)

    def products(unit):
        return [
            (nt(keys[h][k : k + SPAN], q_all[q:end]), nt(vals[h][k : k + SPAN], do_all[q:end]))
            for h, k, q, end, _ in unit[0]
        ]

    def soften(unit, values):
        out = []
        for (h, _, q, end, mask), (scores, d_probs) in zip(unit[0], values):
            scores = scores - lse_ref[0, h : h + 1, q:end]
            probs = jnp.exp2(scores[:, :SPAN] + mask)
            if end - q > SPAN:
                probs = jnp.concatenate([probs, jnp.exp2(scores[:, SPAN:])], axis=1)
            d_scores = probs * (d_probs - delta[h : h + 1, q:end])
            out.append((probs.astype(bf16), d_scores.astype(bf16)))
        return out

    def rotate_back(tile, row):
        at = row % seq
        cosine, sine = cos_ref[at : at + SPAN, :], sin_ref[at : at + SPAN, :]
        return tile * cosine - swap_halves(tile) * sine

    def gather(unit, values, sums):
        items, last = unit
        d_vals, d_keys = sums
        for (h, k, q, end, _), (probs, d_scores) in zip(items, values):
            d_vals = d_vals + nn(probs, dos[h][q:end])
            d_keys = d_keys + nn(d_scores, queries[h][q:end])
            at = slice(h * HEAD, (h + 1) * HEAD)
            dqt_ref[at, q:end] += nn(keys_t[at, k : k + SPAN], d_scores)
        if not last:
            return d_vals, d_keys
        k = items[0][1]
        dv_ref[k : k + SPAN, :] = d_vals.astype(bf16)
        dk_ref[k : k + SPAN, :] = rotate_back(d_keys * LN2, k).astype(bf16)
        return 0.0, 0.0

    units = []
    for lo in range(0, seq, SPAN):
        units.append(([(h, lo, lo, lo + SPAN, same) for h in range(2)], True))
        for base, mask in ((0, less), (seq, upto)):
            units.append(([(h, seq + lo, base + lo, base + seq, mask) for h in range(2)], base > 0))
    ahead, behind, sums = products(units[0]), None, (0.0, 0.0)
    for i, unit in enumerate(units):
        now = ahead
        if i + 1 < len(units):
            ahead = products(units[i + 1])
        values = soften(unit, now)
        if behind is not None:
            sums = gather(*behind, sums)
        behind = (unit, values)
    gather(*behind, sums)
    for r in range(0, 2 * seq, SPAN):
        tile = dqt_ref[:, r : r + SPAN].T * 0.125
        dq_ref[r : r + SPAN, :] = rotate_back(tile, r).astype(bf16)


def att_back_call(index, qkv, d_o, o, lse, masks, cosine, sine, start, count):
    rows = qkv.shape[0]
    width = qkv.shape[1] // 3
    pairs = width // PAIR
    seq = rows // 2

    def column(part):
        return pl.BlockSpec((rows, PAIR), lambda p, s: (0, part * pairs + start + p))

    out = pl.BlockSpec((rows, PAIR), lambda p, s: (0, p))
    return call(
        functools.partial(att_back_body, seq),
        "attention_back",
        (count,),
        [column(0), column(1), column(2), column(0), column(0)]
        + [pl.BlockSpec((1, 2, rows), lambda p, s: (start + p, 0, 0))]
        + [fixed((TILE, TILE))] * 3
        + [fixed((seq, PAIR))] * 2,
        [out] * 3,
        [vmem((rows, count * PAIR), bf16)] * 3,
        [pltpu.VMEM((PAIR, rows), f32)],
        16,
        3.6 * count,
    )(index, qkv, qkv, qkv, d_o, o, lse, *masks, cosine, sine)


def up_body(out_at, up_at, idx_ref, x_ref, o_ref, vec_ref, *refs):
    outs, ups, refs = take(refs, out_at, up_at)
    x1_ref, a2t_ref, h_ref, g_ref, w_out, w_up, out_sems, up_sems = refs
    out_weight, up_weight = (out_at, outs, w_out, out_sems), (up_at, ups, w_up, up_sems)
    fetch(idx_ref, out_weight, up_weight)
    arrive(idx_ref, out_weight)
    width = x_ref.shape[1]
    here = step_rows(x_ref.shape[0])
    x1 = x_ref[...].astype(f32) + nn(o_ref[...], w_out[...])
    x1_ref[...] = x1
    scaled, _ = norm_rows(x1)
    a2 = (scaled * vec_ref[1:2, :width]).astype(bf16)
    a2t_ref[:, here] = a2.T
    arrive(idx_ref, up_weight)
    c0 = math.sqrt(2.0 / math.pi)
    c1 = c0 * 0.044715
    chunk = 512
    for at in range(0, w_up.shape[1], chunk):
        u = nn(a2, w_up[:, at : at + chunk]) + vec_ref[3:4, at : at + chunk]
        square = u * u
        t = jnp.tanh(u * (c1 * square + c0))
        half = 0.5 * t + 0.5
        h_ref[here, at : at + chunk] = (u * half).astype(bf16)
        slope = u * (1.5 * c1 * square + 0.5 * c0)
        g_ref[here, at : at + chunk] = (half + slope * (1.0 - t * t)).astype(bf16)


def up_call(index, x, o, vec, w_out, w_up):
    rows, width = x.shape
    ff = w_up.cols
    step = 256

    def row(cols):
        return pl.BlockSpec((step, cols), lambda i, s: (i, 0))

    outs = [
        hbm((rows, width), f32), vmem((width, rows), bf16), vmem((rows, ff), bf16), vmem((rows, ff), bf16),
        w_out.whole(), w_up.whole(),
    ]
    return call(
        functools.partial(up_body, w_out.plan, w_up.plan),
        "feed_up",
        (rows // step,),
        [row(width), row(width), fixed(vec.shape)] + w_out.specs() + w_up.specs(),
        [row(width)] + [fixed(out.shape) for out in outs[1:]],
        outs,
        w_out.sems() + w_up.sems(),
        12,
        18,
        near=w_out.near(3) + w_up.near(3 + len(w_out.plan)),
    )(index, x, o, vec, *w_out.arrays, *w_up.arrays)


def down_body(down_at, idx_ref, dy_ref, x1_ref, g_ref, vec_ref, w_up, w_out, *refs):
    downs, refs = take(refs, down_at)
    du_ref, dx1_ref, do_ref, bias_ref, w_down, down_sems = refs
    weight = (down_at, downs, w_down, down_sems)
    fetch(idx_ref, weight)

    @pl.when(pl.program_id(0) == 0)
    def _():
        bias_ref[...] = jnp.zeros_like(bias_ref)

    width = dy_ref.shape[1]
    here = step_rows(dy_ref.shape[0])
    low = dy_ref[...]
    d_y = low.astype(f32)
    bias_ref[1:2, :width] += jnp.sum(d_y, axis=0, keepdims=True)
    arrive(idx_ref, weight)
    chunk = 512
    d_a2 = 0.0
    for at in range(0, w_up.shape[1], chunk):
        d_u = nt(low, w_down[at : at + chunk, :]) * g_ref[here, at : at + chunk].astype(f32)
        bias_ref[0:1, at : at + chunk] += jnp.sum(d_u, axis=0, keepdims=True)
        d_u = d_u.astype(bf16)
        du_ref[here, at : at + chunk] = d_u
        d_a2 = d_a2 + nt(d_u, w_up[:, at : at + chunk])
    scaled, inverse = norm_rows(x1_ref[...])
    d_x1 = d_y + norm_back(d_a2, scaled, inverse, vec_ref[1:2, :width])
    dx1_ref[...] = d_x1
    d_x1 = d_x1.astype(bf16)
    du_ref[here, w_up.shape[1] :] = d_x1
    do_ref[...] = nt(d_x1, w_out[...]).astype(bf16)


def down_call(index, d_y, x1, g, vec, w_up, w_out, w_down):
    rows, width = d_y.shape
    ff = w_up.shape[1]
    step = 256

    def row(cols):
        return pl.BlockSpec((step, cols), lambda i, s: (i, 0))

    return call(
        functools.partial(down_body, w_down.plan),
        "feed_back",
        (rows // step,),
        [row(width), row(width)] + [fixed(array.shape) for array in (g, vec, w_up, w_out)] + w_down.specs(),
        [fixed((rows, ff + width)), row(width), row(width), fixed((2, ff)),
         fixed((ff, width))],
        [
            vmem((rows, ff + width), bf16), hbm((rows, width), f32), hbm((rows, width), bf16),
            vmem((2, ff), f32), w_down.whole(),
        ],
        w_down.sems(),
        14,
        20,
        near=(2, 4, 5, *w_down.near(6)),
    )(index, d_y, x1, g, vec, w_up, w_out, *w_down.arrays)


def grad_down_body(offsets, idx_ref, dyt_ref, h_ref, out_ref):
    base, step = offsets
    cols = out_ref.shape[2]
    shard = idx_ref[0] ^ (base + step * pl.program_id(0))
    columns = pl.ds(pl.multiple_of(shard * cols, cols), cols)
    out_ref[pl.program_id(0)] = nn(dyt_ref[...], h_ref[:, columns]).astype(bf16)


def grad_down_call(index, dyt, h, offsets, shards):
    width, rows = dyt.shape
    cols = h.shape[1] // shards
    return call(
        functools.partial(grad_down_body, offsets),
        "grad_down",
        (2,),
        [fixed(dyt.shape), fixed(h.shape)],
        fixed((2, width, cols)),
        vmem((2, width, cols), bf16),
        [],
        8,
        3,
        near=(0, 1),
    )(index, dyt, h)


def shard_rows(idx_ref, rows):
    return [pl.ds(pl.multiple_of((idx_ref[0] ^ j) * rows, math.gcd(rows, 256)), rows) for j in ORDER]


def grad_up_body(chunks, idx_ref, a_ref, o_ref, du_ref, bias_ref, send_ref, keep_ref, left_ref):
    rows = send_ref.shape[1]
    width = a_ref.shape[0]
    i = pl.program_id(0)
    columns = pl.ds(pl.multiple_of(i * width, width), width)
    for step, ref in ((0, a_ref), (chunks, o_ref)):

        @pl.when(i == step)
        def _(ref=ref):
            for k, at in enumerate(shard_rows(idx_ref, rows)):
                left_ref[k * rows : (k + 1) * rows, :] = ref[at, :]

    y = nn(left_ref[...], du_ref[:, columns]).astype(bf16)
    for k in range(4):
        (send_ref if k < 2 else keep_ref)[k % 2, :, columns] = y[k * rows : (k + 1) * rows]

    @pl.when(i == chunks)
    def _():
        at = (chunks + 1) * width
        lanes = send_ref.shape[2] - at
        shards = width // rows
        pad = jnp.zeros((1, 2 * lanes - rows), f32)
        for k, j in enumerate(ORDER):
            shard = idx_ref[0] ^ j
            out_ref = send_ref if k < 2 else keep_ref
            tiles = [
                bias_ref[0:1, pl.ds(pl.multiple_of(shard * width + t * lanes, lanes), lanes)]
                for t in range(width // lanes)
            ]
            own = sum(
                jnp.where(shard == t, bias_ref[1:2, t * rows : (t + 1) * rows], 0.0) for t in range(shards)
            )
            own = jnp.concatenate([own, pad], axis=1)
            tiles += [own[:, :lanes], own[:, lanes:]]
            block = jnp.concatenate(tiles + [jnp.zeros((16 - len(tiles), lanes), f32)], axis=0)
            out_ref[k % 2, :16, at:] = block.astype(bf16)
            out_ref[k % 2, 16:, at:] = jnp.zeros((rows - 16, lanes), bf16)


def grad_up_call(index, a2t, ot, d_u, biases, shards):
    width, rows = a2t.shape
    own = width // shards
    ff = d_u.shape[1] - width
    chunks = ff // width
    cols = ff + width + TILE
    return call(
        functools.partial(grad_up_body, chunks),
        "grad_up_out",
        (chunks + 1,),
        [fixed(array.shape) for array in (a2t, ot, d_u, biases)],
        [fixed((2, own, cols))] * 2,
        [vmem((2, own, cols), bf16)] * 2,
        [pltpu.VMEM((width, rows), bf16)],
        10,
        4.7,
        near=range(4),
    )(index, a2t, ot, d_u, biases)


def grad_qkv_body(idx_ref, a_ref, *refs):
    rights, send_ref, keep_ref = refs[:-2], refs[-2], refs[-1]
    rows = send_ref.shape[1]
    left = jnp.concatenate([a_ref[at, :] for at in shard_rows(idx_ref, rows)], axis=0)
    at = 0
    for right in rights:
        cols = right.shape[1]
        y = nn(left, right[...]).astype(bf16)
        for k in range(4):
            (send_ref if k < 2 else keep_ref)[k % 2, :, at : at + cols] = y[k * rows : (k + 1) * rows]
        at += cols


def grad_qkv_call(index, a1t, rights, shards):
    own = a1t.shape[0] // shards
    cols = sum(right.shape[1] for right in rights)
    return call(
        grad_qkv_body,
        "grad_qkv",
        (1,),
        [fixed(array.shape) for array in (a1t, *rights)],
        [fixed((2, own, cols))] * 2,
        [vmem((2, own, cols), bf16)] * 2,
        [],
        10,
        1.0 + cols / 1000.0,
        near=range(1 + len(rights)),
    )(index, a1t, *rights)


def input_body(groups, idx_ref, x_ref, dx1_ref, vec_ref, w_ref, *refs):
    grads, (dx_ref,) = refs[: 3 * groups], refs[3 * groups :]
    width = x_ref.shape[1]
    here = step_rows(x_ref.shape[0])
    scaled, inverse = norm_rows(x_ref[...].astype(f32))
    d_a1 = 0.0
    for part in range(3):
        at = part * width
        for g in range(groups):
            ref = grads[3 * g + part]
            cols = ref.shape[1]
            d_a1 = d_a1 + nt(ref[here, :], w_ref[:, at : at + cols])
            at += cols
    d_x = dx1_ref[...] + norm_back(d_a1, scaled, inverse, vec_ref[0:1, :width])
    dx_ref[...] = d_x.astype(bf16)


def input_call(index, x, dx1, vec, d_groups, weight):
    rows, width = x.shape
    step = 256

    def row(cols):
        return pl.BlockSpec((step, cols), lambda i, s: (i, 0))

    flat = [array for group in d_groups for array in group]
    return call(
        functools.partial(input_body, len(d_groups)),
        "grad_input",
        (rows // step,),
        [row(width), row(width)] + [fixed(array.shape) for array in (vec, weight, *flat)],
        row(width),
        hbm((rows, width), bf16),
        [],
        14,
        9,
        near=range(4, 4 + len(flat)),
    )(index, x, dx1, vec, weight, *flat)


def output_body(idx_ref, x1_ref, h_ref, vec_ref, w_ref, out_ref):
    y = x1_ref[...] + nn(h_ref[...], w_ref[...]) + vec_ref[2:3, : x1_ref.shape[1]]
    out_ref[...] = y.astype(bf16)


def output_call(index, x1, h, vec, weight):
    rows, width = x1.shape

    def row(cols):
        return pl.BlockSpec((256, cols), lambda i, s: (i, 0))

    return call(
        output_body,
        "layer_output",
        (rows // 256,),
        [row(width), row(h.shape[1]), fixed(vec.shape), fixed(weight.shape)],
        row(width),
        hbm((rows, width), bf16),
        [],
        14,
        8,
        near=(3,),
    )(index, x1, h, vec, weight)


def pace_body(idx_ref, tile_ref, out_ref):
    out_ref[...] = tile_ref[:8, :]


def pace_call(index, tile):
    return call(
        pace_body,
        "pace",
        (1,),
        [fixed(tile.shape)],
        fixed((8, tile.shape[1])),
        vmem((8, tile.shape[1]), f32),
        [],
        2,
        5,
        near=(0,),
    )(index, tile)


def whole_call(name, jobs):
    arrays = [array for _, ins, _, _ in jobs for array in ins]
    results = [place(shape, dtype) for _, _, outs, place in jobs for shape, dtype in outs]

    def run(*refs):
        ins, outs = refs[: len(arrays)], refs[len(arrays) :]
        at, to = 0, 0
        for body, job_ins, job_outs, _ in jobs:
            body(ins[at : at + len(job_ins)], outs[to : to + len(job_outs)])
            at, to = at + len(job_ins), to + len(job_outs)

    flat = pl.pallas_call(
        run,
        name=name,
        in_specs=[pl.BlockSpec(memory_space=pltpu.VMEM)] * len(arrays),
        out_specs=[pl.BlockSpec(memory_space=pltpu.VMEM)] * len(results),
        out_shape=results,
        compiler_params=pltpu.CompilerParams(vmem_limit_bytes=10 * MIB),
        cost_estimate=pl.CostEstimate(
            flops=0,
            bytes_accessed=sum(array.size * array.dtype.itemsize for array in arrays),
            transcendentals=0,
        ),
    )(*(pltpu.with_memory_space_constraint(array, pltpu.VMEM) for array in arrays))
    groups, at = [], 0
    for _, _, outs, _ in jobs:
        groups.append(flat[at : at + len(outs)])
        at += len(outs)
    return groups


def half_of(bit, flip, rows):
    mine = (lax.axis_index("wide") // bit) % 2
    return pl.ds(pl.multiple_of((1 - mine if flip else mine) * rows, math.gcd(rows, 256)), rows)


def add_job(terms, rows, cols):
    def body(ins, outs):
        outs[0][...] = sum(
            (ref[...] if lead is None else ref[lead]).astype(f32) for ref, (_, lead) in zip(ins, terms)
        ).astype(bf16)

    return body, [a for a, _ in terms], [((rows, cols), bf16)], vmem


def halve_job(terms, rows, cols, bit):
    def body(ins, outs):
        for flip, out in ((1, outs[0]), (0, outs[1])):
            half = half_of(bit, flip, rows)
            out[...] = sum(
                (ref[half, :] if lead is None else ref[lead, half, :]).astype(f32)
                for ref, (_, lead) in zip(ins, terms)
            ).astype(out.dtype)

    return body, [a for a, _ in terms], [((rows, cols), bf16), ((rows, cols), f32)], vmem


def part_job(keep, core, rows, cols):
    def body(ins, outs):
        kept, got = ins
        for j, out in ((1, outs[0]), (0, outs[1])):
            out[...] = (kept[j].astype(f32) + got[j].astype(f32)).astype(out.dtype)

    return body, [keep, core], [((rows, cols), bf16), ((rows, cols), f32)], vmem


def fork_job(keep, core, rows, cols, left):
    rest = cols - left

    def body(ins, outs):
        kept, got = ins
        for j, out in ((1, outs[0]), (0, outs[2])):
            out[...] = (kept[j, :, :left].astype(f32) + got[j, :, :left].astype(f32)).astype(out.dtype)
        for flip, out in ((1, outs[1]), (0, outs[3])):
            half = half_of(1, flip, rows // 2)
            for j in range(2):
                out[j] = (kept[j, half, left:].astype(f32) + got[j, half, left:].astype(f32)).astype(out.dtype)

    shapes = [(rows, left), (2, rows // 2, rest)]
    return body, [keep, core], [(shape, dtype) for dtype in (bf16, f32) for shape in shapes], vmem


def cross_job(own_left, own_right, got_left, got_right, rows, cols, left):
    rows //= 2

    def body(ins, outs):
        lefts, rights, from_left, from_right = ins
        for flip, out in ((1, outs[0]), (0, outs[2])):
            half = half_of(1, flip, rows)
            out[...] = (lefts[half, :] + from_left[half, :].astype(f32)).astype(out.dtype)
        for j, out in ((1, outs[1]), (0, outs[3])):
            out[...] = (rights[j] + from_right[j].astype(f32)).astype(out.dtype)

    shapes = [(rows, left), (rows, cols - left)]
    return (
        body, [own_left, own_right, got_left, got_right], [(shape, dtype) for dtype in (bf16, f32) for shape in shapes],
        vmem,
    )


def merge_job(lefts, rights, rows, cols, left, bit):
    def body(ins, outs):
        for flip, out in ((1, outs[0]), (0, outs[1])):
            half = half_of(bit, flip, rows)
            out[:, :left] = (ins[0][half, :].astype(f32) + ins[1][half, :].astype(f32)).astype(out.dtype)
            out[:, left:] = (ins[2][half, :].astype(f32) + ins[3][half, :].astype(f32)).astype(out.dtype)

    return body, [*lefts, *rights], [((rows, cols), bf16), ((rows, cols), f32)], vmem


def join_job(mine, other, bit):
    rows, cols = mine.shape

    def body(ins, outs):
        for flip in (0, 1):
            outs[0][half_of(bit, flip, rows), :] = ins[flip][...]

    return body, [mine, other], [((2 * rows, cols), bf16)], vmem


def turn_job(mine, other, bit):
    rows, cols = mine.shape

    def body(ins, outs):
        for flip in (0, 1):
            outs[0][:, half_of(bit, flip, rows)] = ins[flip][...].astype(f32).T

    return body, [mine, other], [((cols, 2 * rows), f32)], hbm


def spread_body(plans, w_ref, gain_ref, *refs):
    ins, outs = refs[: 2 * len(plans)], refs[2 * len(plans) :]
    for c, plan in enumerate(plans):
        mine_ref, other_ref = ins[2 * c], ins[2 * c + 1]
        rows = mine_ref.shape[0]
        for flip, ref in ((0, mine_ref), (1, other_ref)):
            for begin, length, out, to in plan:
                outs[out][half_of(1, flip, rows), to : to + length] = ref[:, begin : begin + length].astype(f32)
    share = jnp.sum(outs[0][...] * w_ref[...].astype(f32), axis=1, keepdims=True)
    share = jnp.broadcast_to(share, (share.shape[0], PAIR)).T[0:1]
    outs[-1][...] = (share / gain_ref[...].astype(f32).reshape(1, -1)).reshape(-1)


def spread_job(weight, gain, sums, plans, shapes):
    arrays = [array for pair in sums for array in pair]
    outs = [(shape, f32) for shape in (*shapes, gain.shape)]
    return lambda ins, outs: spread_body(plans, *ins, *outs), [weight, gain, *arrays], outs, hbm


def after(value, *deps):
    return lax.optimization_barrier((value, *deps))[0] if deps else value


class Moves:
    def __init__(self, narrow, wide):
        self.narrow, self.wide = narrow, wide
        self.n = lax.axis_index("narrow")
        self.w = lax.axis_index("wide")
        self.starts = [self.n, self.w % 2, (self.w // 2) % 2]

    def swap(self, value, axis, bit):
        size = self.narrow if axis == "narrow" else self.wide
        return lax.ppermute(value, axis, [(i, i ^ bit) for i in range(size)])

    def place(self, start):
        self.starts.append(start)
        return len(self.starts) - 1

    def reduce(self, send, keep, left=0):
        rows, cols = send.shape[1:]
        core = self.swap(send, "narrow", 1)
        deps = yield (send,)
        core = after(core, *deps)
        if left:
            to_left, to_right, mine_left, mine_right = yield fork_job(keep, core, rows, cols, left)
            got_left, got_right = self.swap(to_left, "narrow", 2), self.swap(to_right, "wide", 1)
            deps = yield to_left, to_right
            to_left, to_right, mine_left, mine_right = yield cross_job(
                mine_left, mine_right, after(got_left, *deps), after(got_right, *deps), rows, cols, left
            )
            got_left, got_right = self.swap(to_left, "wide", 1), self.swap(to_right, "narrow", 2)
            deps = yield to_left, to_right
            rows //= 4
            total, mine = yield merge_job(
                (mine_left, after(got_left, *deps)), (mine_right, after(got_right, *deps)), rows, cols, left, 2
            )
        else:
            total, mine = yield part_job(keep, core, rows, cols)
            got = self.swap(total, "narrow", 2)
            deps = yield (total,)
            total, mine = yield halve_job([(mine, None), (after(got, *deps), None)], rows // 2, cols, 1)
            got = self.swap(total, "wide", 1)
            deps = yield (total,)
            rows //= 4
            total, mine = yield halve_job([(mine, None), (after(got, *deps), None)], rows, cols, 2)
        got = self.swap(total, "wide", 2)
        deps = yield (total,)
        terms = [(mine, None), (after(got, *deps), None)]
        bit = 4
        while bit < self.wide:
            if bit == 4:
                (total,) = yield add_job(terms, rows, cols)
            else:
                total = whole_call("add_terms", [add_job(terms, rows, cols)])[0][0]
            got = self.swap(total, "wide", bit)
            deps = (yield (total,)) if bit == 4 else ()
            terms = [(total, None), (after(got, *deps), None)]
            bit *= 2
        (total,) = yield add_job(terms, rows, cols)
        got = self.swap(total, "wide", 2)
        deps = yield (total,)
        (total,) = yield join_job(total, after(got, *deps), 2)
        got = self.swap(total, "wide", 1)
        deps = yield (total,)
        yield total, after(got, *deps)


def begin(chain):
    return next(chain)


def close(chain, *deps):
    return chain.send(deps)


def advance(chains, *deps):
    jobs = [chain.send(deps) for chain in chains]
    results = whole_call("gradient_sums", jobs)
    return [array for chain, result in zip(chains, results) for array in chain.send(result)]


def shards(narrow, wide, layer_input, cotangent, block_size, gain_attn, w_qkv, w_out, gain_mlp, w_up, b_up, w_down, b_down):
    moves = Moves(narrow, wide)
    x, d_y = layer_input[0], cotangent[0]
    rows, width = x.shape
    seq = rows // 2
    pairs = width // PAIR
    ff = w_up.shape[1]
    n, bit = moves.n, moves.w % 2

    size = w_qkv.shape[0] // 3
    at_qkv = [
        moves.place((n ^ j) * w_qkv.shape[0] + extra)
        for j, extra in (
            (0, 0), (1, 0), (2, bit * size), (2, 2 * size), (2, (1 - bit) * size),
            (3, bit * size), (3, 2 * size), (3, (1 - bit) * size),
        )
    ]
    at_row = [moves.place((n ^ j) * w_out.shape[0]) for j in range(4)]

    at_down = [moves.place((n ^ j) * w_down.shape[0]) for j in range(4)]
    size_up = w_up.shape[0] // 3
    at_up = [
        moves.place((n ^ j) * w_up.shape[0] + extra)
        for j, extra in (
            (0, 0), (1, 0), (2, bit * size_up), (2, 2 * size_up), (2, (1 - bit) * size_up),
            (3, bit * size_up), (3, 2 * size_up), (3, (1 - bit) * size_up),
        )
    ]
    index = jnp.stack(moves.starts).astype(jnp.int32)

    def ready(*deps):
        return after(index, *deps)

    freq = 10000.0 ** (-jnp.arange(HEAD // 2).astype(f32) / (HEAD // 2))
    angles = jnp.arange(seq).astype(f32)[:, None] * freq[None, :]
    cosine, sine = jnp.cos(angles), jnp.sin(angles)
    cosine = jnp.tile(cosine, (1, 4))
    sine = jnp.concatenate([-sine, sine, -sine, sine], axis=1)

    first = lax.dynamic_slice_in_dim(w_qkv, bit * size, size, 0)
    got_first = moves.swap(first, "narrow", 2)
    second, small = vector_call(ready(first), w_qkv, gain_attn, gain_mlp, b_down, b_up)
    got_second = moves.swap(second, "narrow", 2)
    up_first, up_second = thirds_call(ready(second), w_up, (1, None))
    got_near, got_small, up_near, out_near = (
        moves.swap(after(v, first), "narrow", 1) for v in (w_qkv, small, w_up, w_out)
    )
    up_far, up_more = moves.swap(up_first, "narrow", 2), moves.swap(up_second, "narrow", 2)
    paced = pace_call(ready(up_first), cosine)
    got_first, got_near, got_small, up_near, out_near, _ = lax.optimization_barrier(
        (got_first, got_near, got_small, up_near, out_near, paced)
    )
    got_cross = moves.swap(got_first, "wide", 1)
    far_first = moves.swap(got_first, "narrow", 1)
    out_far = moves.swap(after(w_out, got_first), "narrow", 2)
    far_second, far_cross = (moves.swap(v, "narrow", 1) for v in (got_second, got_cross))
    count = w_qkv.shape[0]
    qkv_w = Weight(
        [
            (array, rows_of, place)
            for (array, rows_of), place in zip(
                (
                    (w_qkv, count), (got_near, count), (got_first, size), (got_second, size), (got_cross, size),
                    (far_first, size), (far_second, size), (far_cross, size),
                ),
                at_qkv,
            )
        ]
    )
    smalls = [small, got_small, got_second, far_second]

    block = jnp.arange(TILE, dtype=jnp.int32) // block_size[0]
    row_block, col_block = block[:, None], block[None, :]
    same, less, upto, less_t, upto_t = (
        jnp.where(ok, 0.0, -1e30).astype(f32)
        for ok in (
            row_block == col_block, col_block < row_block, col_block <= row_block,
            row_block < col_block, row_block <= col_block,
        )
    )
    dyt = d_y.T

    qkv, a1t, vec, qkv_full = qkv_call(index, x, qkv_w, smalls, ff, cosine, sine)
    up_far = after(up_far, vec)
    up_cross = moves.swap(up_far, "wide", 1)
    down_far = moves.swap(after(w_down, up_far), "narrow", 2)
    o, ot, lse = att_call(ready(up_far), qkv, (same, less_t, upto_t))
    up_pieces = [after(v, lse) for v in (up_far, up_more, up_cross)]
    up_last = [moves.swap(v, "narrow", 1) for v in up_pieces]
    out_far = after(out_far, lse)
    out_last = moves.swap(out_far, "narrow", 1)
    out_w = Weight([(a, w_out.shape[0], p) for a, p in zip((w_out, out_near, out_far, out_last), at_row)])
    up_w = Weight(
        [
            (a, r, p)
            for a, r, p in zip(
                (w_up, up_near, *up_pieces, *up_last), (w_up.shape[0],) * 2 + (size_up,) * 6, at_up
            )
        ]
    )
    x1, a2t, h, g, out_full, up_full = up_call(ready(lse), x, o, vec, out_w, up_w)
    send = grad_down_call(index, dyt, h, (1, 2), narrow)
    keep = grad_down_call(ready(send), dyt, h, (0, 2), narrow)
    down_far = after(down_far, keep)
    down_last = moves.swap(down_far, "narrow", 1)
    down_near = moves.swap(after(w_down, send), "narrow", 1)
    down_w = Weight([(a, w_down.shape[0], p) for a, p in zip((w_down, down_near, down_far, down_last), at_down)])
    chain_a = moves.reduce(send, keep, width // 2)
    begin(chain_a)
    d_u, dx1, d_o, biases, down_full = down_call(
        ready(keep, *advance([chain_a], keep)), d_y, x1, g, vec, up_full, out_full, down_w
    )
    send, keep = grad_up_call(ready(*advance([chain_a], biases)), a2t, ot, d_u, biases, narrow)
    chain_b = moves.reduce(send, keep, 2048)
    begin(chain_b)

    def back(start, count, *deps):
        return att_back_call(
            ready(*deps), qkv, d_o, o, lse, (same, less_t, upto_t), cosine, sine, start, count
        )

    paced = pace_call(ready(send), same)
    sent = advance([chain_a], keep, pace_call(ready(keep), same))
    g0 = back(0, 4, keep, *sent, *advance([chain_b], keep, paced, *sent))
    g1 = back(4, pairs - 4, g0[0], *advance([chain_a, chain_b], g0[0]))
    groups = [g0, g1]
    rights = [array for group in groups for array in group]
    send, keep = grad_qkv_call(ready(*advance([chain_b], g1[0])), a1t, rights, narrow)
    chain_c = moves.reduce(send, keep, 1152)
    begin(chain_c)
    paced = pace_call(ready(send), same)
    sent = advance([chain_a], keep)
    sent = advance([chain_b, chain_c], keep, paced, *sent)
    output = output_call(ready(keep, *sent), x1, h, vec, down_full)
    sent = advance([chain_a, chain_c], output)
    d_input = input_call(ready(output, *sent), x, dx1, vec, groups, qkv_full)
    sent = advance([chain_b, chain_c], d_input)
    sent = advance([chain_b, chain_c], *sent)
    sum_a = close(chain_a, *sent)
    (grad_down,) = whole_call("last_down", [turn_job(*sum_a, 1)])[0]
    sent = advance([chain_c], *sent, grad_down)
    sent = advance([chain_c], *sent)
    sum_b = close(chain_b, *sent)
    sum_c = close(chain_c)

    own = width // narrow
    grad_up, grad_out, biases, grad_gain_mlp = whole_call(
        "last_up",
        [
            spread_job(
                w_up, gain_mlp, [sum_b], [[(0, ff, 0, 0), (ff, width, 1, 0), (ff + width, TILE, 2, 0)]],
                [(own, ff), (own, width), (own, TILE)],
            )
        ],
    )[0]
    biases = biases[:8].reshape(-1)
    plan, begin_at, to = [], 0, 0
    for group in groups:
        cols = group[0].shape[1]
        for part in range(3):
            plan.append((begin_at, cols, 0, part * width + to))
            begin_at += cols
        to += cols
    grad_qkv, grad_gain_attn = whole_call("last_qkv", [spread_job(w_qkv, gain_attn, [sum_c], [plan], [(own, 3 * width)])])[0]
    return (
        output[None],
        d_input[None],
        grad_gain_attn,
        grad_qkv,
        grad_out,
        grad_gain_mlp,
        grad_up,
        biases[:width],
        grad_down,
        biases[width : width + own],
    )


def solution(mesh):
    return jax.shard_map(
        functools.partial(shards, mesh.shape["narrow"], mesh.shape["wide"]),
        mesh=mesh,
        in_specs=(
            P(("wide", "narrow"), None, None),
            P(("wide", "narrow"), None, None),
            P(("wide", "narrow")),
            P("narrow"),
            P("narrow", None),
            P("narrow", None),
            P("narrow"),
            P("narrow", None),
            P("narrow"),
            P("narrow", None),
            P("narrow"),
        ),
        out_specs=(
            P(("wide", "narrow"), None, None),
            P(("wide", "narrow"), None, None),
            P("narrow"),
            P("narrow", None),
            P("narrow", None),
            P("narrow"),
            P("narrow", None),
            P("narrow"),
            P("narrow", None),
            P("narrow"),
        ),
        check_vma=False,
    )
```

```python
import functools
import math

import jax
import jax.numpy as jnp
from jax import lax
from jax.experimental import pallas as pl
from jax.experimental.pallas import tpu as pltpu
from jax.sharding import PartitionSpec as P

HEAD = 64
PAIR = 2 * HEAD
TILE = 128
ORDER = (1, 3, 0, 2)
SPAN = 256
LOG2E = 1.4426950408889634
LN2 = 0.6931471805599453
f32 = jnp.float32
bf16 = jnp.bfloat16
MIB = 1 << 20


def nn(left, right):
    return jnp.dot(left, right, preferred_element_type=f32)


def nt(left, right):
    return lax.dot_general(left, right, (((1,), (1,)), ((), ())), preferred_element_type=f32)


def norm_rows(values):
    centre = values - jnp.mean(values, axis=-1, keepdims=True)
    inverse = lax.rsqrt(jnp.mean(centre * centre, axis=-1, keepdims=True) + 1e-05)
    return centre * inverse, inverse


def norm_back(d_norm, scaled, inverse, gain):
    d_scaled = d_norm * gain
    return inverse * (
        d_scaled
        - jnp.mean(d_scaled, axis=-1, keepdims=True)
        - scaled * jnp.mean(d_scaled * scaled, axis=-1, keepdims=True)
    )


def swap_halves(tile):
    lane = lax.broadcasted_iota(jnp.int32, (1, PAIR), 1) % HEAD
    return jnp.where(
        lane < HEAD // 2,
        pltpu.roll(tile, PAIR - HEAD // 2, 1),
        pltpu.roll(tile, HEAD // 2, 1),
    )


class Weight:
    def __init__(self, pieces):
        self.arrays = [array for array, _, _ in pieces]
        self.plan = [(rows, place) for _, rows, place in pieces]
        self.rows = sum(rows for rows, _ in self.plan)
        self.cols = self.arrays[0].shape[1]

    def specs(self, near=True):
        space = pltpu.VMEM if near else pltpu.HBM
        return [pl.BlockSpec(memory_space=pltpu.HBM)] + [pl.BlockSpec(memory_space=space)] * (len(self.plan) - 1)

    def near(self, at):
        return list(range(at + 1, at + len(self.plan)))

    def whole(self):
        return pltpu.VMEM((self.rows, self.cols), bf16)

    def sems(self):
        return [pltpu.SemaphoreType.DMA((len(self.plan),))]

    def scratch(self):
        return [self.whole(), *self.sems()]


def fetches(at_ref, plan, parts, whole, sems):
    copies = []
    for i, ((rows, place), part) in enumerate(zip(plan, parts)):
        start = pl.multiple_of(at_ref[place], math.gcd(rows, 256))
        copies.append(pltpu.make_async_copy(part.at[pl.ds(0, rows)], whole.at[pl.ds(start, rows)], sems.at[i]))
    return copies


def fetch(at_ref, *weights):
    @pl.when(pl.program_id(0) == 0)
    def _():
        for weight in weights:
            for copy in fetches(at_ref, *weight):
                copy.start()


def arrive(at_ref, weight):
    @pl.when(pl.program_id(0) == 0)
    def _():
        for copy in fetches(at_ref, *weight):
            copy.wait()


def step_rows(step):
    return pl.ds(pl.multiple_of(pl.program_id(0) * step, step), step)


def take(refs, *groups):
    out, at = [], 0
    for group in groups:
        out.append(refs[at : at + len(group)])
        at += len(group)
    return out + [refs[at:]]


def fixed(shape):
    return pl.BlockSpec(shape, lambda *_: (0,) * len(shape), pipeline_mode=pl.Buffered(1))


def call(body, name, grid, in_specs, out_specs, out_shape, scratch, limit, cost, near=(), aliases=None, moved=1 << 20):
    fun = pl.pallas_call(
        body,
        name=name,
        out_shape=out_shape,
        input_output_aliases=aliases or {},
        grid_spec=pltpu.PrefetchScalarGridSpec(
            num_scalar_prefetch=1,
            grid=grid,
            in_specs=in_specs,
            out_specs=out_specs,
            scratch_shapes=scratch,
        ),
        compiler_params=pltpu.CompilerParams(
            dimension_semantics=("arbitrary",) * len(grid), vmem_limit_bytes=limit * MIB
        ),
        cost_estimate=pl.CostEstimate(
            flops=int(cost * 1e12), bytes_accessed=moved, transcendentals=0
        ),
    )

    def run(index, *args):
        args = [
            pltpu.with_memory_space_constraint(arg, pltpu.VMEM if i in near else pltpu.HBM)
            for i, arg in enumerate(args)
        ]
        return fun(index, *args)

    return run


def hbm(shape, dtype):
    return pltpu.HBM(shape, dtype)


def vmem(shape, dtype):
    return pltpu.VMEM(shape, dtype)


def sds(shape, dtype):
    return jax.ShapeDtypeStruct(shape, dtype)


def small_rows(cols, gain1_ref, gain2_ref, down_ref, up_ref):
    def lanes(*refs):
        values = [ref[...].astype(f32).reshape(1, -1) for ref in refs]
        return jnp.concatenate(
            [v for v in values for _ in range(cols // (len(refs) * v.shape[1]))], axis=1
        )

    row = lax.broadcasted_iota(jnp.int32, (8, cols), 0)
    return jnp.where(row == 0, lanes(gain1_ref, gain2_ref, down_ref), lanes(up_ref)).astype(bf16)


def vector_body(idx_ref, w_ref, gain1_ref, gain2_ref, down_ref, up_ref, out_ref, small_ref):
    size = w_ref.shape[0]
    small = small_rows(w_ref.shape[1], gain1_ref, gain2_ref, down_ref, up_ref)
    out_ref[:size, :] = w_ref[...]
    out_ref[size:, :] = small
    small_ref[...] = small


def vector_call(index, weight, *vectors):
    size, cols = weight.shape[0] // 3, weight.shape[1]
    shapes = [(size + 8, cols), (8, cols)]
    return call(
        vector_body,
        "vector_message",
        (1,),
        [pl.BlockSpec((size, cols), lambda i, s: (2, 0))] + [fixed(v.shape) for v in vectors],
        [fixed(shape) for shape in shapes],
        [vmem(shape, bf16) for shape in shapes],
        [],
        6,
        1.5,
    )(index, weight, *vectors)


def thirds_body(idx_ref, *refs):
    count = len(refs) // 2
    for ref, out_ref in zip(refs[:count], refs[count:]):
        out_ref[...] = ref[...]


def thirds_call(index, weight, places):
    size, cols = weight.shape[0] // 3, weight.shape[1]
    return call(
        thirds_body,
        "next_message",
        (1,),
        [pl.BlockSpec((size, cols), lambda i, s, p=p: (2 if p is None else s[p], 0)) for p in places],
        [fixed((size, cols))] * len(places),
        [vmem((size, cols), bf16)] * len(places),
        [],
        6,
        1.5,
    )(index, *[weight] * len(places))


def qkv_body(plan, n, idx_ref, x_ref, cos_ref, sin_ref, *refs):
    smalls, parts, refs = take(refs, range(n), plan)
    qkv_ref, a1t_ref, vec_ref, whole, sems = refs
    weight = (plan, parts, whole, sems)
    fetch(idx_ref, weight)
    width = x_ref.shape[1]
    here = step_rows(x_ref.shape[0])

    @pl.when(pl.program_id(0) == 0)
    def _():
        lane = lax.broadcasted_iota(jnp.int32, (1, width), 1) // (width // n)
        values = [ref[...].astype(f32) for ref in smalls]
        vec_ref[...] = jnp.zeros_like(vec_ref)
        for i in range(3):
            vec_ref[i : i + 1, :width] = sum(
                jnp.where(lane == (idx_ref[0] ^ j), v[0:1, i * width : (i + 1) * width], 0.0)
                for j, v in enumerate(values)
            )
        size = vec_ref.shape[1] // n
        for c in range(n):
            vec_ref[3:4, c * size : (c + 1) * size] = sum(
                jnp.where((idx_ref[0] ^ j) == c, v[1:2, :size], 0.0) for j, v in enumerate(values)
            )

    scaled, _ = norm_rows(x_ref[...].astype(f32))
    a1 = (scaled * vec_ref[0:1, :width]).astype(bf16)
    a1t_ref[...] = a1.T
    cosine, sine = cos_ref[...], sin_ref[...]
    arrive(idx_ref, weight)
    for part in range(3):
        y = nn(a1, whole[:, part * width : (part + 1) * width])
        if part == 2:
            qkv_ref[here, part * width :] = y.astype(bf16)
            continue
        for t in range(width // PAIR):
            tile = y[:, t * PAIR : (t + 1) * PAIR]
            tile = tile * cosine + swap_halves(tile) * sine
            if part == 0:
                tile = tile * (LOG2E / 8.0)
            at = part * width + t * PAIR
            qkv_ref[here, at : at + PAIR] = tile.astype(bf16)


def qkv_call(index, x, weight, smalls, ff, cosine, sine):
    rows, width = x.shape
    wide = weight.cols
    step = 256
    per = cosine.shape[0] // step

    def vector(array):
        return pl.BlockSpec((8, wide), lambda i, s: (array.shape[0] // 8 - 1, 0))

    return call(
        functools.partial(qkv_body, weight.plan, len(smalls)),
        "norm_qkv",
        (rows // step,),
        [
            pl.BlockSpec((step, width), lambda i, s: (i, 0)),
            pl.BlockSpec((step, PAIR), lambda i, s: (i % per, 0)),
            pl.BlockSpec((step, PAIR), lambda i, s: (i % per, 0)),
        ]
        + [vector(array) for array in smalls]
        + weight.specs(),
        [
            fixed((rows, wide)),
            pl.BlockSpec((width, step), lambda i, s: (0, i)),
            pl.BlockSpec((8, ff), lambda i, s: (0, 0)),
            fixed((weight.rows, wide)),
        ],
        [vmem((rows, wide), bf16), hbm((width, rows), bf16), hbm((8, ff), f32), hbm((weight.rows, wide), bf16)],
        weight.sems(),
        16,
        7,
        near=(*range(3, 3 + len(smalls)), *weight.near(3 + len(smalls))),
    )(index, x, cosine, sine, *smalls, *weight.arrays)


def head_masks():
    lane = lax.broadcasted_iota(jnp.int32, (1, PAIR), 1)
    return lane < HEAD, lane >= HEAD


def widen(tile, allowed):
    count = SPAN // TILE
    never = jnp.full(tile.shape, -1e30, f32)
    before = jnp.zeros(tile.shape, f32) if allowed else never
    return jnp.concatenate(
        [
            jnp.concatenate([tile if a == b else (before if a < b else never) for b in range(count)], axis=1)
            for a in range(count)
        ],
        axis=0,
    )


def att_body(seq, idx_ref, qkv_ref, same_ref, less_ref, upto_ref, o_ref, ot_ref, lse_ref):
    def columns(part):
        start = part * (qkv_ref.shape[1] // 3) + pl.program_id(0) * PAIR
        return pl.ds(pl.multiple_of(start, PAIR), PAIR)

    queries, k_all = columns(0), qkv_ref[:, columns(1)]
    keys = [jnp.where(m, k_all, jnp.zeros_like(k_all)) for m in head_masks()]
    v_t = qkv_ref[:, columns(2)].T
    ones = jnp.ones((16, 2 * seq), bf16)
    vals = [jnp.concatenate([v_t[h * HEAD : (h + 1) * HEAD], ones], axis=0) for h in range(2)]
    same, less, upto = widen(same_ref[...], False), widen(less_ref[...], True), widen(upto_ref[...], True)

    def scores(lo, clean, h):
        hi = lo + SPAN
        row = lo + seq if clean else lo
        query = qkv_ref[row : row + SPAN, queries]
        pieces = [nt(keys[h][seq + lo : seq + hi], query) + (upto if clean else less)]
        if lo > 0:
            pieces.append(nt(keys[h][seq : seq + lo], query))
        if not clean:
            pieces.append(nt(keys[h][lo:hi], query) + same)
        return pieces

    def soften(pieces):
        top = functools.reduce(jnp.maximum, [jnp.max(p, axis=0, keepdims=True) for p in pieces])
        return top, [jnp.exp2(p - top).astype(bf16) for p in pieces]

    def mix(lo, clean, h, weights):
        hi = lo + SPAN
        out = nn(vals[h][:, seq + lo : seq + hi], weights[0])
        if lo > 0:
            out = out + nn(vals[h][:, seq : seq + lo], weights[1])
        if not clean:
            out = out + nn(vals[h][:, lo:hi], weights[-1])
        return out

    def finish(lo, clean, softened):
        row = lo + seq if clean else lo
        outs = [mix(lo, clean, h, softened[h][1]) for h in range(2)]
        out = jnp.concatenate([o[:HEAD] / o[HEAD : HEAD + 1] for o in outs], axis=0)
        ot_ref[:, row : row + SPAN] = out.astype(bf16)
        o_ref[row : row + SPAN, :] = out.T.astype(bf16)
        for h in range(2):
            lse_ref[0, h : h + 1, row : row + SPAN] = softened[h][0] + jnp.log2(outs[h][HEAD : HEAD + 1])

    work = [(lo, clean) for lo in range(0, seq, SPAN) for clean in (False, True)]
    ahead = [scores(*work[0], h) for h in range(2)]
    behind = None
    for i, item in enumerate(work):
        now = ahead
        if i + 1 < len(work):
            ahead = [scores(*work[i + 1], h) for h in range(2)]
        softened = [soften(pieces) for pieces in now]
        if behind is not None:
            finish(*behind)
        behind = (*item, softened)
    finish(*behind)


def att_call(index, qkv, masks):
    rows = qkv.shape[0]
    width = qkv.shape[1] // 3
    pairs = width // PAIR
    return call(
        functools.partial(att_body, rows // 2),
        "attention",
        (pairs,),
        [fixed(qkv.shape)] + [fixed((TILE, TILE))] * 3,
        [
            pl.BlockSpec((rows, PAIR), lambda p, s: (0, p)),
            pl.BlockSpec((PAIR, rows), lambda p, s: (p, 0)),
            pl.BlockSpec((1, 2, rows), lambda p, s: (p, 0, 0)),
        ],
        [hbm((rows, width), bf16), hbm((width, rows), bf16), hbm((pairs, 2, rows), f32)],
        [],
        16,
        12.0,
        near=(0,),
    )(index, qkv, *masks)


def att_back_body(
    seq, idx_ref, q_ref, k_ref, v_ref, do_ref, o_ref, lse_ref, same_ref, less_ref, upto_ref,
    cos_ref, sin_ref, dq_ref, dk_ref, dv_ref, dqt_ref,
):
    first, second = head_masks()
    q_all, k_all, v_all, do_all = q_ref[...], k_ref[...], v_ref[...], do_ref[...]

    def split(array):
        return [jnp.where(m, array, jnp.zeros_like(array)) for m in (first, second)]

    queries, keys, vals, dos = split(q_all), split(k_all), split(v_all), split(do_all)
    keys_t = k_all.T
    product = do_all.astype(f32) * o_ref[...].astype(f32)
    high = product.astype(bf16)
    rest = (product - high.astype(f32)).astype(bf16)
    picked = lax.broadcasted_iota(jnp.int32, (8, PAIR), 0)
    picked = jnp.where(picked == lax.broadcasted_iota(jnp.int32, (8, PAIR), 1) // HEAD, 1.0, 0.0).astype(bf16)
    delta = nt(picked, high) + nt(picked, rest)
    same, less, upto = widen(same_ref[...], False), widen(less_ref[...], True), widen(upto_ref[...], True)
    dqt_ref[...] = jnp.zeros_like(dqt_ref)

    def products(unit):
        return [
            (nt(keys[h][k : k + SPAN], q_all[q:end]), nt(vals[h][k : k + SPAN], do_all[q:end]))
            for h, k, q, end, _ in unit[0]
        ]

    def soften(unit, values):
        out = []
        for (h, _, q, end, mask), (scores, d_probs) in zip(unit[0], values):
            scores = scores - lse_ref[0, h : h + 1, q:end]
            probs = jnp.exp2(scores[:, :SPAN] + mask)
            if end - q > SPAN:
                probs = jnp.concatenate([probs, jnp.exp2(scores[:, SPAN:])], axis=1)
            d_scores = probs * (d_probs - delta[h : h + 1, q:end])
            out.append((probs.astype(bf16), d_scores.astype(bf16)))
        return out

    def rotate_back(tile, row):
        at = row % seq
        cosine, sine = cos_ref[at : at + SPAN, :], sin_ref[at : at + SPAN, :]
        return tile * cosine - swap_halves(tile) * sine

    def gather(unit, values, sums):
        items, last = unit
        d_vals, d_keys = sums
        for (h, k, q, end, _), (probs, d_scores) in zip(items, values):
            d_vals = d_vals + nn(probs, dos[h][q:end])
            d_keys = d_keys + nn(d_scores, queries[h][q:end])
            at = slice(h * HEAD, (h + 1) * HEAD)
            dqt_ref[at, q:end] += nn(keys_t[at, k : k + SPAN], d_scores)
        if not last:
            return d_vals, d_keys
        k = items[0][1]
        dv_ref[k : k + SPAN, :] = d_vals.astype(bf16)
        dk_ref[k : k + SPAN, :] = rotate_back(d_keys * LN2, k).astype(bf16)
        return 0.0, 0.0

    units = []
    for lo in range(0, seq, SPAN):
        units.append(([(h, lo, lo, lo + SPAN, same) for h in range(2)], True))
        for base, mask in ((0, less), (seq, upto)):
            units.append(([(h, seq + lo, base + lo, base + seq, mask) for h in range(2)], base > 0))
    ahead, behind, sums = products(units[0]), None, (0.0, 0.0)
    for i, unit in enumerate(units):
        now = ahead
        if i + 1 < len(units):
            ahead = products(units[i + 1])
        values = soften(unit, now)
        if behind is not None:
            sums = gather(*behind, sums)
        behind = (unit, values)
    gather(*behind, sums)
    for r in range(0, 2 * seq, SPAN):
        tile = dqt_ref[:, r : r + SPAN].T * 0.125
        dq_ref[r : r + SPAN, :] = rotate_back(tile, r).astype(bf16)


def att_back_call(index, qkv, d_o, o, lse, masks, cosine, sine, start, count):
    rows = qkv.shape[0]
    width = qkv.shape[1] // 3
    pairs = width // PAIR
    seq = rows // 2

    def column(part):
        return pl.BlockSpec((rows, PAIR), lambda p, s: (0, part * pairs + start + p))

    out = pl.BlockSpec((rows, PAIR), lambda p, s: (0, p))
    return call(
        functools.partial(att_back_body, seq),
        "attention_back",
        (count,),
        [column(0), column(1), column(2), column(0), column(0)]
        + [pl.BlockSpec((1, 2, rows), lambda p, s: (start + p, 0, 0))]
        + [fixed((TILE, TILE))] * 3
        + [fixed((seq, PAIR))] * 2,
        [out] * 3,
        [vmem((rows, count * PAIR), bf16)] * 3,
        [pltpu.VMEM((PAIR, rows), f32)],
        16,
        3.6 * count,
    )(index, qkv, qkv, qkv, d_o, o, lse, *masks, cosine, sine)


def up_body(out_at, up_at, idx_ref, x_ref, o_ref, vec_ref, *refs):
    outs, ups, refs = take(refs, out_at, up_at)
    x1_ref, a2t_ref, h_ref, g_ref, w_out, w_up, out_sems, up_sems = refs
    out_weight, up_weight = (out_at, outs, w_out, out_sems), (up_at, ups, w_up, up_sems)
    fetch(idx_ref, out_weight, up_weight)
    arrive(idx_ref, out_weight)
    width = x_ref.shape[1]
    here = step_rows(x_ref.shape[0])
    x1 = x_ref[...].astype(f32) + nn(o_ref[...], w_out[...])
    x1_ref[...] = x1
    scaled, _ = norm_rows(x1)
    a2 = (scaled * vec_ref[1:2, :width]).astype(bf16)
    a2t_ref[:, here] = a2.T
    arrive(idx_ref, up_weight)
    c0 = math.sqrt(2.0 / math.pi)
    c1 = c0 * 0.044715
    chunk = 512
    for at in range(0, w_up.shape[1], chunk):
        u = nn(a2, w_up[:, at : at + chunk]) + vec_ref[3:4, at : at + chunk]
        square = u * u
        t = jnp.tanh(u * (c1 * square + c0))
        half = 0.5 * t + 0.5
        h_ref[here, at : at + chunk] = (u * half).astype(bf16)
        slope = u * (1.5 * c1 * square + 0.5 * c0)
        g_ref[here, at : at + chunk] = (half + slope * (1.0 - t * t)).astype(bf16)


def up_call(index, x, o, vec, w_out, w_up):
    rows, width = x.shape
    ff = w_up.cols
    step = 256

    def row(cols):
        return pl.BlockSpec((step, cols), lambda i, s: (i, 0))

    outs = [
        hbm((rows, width), f32), vmem((width, rows), bf16), vmem((rows, ff), bf16), vmem((rows, ff), bf16),
        w_out.whole(), w_up.whole(),
    ]
    return call(
        functools.partial(up_body, w_out.plan, w_up.plan),
        "feed_up",
        (rows // step,),
        [row(width), row(width), fixed(vec.shape)] + w_out.specs() + w_up.specs(),
        [row(width)] + [fixed(out.shape) for out in outs[1:]],
        outs,
        w_out.sems() + w_up.sems(),
        12,
        18,
        near=w_out.near(3) + w_up.near(3 + len(w_out.plan)),
    )(index, x, o, vec, *w_out.arrays, *w_up.arrays)


def down_body(down_at, idx_ref, dy_ref, x1_ref, g_ref, vec_ref, w_up, w_out, *refs):
    downs, refs = take(refs, down_at)
    du_ref, dx1_ref, do_ref, bias_ref, w_down, down_sems = refs
    weight = (down_at, downs, w_down, down_sems)
    fetch(idx_ref, weight)

    @pl.when(pl.program_id(0) == 0)
    def _():
        bias_ref[...] = jnp.zeros_like(bias_ref)

    width = dy_ref.shape[1]
    here = step_rows(dy_ref.shape[0])
    low = dy_ref[...]
    d_y = low.astype(f32)
    bias_ref[1:2, :width] += jnp.sum(d_y, axis=0, keepdims=True)
    arrive(idx_ref, weight)
    chunk = 512
    d_a2 = 0.0
    for at in range(0, w_up.shape[1], chunk):
        d_u = nt(low, w_down[at : at + chunk, :]) * g_ref[here, at : at + chunk].astype(f32)
        bias_ref[0:1, at : at + chunk] += jnp.sum(d_u, axis=0, keepdims=True)
        d_u = d_u.astype(bf16)
        du_ref[here, at : at + chunk] = d_u
        d_a2 = d_a2 + nt(d_u, w_up[:, at : at + chunk])
    scaled, inverse = norm_rows(x1_ref[...])
    d_x1 = d_y + norm_back(d_a2, scaled, inverse, vec_ref[1:2, :width])
    dx1_ref[...] = d_x1
    d_x1 = d_x1.astype(bf16)
    du_ref[here, w_up.shape[1] :] = d_x1
    do_ref[...] = nt(d_x1, w_out[...]).astype(bf16)


def down_call(index, d_y, x1, g, vec, w_up, w_out, w_down):
    rows, width = d_y.shape
    ff = w_up.shape[1]
    step = 256

    def row(cols):
        return pl.BlockSpec((step, cols), lambda i, s: (i, 0))

    return call(
        functools.partial(down_body, w_down.plan),
        "feed_back",
        (rows // step,),
        [row(width), row(width)] + [fixed(array.shape) for array in (g, vec, w_up, w_out)] + w_down.specs(),
        [fixed((rows, ff + width)), row(width), row(width), fixed((2, ff)),
         fixed((ff, width))],
        [
            vmem((rows, ff + width), bf16), hbm((rows, width), f32), hbm((rows, width), bf16),
            vmem((2, ff), f32), w_down.whole(),
        ],
        w_down.sems(),
        14,
        20,
        near=(2, 4, 5, *w_down.near(6)),
    )(index, d_y, x1, g, vec, w_up, w_out, *w_down.arrays)


def grad_down_body(offsets, idx_ref, dyt_ref, h_ref, out_ref):
    base, step = offsets
    cols = out_ref.shape[2]
    shard = idx_ref[0] ^ (base + step * pl.program_id(0))
    columns = pl.ds(pl.multiple_of(shard * cols, cols), cols)
    out_ref[pl.program_id(0)] = nn(dyt_ref[...], h_ref[:, columns]).astype(bf16)


def grad_down_call(index, dyt, h, offsets, shards):
    width, rows = dyt.shape
    cols = h.shape[1] // shards
    return call(
        functools.partial(grad_down_body, offsets),
        "grad_down",
        (2,),
        [fixed(dyt.shape), fixed(h.shape)],
        fixed((2, width, cols)),
        vmem((2, width, cols), bf16),
        [],
        8,
        3,
        near=(0, 1),
    )(index, dyt, h)


def shard_rows(idx_ref, rows):
    return [pl.ds(pl.multiple_of((idx_ref[0] ^ j) * rows, math.gcd(rows, 256)), rows) for j in ORDER]


def grad_up_body(chunks, idx_ref, a_ref, o_ref, du_ref, bias_ref, send_ref, keep_ref, left_ref):
    rows = send_ref.shape[1]
    width = a_ref.shape[0]
    i = pl.program_id(0)
    columns = pl.ds(pl.multiple_of(i * width, width), width)
    for step, ref in ((0, a_ref), (chunks, o_ref)):

        @pl.when(i == step)
        def _(ref=ref):
            for k, at in enumerate(shard_rows(idx_ref, rows)):
                left_ref[k * rows : (k + 1) * rows, :] = ref[at, :]

    y = nn(left_ref[...], du_ref[:, columns]).astype(bf16)
    for k in range(4):
        (send_ref if k < 2 else keep_ref)[k % 2, :, columns] = y[k * rows : (k + 1) * rows]

    @pl.when(i == chunks)
    def _():
        at = (chunks + 1) * width
        lanes = send_ref.shape[2] - at
        shards = width // rows
        pad = jnp.zeros((1, 2 * lanes - rows), f32)
        for k, j in enumerate(ORDER):
            shard = idx_ref[0] ^ j
            out_ref = send_ref if k < 2 else keep_ref
            tiles = [
                bias_ref[0:1, pl.ds(pl.multiple_of(shard * width + t * lanes, lanes), lanes)]
                for t in range(width // lanes)
            ]
            own = sum(
                jnp.where(shard == t, bias_ref[1:2, t * rows : (t + 1) * rows], 0.0) for t in range(shards)
            )
            own = jnp.concatenate([own, pad], axis=1)
            tiles += [own[:, :lanes], own[:, lanes:]]
            block = jnp.concatenate(tiles + [jnp.zeros((16 - len(tiles), lanes), f32)], axis=0)
            out_ref[k % 2, :16, at:] = block.astype(bf16)
            out_ref[k % 2, 16:, at:] = jnp.zeros((rows - 16, lanes), bf16)


def grad_up_call(index, a2t, ot, d_u, biases, shards):
    width, rows = a2t.shape
    own = width // shards
    ff = d_u.shape[1] - width
    chunks = ff // width
    cols = ff + width + TILE
    return call(
        functools.partial(grad_up_body, chunks),
        "grad_up_out",
        (chunks + 1,),
        [fixed(array.shape) for array in (a2t, ot, d_u, biases)],
        [fixed((2, own, cols))] * 2,
        [vmem((2, own, cols), bf16)] * 2,
        [pltpu.VMEM((width, rows), bf16)],
        10,
        4.7,
        near=range(4),
    )(index, a2t, ot, d_u, biases)


def grad_qkv_body(idx_ref, a_ref, *refs):
    rights, send_ref, keep_ref = refs[:-2], refs[-2], refs[-1]
    rows = send_ref.shape[1]
    left = jnp.concatenate([a_ref[at, :] for at in shard_rows(idx_ref, rows)], axis=0)
    at = 0
    for right in rights:
        cols = right.shape[1]
        y = nn(left, right[...]).astype(bf16)
        for k in range(4):
            (send_ref if k < 2 else keep_ref)[k % 2, :, at : at + cols] = y[k * rows : (k + 1) * rows]
        at += cols


def grad_qkv_call(index, a1t, rights, shards):
    own = a1t.shape[0] // shards
    cols = sum(right.shape[1] for right in rights)
    return call(
        grad_qkv_body,
        "grad_qkv",
        (1,),
        [fixed(array.shape) for array in (a1t, *rights)],
        [fixed((2, own, cols))] * 2,
        [vmem((2, own, cols), bf16)] * 2,
        [],
        10,
        1.0 + cols / 1000.0,
        near=range(1 + len(rights)),
    )(index, a1t, *rights)


def input_body(groups, idx_ref, x_ref, dx1_ref, vec_ref, w_ref, *refs):
    grads, (dx_ref,) = refs[: 3 * groups], refs[3 * groups :]
    width = x_ref.shape[1]
    here = step_rows(x_ref.shape[0])
    scaled, inverse = norm_rows(x_ref[...].astype(f32))
    d_a1 = 0.0
    for part in range(3):
        at = part * width
        for g in range(groups):
            ref = grads[3 * g + part]
            cols = ref.shape[1]
            d_a1 = d_a1 + nt(ref[here, :], w_ref[:, at : at + cols])
            at += cols
    d_x = dx1_ref[...] + norm_back(d_a1, scaled, inverse, vec_ref[0:1, :width])
    dx_ref[...] = d_x.astype(bf16)


def input_call(index, x, dx1, vec, d_groups, weight):
    rows, width = x.shape
    step = 256

    def row(cols):
        return pl.BlockSpec((step, cols), lambda i, s: (i, 0))

    flat = [array for group in d_groups for array in group]
    return call(
        functools.partial(input_body, len(d_groups)),
        "grad_input",
        (rows // step,),
        [row(width), row(width)] + [fixed(array.shape) for array in (vec, weight, *flat)],
        row(width),
        hbm((rows, width), bf16),
        [],
        14,
        9,
        near=range(4, 4 + len(flat)),
    )(index, x, dx1, vec, weight, *flat)


def output_body(idx_ref, x1_ref, h_ref, vec_ref, w_ref, out_ref):
    y = x1_ref[...] + nn(h_ref[...], w_ref[...]) + vec_ref[2:3, : x1_ref.shape[1]]
    out_ref[...] = y.astype(bf16)


def output_call(index, x1, h, vec, weight):
    rows, width = x1.shape

    def row(cols):
        return pl.BlockSpec((256, cols), lambda i, s: (i, 0))

    return call(
        output_body,
        "layer_output",
        (rows // 256,),
        [row(width), row(h.shape[1]), fixed(vec.shape), fixed(weight.shape)],
        row(width),
        hbm((rows, width), bf16),
        [],
        14,
        8,
        near=(3,),
    )(index, x1, h, vec, weight)


def pace_body(idx_ref, tile_ref, out_ref):
    out_ref[...] = tile_ref[:8, :]


def pace_call(index, tile):
    return call(
        pace_body,
        "pace",
        (1,),
        [fixed(tile.shape)],
        fixed((8, tile.shape[1])),
        vmem((8, tile.shape[1]), f32),
        [],
        2,
        5,
        near=(0,),
    )(index, tile)


def whole_call(name, jobs):
    arrays = [array for _, ins, _, _ in jobs for array in ins]
    results = [place(shape, dtype) for _, _, outs, place in jobs for shape, dtype in outs]

    def run(*refs):
        ins, outs = refs[: len(arrays)], refs[len(arrays) :]
        at, to = 0, 0
        for body, job_ins, job_outs, _ in jobs:
            body(ins[at : at + len(job_ins)], outs[to : to + len(job_outs)])
            at, to = at + len(job_ins), to + len(job_outs)

    flat = pl.pallas_call(
        run,
        name=name,
        in_specs=[pl.BlockSpec(memory_space=pltpu.VMEM)] * len(arrays),
        out_specs=[pl.BlockSpec(memory_space=pltpu.VMEM)] * len(results),
        out_shape=results,
        compiler_params=pltpu.CompilerParams(vmem_limit_bytes=10 * MIB),
        cost_estimate=pl.CostEstimate(
            flops=0,
            bytes_accessed=sum(array.size * array.dtype.itemsize for array in arrays),
            transcendentals=0,
        ),
    )(*(pltpu.with_memory_space_constraint(array, pltpu.VMEM) for array in arrays))
    groups, at = [], 0
    for _, _, outs, _ in jobs:
        groups.append(flat[at : at + len(outs)])
        at += len(outs)
    return groups


def half_of(bit, flip, rows):
    mine = (lax.axis_index("wide") // bit) % 2
    return pl.ds(pl.multiple_of((1 - mine if flip else mine) * rows, math.gcd(rows, 256)), rows)


def add_job(terms, rows, cols):
    def body(ins, outs):
        outs[0][...] = sum(
            (ref[...] if lead is None else ref[lead]).astype(f32) for ref, (_, lead) in zip(ins, terms)
        ).astype(bf16)

    return body, [a for a, _ in terms], [((rows, cols), bf16)], vmem


def halve_job(terms, rows, cols, bit):
    def body(ins, outs):
        for flip, out in ((1, outs[0]), (0, outs[1])):
            half = half_of(bit, flip, rows)
            out[...] = sum(
                (ref[half, :] if lead is None else ref[lead, half, :]).astype(f32)
                for ref, (_, lead) in zip(ins, terms)
            ).astype(out.dtype)

    return body, [a for a, _ in terms], [((rows, cols), bf16), ((rows, cols), f32)], vmem


def part_job(keep, core, rows, cols):
    def body(ins, outs):
        kept, got = ins
        for j, out in ((1, outs[0]), (0, outs[1])):
            out[...] = (kept[j].astype(f32) + got[j].astype(f32)).astype(out.dtype)

    return body, [keep, core], [((rows, cols), bf16), ((rows, cols), f32)], vmem


def fork_job(keep, core, rows, cols, left):
    rest = cols - left

    def body(ins, outs):
        kept, got = ins
        for j, out in ((1, outs[0]), (0, outs[2])):
            out[...] = (kept[j, :, :left].astype(f32) + got[j, :, :left].astype(f32)).astype(out.dtype)
        for flip, out in ((1, outs[1]), (0, outs[3])):
            half = half_of(1, flip, rows // 2)
            for j in range(2):
                out[j] = (kept[j, half, left:].astype(f32) + got[j, half, left:].astype(f32)).astype(out.dtype)

    shapes = [(rows, left), (2, rows // 2, rest)]
    return body, [keep, core], [(shape, dtype) for dtype in (bf16, f32) for shape in shapes], vmem


def cross_job(own_left, own_right, got_left, got_right, rows, cols, left):
    rows //= 2

    def body(ins, outs):
        lefts, rights, from_left, from_right = ins
        for flip, out in ((1, outs[0]), (0, outs[2])):
            half = half_of(1, flip, rows)
            out[...] = (lefts[half, :] + from_left[half, :].astype(f32)).astype(out.dtype)
        for j, out in ((1, outs[1]), (0, outs[3])):
            out[...] = (rights[j] + from_right[j].astype(f32)).astype(out.dtype)

    shapes = [(rows, left), (rows, cols - left)]
    return (
        body, [own_left, own_right, got_left, got_right], [(shape, dtype) for dtype in (bf16, f32) for shape in shapes],
        vmem,
    )


def merge_job(lefts, rights, rows, cols, left, bit):
    def body(ins, outs):
        for flip, out in ((1, outs[0]), (0, outs[1])):
            half = half_of(bit, flip, rows)
            out[:, :left] = (ins[0][half, :].astype(f32) + ins[1][half, :].astype(f32)).astype(out.dtype)
            out[:, left:] = (ins[2][half, :].astype(f32) + ins[3][half, :].astype(f32)).astype(out.dtype)

    return body, [*lefts, *rights], [((rows, cols), bf16), ((rows, cols), f32)], vmem


def join_job(mine, other, bit):
    rows, cols = mine.shape

    def body(ins, outs):
        for flip in (0, 1):
            outs[0][half_of(bit, flip, rows), :] = ins[flip][...]

    return body, [mine, other], [((2 * rows, cols), bf16)], vmem


def turn_job(mine, other, bit):
    rows, cols = mine.shape

    def body(ins, outs):
        for flip in (0, 1):
            outs[0][:, half_of(bit, flip, rows)] = ins[flip][...].astype(f32).T

    return body, [mine, other], [((cols, 2 * rows), f32)], hbm


def spread_body(plans, w_ref, gain_ref, *refs):
    ins, outs = refs[: 2 * len(plans)], refs[2 * len(plans) :]
    for c, plan in enumerate(plans):
        mine_ref, other_ref = ins[2 * c], ins[2 * c + 1]
        rows = mine_ref.shape[0]
        for flip, ref in ((0, mine_ref), (1, other_ref)):
            for begin, length, out, to in plan:
                outs[out][half_of(1, flip, rows), to : to + length] = ref[:, begin : begin + length].astype(f32)
    share = jnp.sum(outs[0][...] * w_ref[...].astype(f32), axis=1, keepdims=True)
    share = jnp.broadcast_to(share, (share.shape[0], PAIR)).T[0:1]
    outs[-1][...] = (share / gain_ref[...].astype(f32).reshape(1, -1)).reshape(-1)


def spread_job(weight, gain, sums, plans, shapes):
    arrays = [array for pair in sums for array in pair]
    outs = [(shape, f32) for shape in (*shapes, gain.shape)]
    return lambda ins, outs: spread_body(plans, *ins, *outs), [weight, gain, *arrays], outs, hbm


def after(value, *deps):
    return lax.optimization_barrier((value, *deps))[0] if deps else value


class Moves:
    def __init__(self, narrow, wide):
        self.narrow, self.wide = narrow, wide
        self.n = lax.axis_index("narrow")
        self.w = lax.axis_index("wide")
        self.starts = [self.n, self.w % 2, (self.w // 2) % 2]

    def swap(self, value, axis, bit):
        size = self.narrow if axis == "narrow" else self.wide
        return lax.ppermute(value, axis, [(i, i ^ bit) for i in range(size)])

    def place(self, start):
        self.starts.append(start)
        return len(self.starts) - 1

    def reduce(self, send, keep, left=0):
        rows, cols = send.shape[1:]
        core = self.swap(send, "narrow", 1)
        deps = yield (send,)
        core = after(core, *deps)
        if left:
            to_left, to_right, mine_left, mine_right = yield fork_job(keep, core, rows, cols, left)
            got_left, got_right = self.swap(to_left, "narrow", 2), self.swap(to_right, "wide", 1)
            deps = yield to_left, to_right
            to_left, to_right, mine_left, mine_right = yield cross_job(
                mine_left, mine_right, after(got_left, *deps), after(got_right, *deps), rows, cols, left
            )
            got_left, got_right = self.swap(to_left, "wide", 1), self.swap(to_right, "narrow", 2)
            deps = yield to_left, to_right
            rows //= 4
            total, mine = yield merge_job(
                (mine_left, after(got_left, *deps)), (mine_right, after(got_right, *deps)), rows, cols, left, 2
            )
        else:
            total, mine = yield part_job(keep, core, rows, cols)
            got = self.swap(total, "narrow", 2)
            deps = yield (total,)
            total, mine = yield halve_job([(mine, None), (after(got, *deps), None)], rows // 2, cols, 1)
            got = self.swap(total, "wide", 1)
            deps = yield (total,)
            rows //= 4
            total, mine = yield halve_job([(mine, None), (after(got, *deps), None)], rows, cols, 2)
        got = self.swap(total, "wide", 2)
        deps = yield (total,)
        terms = [(mine, None), (after(got, *deps), None)]
        bit = 4
        while bit < self.wide:
            if bit == 4:
                (total,) = yield add_job(terms, rows, cols)
            else:
                total = whole_call("add_terms", [add_job(terms, rows, cols)])[0][0]
            got = self.swap(total, "wide", bit)
            deps = (yield (total,)) if bit == 4 else ()
            terms = [(total, None), (after(got, *deps), None)]
            bit *= 2
        (total,) = yield add_job(terms, rows, cols)
        got = self.swap(total, "wide", 2)
        deps = yield (total,)
        (total,) = yield join_job(total, after(got, *deps), 2)
        got = self.swap(total, "wide", 1)
        deps = yield (total,)
        yield total, after(got, *deps)


def begin(chain):
    return next(chain)


def close(chain, *deps):
    return chain.send(deps)


def advance(chains, *deps):
    jobs = [chain.send(deps) for chain in chains]
    results = whole_call("gradient_sums", jobs)
    return [array for chain, result in zip(chains, results) for array in chain.send(result)]


def shards(narrow, wide, layer_input, cotangent, block_size, gain_attn, w_qkv, w_out, gain_mlp, w_up, b_up, w_down, b_down):
    moves = Moves(narrow, wide)
    x, d_y = layer_input[0], cotangent[0]
    rows, width = x.shape
    seq = rows // 2
    pairs = width // PAIR
    ff = w_up.shape[1]
    n, bit = moves.n, moves.w % 2

    size = w_qkv.shape[0] // 3
    at_qkv = [
        moves.place((n ^ j) * w_qkv.shape[0] + extra)
        for j, extra in (
            (0, 0), (1, 0), (2, bit * size), (2, 2 * size), (2, (1 - bit) * size),
            (3, bit * size), (3, 2 * size), (3, (1 - bit) * size),
        )
    ]
    at_row = [moves.place((n ^ j) * w_out.shape[0]) for j in range(4)]

    at_down = [moves.place((n ^ j) * w_down.shape[0]) for j in range(4)]
    size_up = w_up.shape[0] // 3
    at_up = [
        moves.place((n ^ j) * w_up.shape[0] + extra)
        for j, extra in (
            (0, 0), (1, 0), (2, bit * size_up), (2, 2 * size_up), (2, (1 - bit) * size_up),
            (3, bit * size_up), (3, 2 * size_up), (3, (1 - bit) * size_up),
        )
    ]
    index = jnp.stack(moves.starts).astype(jnp.int32)

    def ready(*deps):
        return after(index, *deps)

    freq = 10000.0 ** (-jnp.arange(HEAD // 2).astype(f32) / (HEAD // 2))
    angles = jnp.arange(seq).astype(f32)[:, None] * freq[None, :]
    cosine, sine = jnp.cos(angles), jnp.sin(angles)
    cosine = jnp.tile(cosine, (1, 4))
    sine = jnp.concatenate([-sine, sine, -sine, sine], axis=1)

    first = lax.dynamic_slice_in_dim(w_qkv, bit * size, size, 0)
    got_first = moves.swap(first, "narrow", 2)
    second, small = vector_call(ready(first), w_qkv, gain_attn, gain_mlp, b_down, b_up)
    got_second = moves.swap(second, "narrow", 2)
    up_first, up_second = thirds_call(ready(second), w_up, (1, None))
    got_near, got_small, up_near, out_near = (
        moves.swap(after(v, first), "narrow", 1) for v in (w_qkv, small, w_up, w_out)
    )
    up_far, up_more = moves.swap(up_first, "narrow", 2), moves.swap(up_second, "narrow", 2)
    paced = pace_call(ready(up_first), cosine)
    got_first, got_near, got_small, up_near, out_near, _ = lax.optimization_barrier(
        (got_first, got_near, got_small, up_near, out_near, paced)
    )
    got_cross = moves.swap(got_first, "wide", 1)
    far_first = moves.swap(got_first, "narrow", 1)
    out_far = moves.swap(after(w_out, got_first), "narrow", 2)
    far_second, far_cross = (moves.swap(v, "narrow", 1) for v in (got_second, got_cross))
    count = w_qkv.shape[0]
    qkv_w = Weight(
        [
            (array, rows_of, place)
            for (array, rows_of), place in zip(
                (
                    (w_qkv, count), (got_near, count), (got_first, size), (got_second, size), (got_cross, size),
                    (far_first, size), (far_second, size), (far_cross, size),
                ),
                at_qkv,
            )
        ]
    )
    smalls = [small, got_small, got_second, far_second]

    block = jnp.arange(TILE, dtype=jnp.int32) // block_size[0]
    row_block, col_block = block[:, None], block[None, :]
    same, less, upto, less_t, upto_t = (
        jnp.where(ok, 0.0, -1e30).astype(f32)
        for ok in (
            row_block == col_block, col_block < row_block, col_block <= row_block,
            row_block < col_block, row_block <= col_block,
        )
    )
    dyt = d_y.T

    qkv, a1t, vec, qkv_full = qkv_call(index, x, qkv_w, smalls, ff, cosine, sine)
    up_far = after(up_far, vec)
    up_cross = moves.swap(up_far, "wide", 1)
    down_far = moves.swap(after(w_down, up_far), "narrow", 2)
    o, ot, lse = att_call(ready(up_far), qkv, (same, less_t, upto_t))
    up_pieces = [after(v, lse) for v in (up_far, up_more, up_cross)]
    up_last = [moves.swap(v, "narrow", 1) for v in up_pieces]
    out_far = after(out_far, lse)
    out_last = moves.swap(out_far, "narrow", 1)
    out_w = Weight([(a, w_out.shape[0], p) for a, p in zip((w_out, out_near, out_far, out_last), at_row)])
    up_w = Weight(
        [
            (a, r, p)
            for a, r, p in zip(
                (w_up, up_near, *up_pieces, *up_last), (w_up.shape[0],) * 2 + (size_up,) * 6, at_up
            )
        ]
    )
    x1, a2t, h, g, out_full, up_full = up_call(ready(lse), x, o, vec, out_w, up_w)
    send = grad_down_call(index, dyt, h, (1, 2), narrow)
    keep = grad_down_call(ready(send), dyt, h, (0, 2), narrow)
    down_far = after(down_far, keep)
    down_last = moves.swap(down_far, "narrow", 1)
    down_near = moves.swap(after(w_down, send), "narrow", 1)
    down_w = Weight([(a, w_down.shape[0], p) for a, p in zip((w_down, down_near, down_far, down_last), at_down)])
    chain_a = moves.reduce(send, keep, width // 2)
    begin(chain_a)
    d_u, dx1, d_o, biases, down_full = down_call(
        ready(keep, *advance([chain_a], keep)), d_y, x1, g, vec, up_full, out_full, down_w
    )
    send, keep = grad_up_call(ready(*advance([chain_a], biases)), a2t, ot, d_u, biases, narrow)
    chain_b = moves.reduce(send, keep, 2048)
    begin(chain_b)

    def back(start, count, *deps):
        return att_back_call(
            ready(*deps), qkv, d_o, o, lse, (same, less_t, upto_t), cosine, sine, start, count
        )

    paced = pace_call(ready(send), same)
    sent = advance([chain_a], keep, pace_call(ready(keep), same))
    g0 = back(0, 4, keep, *sent, *advance([chain_b], keep, paced, *sent))
    sent = advance([chain_a], g0[0])
    g1 = back(4, pairs - 4, g0[0], *sent, *advance([chain_b], g0[0], *sent))
    groups = [g0, g1]
    rights = [array for group in groups for array in group]
    send, keep = grad_qkv_call(ready(*advance([chain_b], g1[0])), a1t, rights, narrow)
    chain_c = moves.reduce(send, keep, 1152)
    begin(chain_c)
    paced = pace_call(ready(send), same)
    sent = advance([chain_a], keep)
    sent = advance([chain_b, chain_c], keep, paced, *sent)
    output = output_call(ready(keep, *sent), x1, h, vec, down_full)
    sent_a = advance([chain_a], output)
    sent = advance([chain_c], output, *sent_a)
    d_input = input_call(ready(output, *sent_a, *sent), x, dx1, vec, groups, qkv_full)
    sent = advance([chain_b, chain_c], d_input)
    sent = advance([chain_b, chain_c], *sent)
    sum_a = close(chain_a, *sent)
    (grad_down,) = whole_call("last_down", [turn_job(*sum_a, 1)])[0]
    sent = advance([chain_c], *sent, grad_down)
    sent = advance([chain_c], *sent)
    sum_b = close(chain_b, *sent)
    sum_c = close(chain_c)

    own = width // narrow
    grad_up, grad_out, biases, grad_gain_mlp = whole_call(
        "last_up",
        [
            spread_job(
                w_up, gain_mlp, [sum_b], [[(0, ff, 0, 0), (ff, width, 1, 0), (ff + width, TILE, 2, 0)]],
                [(own, ff), (own, width), (own, TILE)],
            )
        ],
    )[0]
    biases = biases[:8].reshape(-1)
    plan, begin_at, to = [], 0, 0
    for group in groups:
        cols = group[0].shape[1]
        for part in range(3):
            plan.append((begin_at, cols, 0, part * width + to))
            begin_at += cols
        to += cols
    grad_qkv, grad_gain_attn = whole_call("last_qkv", [spread_job(w_qkv, gain_attn, [sum_c], [plan], [(own, 3 * width)])])[0]
    return (
        output[None],
        d_input[None],
        grad_gain_attn,
        grad_qkv,
        grad_out,
        grad_gain_mlp,
        grad_up,
        biases[:width],
        grad_down,
        biases[width : width + own],
    )


def solution(mesh):
    return jax.shard_map(
        functools.partial(shards, mesh.shape["narrow"], mesh.shape["wide"]),
        mesh=mesh,
        in_specs=(
            P(("wide", "narrow"), None, None),
            P(("wide", "narrow"), None, None),
            P(("wide", "narrow")),
            P("narrow"),
            P("narrow", None),
            P("narrow", None),
            P("narrow"),
            P("narrow", None),
            P("narrow"),
            P("narrow", None),
            P("narrow"),
        ),
        out_specs=(
            P(("wide", "narrow"), None, None),
            P(("wide", "narrow"), None, None),
            P("narrow"),
            P("narrow", None),
            P("narrow", None),
            P("narrow"),
            P("narrow", None),
            P("narrow"),
            P("narrow", None),
            P("narrow"),
        ),
        check_vma=False,
    )
```

```python
import functools
import math

import jax
import jax.numpy as jnp
from jax import lax
from jax.experimental import pallas as pl
from jax.experimental.pallas import tpu as pltpu
from jax.sharding import PartitionSpec as P

HEAD = 64
PAIR = 2 * HEAD
TILE = 128
ORDER = (1, 3, 0, 2)
SPAN = 256
LOG2E = 1.4426950408889634
LN2 = 0.6931471805599453
f32 = jnp.float32
bf16 = jnp.bfloat16
MIB = 1 << 20


def nn(left, right):
    return jnp.dot(left, right, preferred_element_type=f32)


def nt(left, right):
    return lax.dot_general(left, right, (((1,), (1,)), ((), ())), preferred_element_type=f32)


def norm_rows(values):
    centre = values - jnp.mean(values, axis=-1, keepdims=True)
    inverse = lax.rsqrt(jnp.mean(centre * centre, axis=-1, keepdims=True) + 1e-05)
    return centre * inverse, inverse


def norm_back(d_norm, scaled, inverse, gain):
    d_scaled = d_norm * gain
    return inverse * (
        d_scaled
        - jnp.mean(d_scaled, axis=-1, keepdims=True)
        - scaled * jnp.mean(d_scaled * scaled, axis=-1, keepdims=True)
    )


def swap_halves(tile):
    lane = lax.broadcasted_iota(jnp.int32, (1, PAIR), 1) % HEAD
    return jnp.where(
        lane < HEAD // 2,
        pltpu.roll(tile, PAIR - HEAD // 2, 1),
        pltpu.roll(tile, HEAD // 2, 1),
    )


class Weight:
    def __init__(self, pieces):
        self.arrays = [array for array, _, _ in pieces]
        self.plan = [(rows, place) for _, rows, place in pieces]
        self.rows = sum(rows for rows, _ in self.plan)
        self.cols = self.arrays[0].shape[1]

    def specs(self, near=True):
        space = pltpu.VMEM if near else pltpu.HBM
        return [pl.BlockSpec(memory_space=pltpu.HBM)] + [pl.BlockSpec(memory_space=space)] * (len(self.plan) - 1)

    def near(self, at):
        return list(range(at + 1, at + len(self.plan)))

    def whole(self):
        return pltpu.VMEM((self.rows, self.cols), bf16)

    def sems(self):
        return [pltpu.SemaphoreType.DMA((len(self.plan),))]

    def scratch(self):
        return [self.whole(), *self.sems()]


def fetches(at_ref, plan, parts, whole, sems):
    copies = []
    for i, ((rows, place), part) in enumerate(zip(plan, parts)):
        start = pl.multiple_of(at_ref[place], math.gcd(rows, 256))
        copies.append(pltpu.make_async_copy(part.at[pl.ds(0, rows)], whole.at[pl.ds(start, rows)], sems.at[i]))
    return copies


def fetch(at_ref, *weights):
    @pl.when(pl.program_id(0) == 0)
    def _():
        for weight in weights:
            for copy in fetches(at_ref, *weight):
                copy.start()


def arrive(at_ref, weight):
    @pl.when(pl.program_id(0) == 0)
    def _():
        for copy in fetches(at_ref, *weight):
            copy.wait()


def step_rows(step):
    return pl.ds(pl.multiple_of(pl.program_id(0) * step, step), step)


def take(refs, *groups):
    out, at = [], 0
    for group in groups:
        out.append(refs[at : at + len(group)])
        at += len(group)
    return out + [refs[at:]]


def fixed(shape):
    return pl.BlockSpec(shape, lambda *_: (0,) * len(shape), pipeline_mode=pl.Buffered(1))


def call(body, name, grid, in_specs, out_specs, out_shape, scratch, limit, cost, near=(), aliases=None, moved=1 << 20):
    fun = pl.pallas_call(
        body,
        name=name,
        out_shape=out_shape,
        input_output_aliases=aliases or {},
        grid_spec=pltpu.PrefetchScalarGridSpec(
            num_scalar_prefetch=1,
            grid=grid,
            in_specs=in_specs,
            out_specs=out_specs,
            scratch_shapes=scratch,
        ),
        compiler_params=pltpu.CompilerParams(
            dimension_semantics=("arbitrary",) * len(grid), vmem_limit_bytes=limit * MIB
        ),
        cost_estimate=pl.CostEstimate(
            flops=int(cost * 1e12), bytes_accessed=moved, transcendentals=0
        ),
    )

    def run(index, *args):
        args = [
            pltpu.with_memory_space_constraint(arg, pltpu.VMEM if i in near else pltpu.HBM)
            for i, arg in enumerate(args)
        ]
        return fun(index, *args)

    return run


def hbm(shape, dtype):
    return pltpu.HBM(shape, dtype)


def vmem(shape, dtype):
    return pltpu.VMEM(shape, dtype)


def sds(shape, dtype):
    return jax.ShapeDtypeStruct(shape, dtype)


def small_rows(cols, gain1_ref, gain2_ref, down_ref, up_ref):
    def lanes(*refs):
        values = [ref[...].astype(f32).reshape(1, -1) for ref in refs]
        return jnp.concatenate(
            [v for v in values for _ in range(cols // (len(refs) * v.shape[1]))], axis=1
        )

    row = lax.broadcasted_iota(jnp.int32, (8, cols), 0)
    return jnp.where(row == 0, lanes(gain1_ref, gain2_ref, down_ref), lanes(up_ref)).astype(bf16)


def vector_body(idx_ref, w_ref, gain1_ref, gain2_ref, down_ref, up_ref, out_ref, small_ref):
    size = w_ref.shape[0]
    small = small_rows(w_ref.shape[1], gain1_ref, gain2_ref, down_ref, up_ref)
    out_ref[:size, :] = w_ref[...]
    out_ref[size:, :] = small
    small_ref[...] = small


def vector_call(index, weight, *vectors):
    size, cols = weight.shape[0] // 3, weight.shape[1]
    shapes = [(size + 8, cols), (8, cols)]
    return call(
        vector_body,
        "vector_message",
        (1,),
        [pl.BlockSpec((size, cols), lambda i, s: (2, 0))] + [fixed(v.shape) for v in vectors],
        [fixed(shape) for shape in shapes],
        [vmem(shape, bf16) for shape in shapes],
        [],
        6,
        1.5,
    )(index, weight, *vectors)


def thirds_body(idx_ref, *refs):
    count = len(refs) // 2
    for ref, out_ref in zip(refs[:count], refs[count:]):
        out_ref[...] = ref[...]


def thirds_call(index, weight, places):
    size, cols = weight.shape[0] // 3, weight.shape[1]
    return call(
        thirds_body,
        "next_message",
        (1,),
        [pl.BlockSpec((size, cols), lambda i, s, p=p: (2 if p is None else s[p], 0)) for p in places],
        [fixed((size, cols))] * len(places),
        [vmem((size, cols), bf16)] * len(places),
        [],
        6,
        1.5,
    )(index, *[weight] * len(places))


def qkv_body(plan, n, idx_ref, x_ref, cos_ref, sin_ref, *refs):
    smalls, parts, refs = take(refs, range(n), plan)
    qkv_ref, a1t_ref, vec_ref, whole, sems = refs
    weight = (plan, parts, whole, sems)
    fetch(idx_ref, weight)
    width = x_ref.shape[1]
    here = step_rows(x_ref.shape[0])

    @pl.when(pl.program_id(0) == 0)
    def _():
        lane = lax.broadcasted_iota(jnp.int32, (1, width), 1) // (width // n)
        values = [ref[...].astype(f32) for ref in smalls]
        vec_ref[...] = jnp.zeros_like(vec_ref)
        for i in range(3):
            vec_ref[i : i + 1, :width] = sum(
                jnp.where(lane == (idx_ref[0] ^ j), v[0:1, i * width : (i + 1) * width], 0.0)
                for j, v in enumerate(values)
            )
        size = vec_ref.shape[1] // n
        for c in range(n):
            vec_ref[3:4, c * size : (c + 1) * size] = sum(
                jnp.where((idx_ref[0] ^ j) == c, v[1:2, :size], 0.0) for j, v in enumerate(values)
            )

    scaled, _ = norm_rows(x_ref[...].astype(f32))
    a1 = (scaled * vec_ref[0:1, :width]).astype(bf16)
    a1t_ref[...] = a1.T
    cosine, sine = cos_ref[...], sin_ref[...]
    arrive(idx_ref, weight)
    for part in range(3):
        y = nn(a1, whole[:, part * width : (part + 1) * width])
        if part == 2:
            qkv_ref[here, part * width :] = y.astype(bf16)
            continue
        for t in range(width // PAIR):
            tile = y[:, t * PAIR : (t + 1) * PAIR]
            tile = tile * cosine + swap_halves(tile) * sine
            if part == 0:
                tile = tile * (LOG2E / 8.0)
            at = part * width + t * PAIR
            qkv_ref[here, at : at + PAIR] = tile.astype(bf16)


def qkv_call(index, x, weight, smalls, ff, cosine, sine):
    rows, width = x.shape
    wide = weight.cols
    step = 256
    per = cosine.shape[0] // step

    def vector(array):
        return pl.BlockSpec((8, wide), lambda i, s: (array.shape[0] // 8 - 1, 0))

    return call(
        functools.partial(qkv_body, weight.plan, len(smalls)),
        "norm_qkv",
        (rows // step,),
        [
            pl.BlockSpec((step, width), lambda i, s: (i, 0)),
            pl.BlockSpec((step, PAIR), lambda i, s: (i % per, 0)),
            pl.BlockSpec((step, PAIR), lambda i, s: (i % per, 0)),
        ]
        + [vector(array) for array in smalls]
        + weight.specs(),
        [
            fixed((rows, wide)),
            pl.BlockSpec((width, step), lambda i, s: (0, i)),
            pl.BlockSpec((8, ff), lambda i, s: (0, 0)),
            fixed((weight.rows, wide)),
        ],
        [vmem((rows, wide), bf16), hbm((width, rows), bf16), hbm((8, ff), f32), hbm((weight.rows, wide), bf16)],
        weight.sems(),
        16,
        7,
        near=(*range(3, 3 + len(smalls)), *weight.near(3 + len(smalls))),
    )(index, x, cosine, sine, *smalls, *weight.arrays)


def head_masks():
    lane = lax.broadcasted_iota(jnp.int32, (1, PAIR), 1)
    return lane < HEAD, lane >= HEAD


def widen(tile, allowed):
    count = SPAN // TILE
    never = jnp.full(tile.shape, -1e30, f32)
    before = jnp.zeros(tile.shape, f32) if allowed else never
    return jnp.concatenate(
        [
            jnp.concatenate([tile if a == b else (before if a < b else never) for b in range(count)], axis=1)
            for a in range(count)
        ],
        axis=0,
    )


def att_body(seq, idx_ref, qkv_ref, same_ref, less_ref, upto_ref, o_ref, ot_ref, lse_ref):
    def columns(part):
        start = part * (qkv_ref.shape[1] // 3) + pl.program_id(0) * PAIR
        return pl.ds(pl.multiple_of(start, PAIR), PAIR)

    queries, k_all = columns(0), qkv_ref[:, columns(1)]
    keys = [jnp.where(m, k_all, jnp.zeros_like(k_all)) for m in head_masks()]
    v_t = qkv_ref[:, columns(2)].T
    ones = jnp.ones((16, 2 * seq), bf16)
    vals = [jnp.concatenate([v_t[h * HEAD : (h + 1) * HEAD], ones], axis=0) for h in range(2)]
    same, less, upto = widen(same_ref[...], False), widen(less_ref[...], True), widen(upto_ref[...], True)

    def scores(lo, clean, h):
        hi = lo + SPAN
        row = lo + seq if clean else lo
        query = qkv_ref[row : row + SPAN, queries]
        pieces = [nt(keys[h][seq + lo : seq + hi], query) + (upto if clean else less)]
        if lo > 0:
            pieces.append(nt(keys[h][seq : seq + lo], query))
        if not clean:
            pieces.append(nt(keys[h][lo:hi], query) + same)
        return pieces

    def soften(pieces):
        top = functools.reduce(jnp.maximum, [jnp.max(p, axis=0, keepdims=True) for p in pieces])
        return top, [jnp.exp2(p - top).astype(bf16) for p in pieces]

    def mix(lo, clean, h, weights):
        hi = lo + SPAN
        out = nn(vals[h][:, seq + lo : seq + hi], weights[0])
        if lo > 0:
            out = out + nn(vals[h][:, seq : seq + lo], weights[1])
        if not clean:
            out = out + nn(vals[h][:, lo:hi], weights[-1])
        return out

    def finish(lo, clean, softened):
        row = lo + seq if clean else lo
        outs = [mix(lo, clean, h, softened[h][1]) for h in range(2)]
        out = jnp.concatenate([o[:HEAD] / o[HEAD : HEAD + 1] for o in outs], axis=0)
        ot_ref[:, row : row + SPAN] = out.astype(bf16)
        o_ref[row : row + SPAN, :] = out.T.astype(bf16)
        for h in range(2):
            lse_ref[0, h : h + 1, row : row + SPAN] = softened[h][0] + jnp.log2(outs[h][HEAD : HEAD + 1])

    work = [(lo, clean) for lo in range(0, seq, SPAN) for clean in (False, True)]
    ahead = [scores(*work[0], h) for h in range(2)]
    behind = None
    for i, item in enumerate(work):
        now = ahead
        if i + 1 < len(work):
            ahead = [scores(*work[i + 1], h) for h in range(2)]
        softened = [soften(pieces) for pieces in now]
        if behind is not None:
            finish(*behind)
        behind = (*item, softened)
    finish(*behind)


def att_call(index, qkv, masks):
    rows = qkv.shape[0]
    width = qkv.shape[1] // 3
    pairs = width // PAIR
    return call(
        functools.partial(att_body, rows // 2),
        "attention",
        (pairs,),
        [fixed(qkv.shape)] + [fixed((TILE, TILE))] * 3,
        [
            pl.BlockSpec((rows, PAIR), lambda p, s: (0, p)),
            pl.BlockSpec((PAIR, rows), lambda p, s: (p, 0)),
            pl.BlockSpec((1, 2, rows), lambda p, s: (p, 0, 0)),
        ],
        [hbm((rows, width), bf16), hbm((width, rows), bf16), hbm((pairs, 2, rows), f32)],
        [],
        16,
        12.0,
        near=(0,),
    )(index, qkv, *masks)


def att_back_body(
    seq, idx_ref, q_ref, k_ref, v_ref, do_ref, o_ref, lse_ref, same_ref, less_ref, upto_ref,
    cos_ref, sin_ref, dq_ref, dk_ref, dv_ref, dqt_ref,
):
    first, second = head_masks()
    q_all, k_all, v_all, do_all = q_ref[...], k_ref[...], v_ref[...], do_ref[...]

    def split(array):
        return [jnp.where(m, array, jnp.zeros_like(array)) for m in (first, second)]

    queries, keys, vals, dos = split(q_all), split(k_all), split(v_all), split(do_all)
    keys_t = k_all.T
    product = do_all.astype(f32) * o_ref[...].astype(f32)
    high = product.astype(bf16)
    rest = (product - high.astype(f32)).astype(bf16)
    picked = lax.broadcasted_iota(jnp.int32, (8, PAIR), 0)
    picked = jnp.where(picked == lax.broadcasted_iota(jnp.int32, (8, PAIR), 1) // HEAD, 1.0, 0.0).astype(bf16)
    delta = nt(picked, high) + nt(picked, rest)
    same, less, upto = widen(same_ref[...], False), widen(less_ref[...], True), widen(upto_ref[...], True)
    dqt_ref[...] = jnp.zeros_like(dqt_ref)

    def products(unit):
        return [
            (nt(keys[h][k : k + SPAN], q_all[q:end]), nt(vals[h][k : k + SPAN], do_all[q:end]))
            for h, k, q, end, _ in unit[0]
        ]

    def soften(unit, values):
        out = []
        for (h, _, q, end, mask), (scores, d_probs) in zip(unit[0], values):
            scores = scores - lse_ref[0, h : h + 1, q:end]
            probs = jnp.exp2(scores[:, :SPAN] + mask)
            if end - q > SPAN:
                probs = jnp.concatenate([probs, jnp.exp2(scores[:, SPAN:])], axis=1)
            d_scores = probs * (d_probs - delta[h : h + 1, q:end])
            out.append((probs.astype(bf16), d_scores.astype(bf16)))
        return out

    def rotate_back(tile, row):
        at = row % seq
        cosine, sine = cos_ref[at : at + SPAN, :], sin_ref[at : at + SPAN, :]
        return tile * cosine - swap_halves(tile) * sine

    def gather(unit, values, sums):
        items, last = unit
        d_vals, d_keys = sums
        for (h, k, q, end, _), (probs, d_scores) in zip(items, values):
            d_vals = d_vals + nn(probs, dos[h][q:end])
            d_keys = d_keys + nn(d_scores, queries[h][q:end])
            at = slice(h * HEAD, (h + 1) * HEAD)
            dqt_ref[at, q:end] += nn(keys_t[at, k : k + SPAN], d_scores)
        if not last:
            return d_vals, d_keys
        k = items[0][1]
        dv_ref[k : k + SPAN, :] = d_vals.astype(bf16)
        dk_ref[k : k + SPAN, :] = rotate_back(d_keys * LN2, k).astype(bf16)
        return 0.0, 0.0

    units = []
    for lo in range(0, seq, SPAN):
        units.append(([(h, lo, lo, lo + SPAN, same) for h in range(2)], True))
        for base, mask in ((0, less), (seq, upto)):
            units.append(([(h, seq + lo, base + lo, base + seq, mask) for h in range(2)], base > 0))
    ahead, behind, sums = products(units[0]), None, (0.0, 0.0)
    for i, unit in enumerate(units):
        now = ahead
        if i + 1 < len(units):
            ahead = products(units[i + 1])
        values = soften(unit, now)
        if behind is not None:
            sums = gather(*behind, sums)
        behind = (unit, values)
    gather(*behind, sums)
    for r in range(0, 2 * seq, SPAN):
        tile = dqt_ref[:, r : r + SPAN].T * 0.125
        dq_ref[r : r + SPAN, :] = rotate_back(tile, r).astype(bf16)


def att_back_call(index, qkv, d_o, o, lse, masks, cosine, sine, start, count):
    rows = qkv.shape[0]
    width = qkv.shape[1] // 3
    pairs = width // PAIR
    seq = rows // 2

    def column(part):
        return pl.BlockSpec((rows, PAIR), lambda p, s: (0, part * pairs + start + p))

    out = pl.BlockSpec((rows, PAIR), lambda p, s: (0, p))
    return call(
        functools.partial(att_back_body, seq),
        "attention_back",
        (count,),
        [column(0), column(1), column(2), column(0), column(0)]
        + [pl.BlockSpec((1, 2, rows), lambda p, s: (start + p, 0, 0))]
        + [fixed((TILE, TILE))] * 3
        + [fixed((seq, PAIR))] * 2,
        [out] * 3,
        [vmem((rows, count * PAIR), bf16)] * 3,
        [pltpu.VMEM((PAIR, rows), f32)],
        16,
        3.6 * count,
    )(index, qkv, qkv, qkv, d_o, o, lse, *masks, cosine, sine)


def up_body(out_at, up_at, idx_ref, x_ref, o_ref, vec_ref, *refs):
    outs, ups, refs = take(refs, out_at, up_at)
    x1_ref, a2t_ref, h_ref, g_ref, w_out, w_up, out_sems, up_sems = refs
    out_weight, up_weight = (out_at, outs, w_out, out_sems), (up_at, ups, w_up, up_sems)
    fetch(idx_ref, out_weight, up_weight)
    arrive(idx_ref, out_weight)
    width = x_ref.shape[1]
    here = step_rows(x_ref.shape[0])
    x1 = x_ref[...].astype(f32) + nn(o_ref[...], w_out[...])
    x1_ref[...] = x1
    scaled, _ = norm_rows(x1)
    a2 = (scaled * vec_ref[1:2, :width]).astype(bf16)
    a2t_ref[:, here] = a2.T
    arrive(idx_ref, up_weight)
    c0 = math.sqrt(2.0 / math.pi)
    c1 = c0 * 0.044715
    chunk = 512
    for at in range(0, w_up.shape[1], chunk):
        u = nn(a2, w_up[:, at : at + chunk]) + vec_ref[3:4, at : at + chunk]
        square = u * u
        t = jnp.tanh(u * (c1 * square + c0))
        half = 0.5 * t + 0.5
        h_ref[here, at : at + chunk] = (u * half).astype(bf16)
        slope = u * (1.5 * c1 * square + 0.5 * c0)
        g_ref[here, at : at + chunk] = (half + slope * (1.0 - t * t)).astype(bf16)


def up_call(index, x, o, vec, w_out, w_up):
    rows, width = x.shape
    ff = w_up.cols
    step = 256

    def row(cols):
        return pl.BlockSpec((step, cols), lambda i, s: (i, 0))

    outs = [
        hbm((rows, width), f32), vmem((width, rows), bf16), vmem((rows, ff), bf16), vmem((rows, ff), bf16),
        w_out.whole(), w_up.whole(),
    ]
    return call(
        functools.partial(up_body, w_out.plan, w_up.plan),
        "feed_up",
        (rows // step,),
        [row(width), row(width), fixed(vec.shape)] + w_out.specs() + w_up.specs(),
        [row(width)] + [fixed(out.shape) for out in outs[1:]],
        outs,
        w_out.sems() + w_up.sems(),
        12,
        18,
        near=w_out.near(3) + w_up.near(3 + len(w_out.plan)),
    )(index, x, o, vec, *w_out.arrays, *w_up.arrays)


def down_body(down_at, idx_ref, dy_ref, x1_ref, g_ref, vec_ref, w_up, w_out, *refs):
    downs, refs = take(refs, down_at)
    du_ref, dx1_ref, do_ref, bias_ref, w_down, down_sems = refs
    weight = (down_at, downs, w_down, down_sems)
    fetch(idx_ref, weight)

    @pl.when(pl.program_id(0) == 0)
    def _():
        bias_ref[...] = jnp.zeros_like(bias_ref)

    width = dy_ref.shape[1]
    here = step_rows(dy_ref.shape[0])
    low = dy_ref[...]
    d_y = low.astype(f32)
    bias_ref[1:2, :width] += jnp.sum(d_y, axis=0, keepdims=True)
    arrive(idx_ref, weight)
    chunk = 512
    d_a2 = 0.0
    for at in range(0, w_up.shape[1], chunk):
        d_u = nt(low, w_down[at : at + chunk, :]) * g_ref[here, at : at + chunk].astype(f32)
        bias_ref[0:1, at : at + chunk] += jnp.sum(d_u, axis=0, keepdims=True)
        d_u = d_u.astype(bf16)
        du_ref[here, at : at + chunk] = d_u
        d_a2 = d_a2 + nt(d_u, w_up[:, at : at + chunk])
    scaled, inverse = norm_rows(x1_ref[...])
    d_x1 = d_y + norm_back(d_a2, scaled, inverse, vec_ref[1:2, :width])
    dx1_ref[...] = d_x1
    d_x1 = d_x1.astype(bf16)
    du_ref[here, w_up.shape[1] :] = d_x1
    do_ref[...] = nt(d_x1, w_out[...]).astype(bf16)


def down_call(index, d_y, x1, g, vec, w_up, w_out, w_down):
    rows, width = d_y.shape
    ff = w_up.shape[1]
    step = 256

    def row(cols):
        return pl.BlockSpec((step, cols), lambda i, s: (i, 0))

    return call(
        functools.partial(down_body, w_down.plan),
        "feed_back",
        (rows // step,),
        [row(width), row(width)] + [fixed(array.shape) for array in (g, vec, w_up, w_out)] + w_down.specs(),
        [fixed((rows, ff + width)), row(width), row(width), fixed((2, ff)),
         fixed((ff, width))],
        [
            vmem((rows, ff + width), bf16), hbm((rows, width), f32), hbm((rows, width), bf16),
            vmem((2, ff), f32), w_down.whole(),
        ],
        w_down.sems(),
        14,
        20,
        near=(2, 4, 5, *w_down.near(6)),
    )(index, d_y, x1, g, vec, w_up, w_out, *w_down.arrays)


def grad_down_body(offsets, idx_ref, dyt_ref, h_ref, out_ref):
    base, step = offsets
    cols = out_ref.shape[2]
    shard = idx_ref[0] ^ (base + step * pl.program_id(0))
    columns = pl.ds(pl.multiple_of(shard * cols, cols), cols)
    out_ref[pl.program_id(0)] = nn(dyt_ref[...], h_ref[:, columns]).astype(bf16)


def grad_down_call(index, dyt, h, offsets, shards):
    width, rows = dyt.shape
    cols = h.shape[1] // shards
    return call(
        functools.partial(grad_down_body, offsets),
        "grad_down",
        (2,),
        [fixed(dyt.shape), fixed(h.shape)],
        fixed((2, width, cols)),
        vmem((2, width, cols), bf16),
        [],
        8,
        3,
        near=(0, 1),
    )(index, dyt, h)


def shard_rows(idx_ref, rows):
    return [pl.ds(pl.multiple_of((idx_ref[0] ^ j) * rows, math.gcd(rows, 256)), rows) for j in ORDER]


def grad_up_body(chunks, idx_ref, a_ref, o_ref, du_ref, bias_ref, send_ref, keep_ref, left_ref):
    rows = send_ref.shape[1]
    width = a_ref.shape[0]
    i = pl.program_id(0)
    columns = pl.ds(pl.multiple_of(i * width, width), width)
    for step, ref in ((0, a_ref), (chunks, o_ref)):

        @pl.when(i == step)
        def _(ref=ref):
            for k, at in enumerate(shard_rows(idx_ref, rows)):
                left_ref[k * rows : (k + 1) * rows, :] = ref[at, :]

    y = nn(left_ref[...], du_ref[:, columns]).astype(bf16)
    for k in range(4):
        (send_ref if k < 2 else keep_ref)[k % 2, :, columns] = y[k * rows : (k + 1) * rows]

    @pl.when(i == chunks)
    def _():
        at = (chunks + 1) * width
        lanes = send_ref.shape[2] - at
        shards = width // rows
        pad = jnp.zeros((1, 2 * lanes - rows), f32)
        for k, j in enumerate(ORDER):
            shard = idx_ref[0] ^ j
            out_ref = send_ref if k < 2 else keep_ref
            tiles = [
                bias_ref[0:1, pl.ds(pl.multiple_of(shard * width + t * lanes, lanes), lanes)]
                for t in range(width // lanes)
            ]
            own = sum(
                jnp.where(shard == t, bias_ref[1:2, t * rows : (t + 1) * rows], 0.0) for t in range(shards)
            )
            own = jnp.concatenate([own, pad], axis=1)
            tiles += [own[:, :lanes], own[:, lanes:]]
            block = jnp.concatenate(tiles + [jnp.zeros((16 - len(tiles), lanes), f32)], axis=0)
            out_ref[k % 2, :16, at:] = block.astype(bf16)
            out_ref[k % 2, 16:, at:] = jnp.zeros((rows - 16, lanes), bf16)


def grad_up_call(index, a2t, ot, d_u, biases, shards):
    width, rows = a2t.shape
    own = width // shards
    ff = d_u.shape[1] - width
    chunks = ff // width
    cols = ff + width + TILE
    return call(
        functools.partial(grad_up_body, chunks),
        "grad_up_out",
        (chunks + 1,),
        [fixed(array.shape) for array in (a2t, ot, d_u, biases)],
        [fixed((2, own, cols))] * 2,
        [vmem((2, own, cols), bf16)] * 2,
        [pltpu.VMEM((width, rows), bf16)],
        10,
        4.7,
        near=range(4),
    )(index, a2t, ot, d_u, biases)


def grad_qkv_body(idx_ref, a_ref, *refs):
    rights, send_ref, keep_ref = refs[:-2], refs[-2], refs[-1]
    rows = send_ref.shape[1]
    left = jnp.concatenate([a_ref[at, :] for at in shard_rows(idx_ref, rows)], axis=0)
    at = 0
    for right in rights:
        cols = right.shape[1]
        y = nn(left, right[...]).astype(bf16)
        for k in range(4):
            (send_ref if k < 2 else keep_ref)[k % 2, :, at : at + cols] = y[k * rows : (k + 1) * rows]
        at += cols


def grad_qkv_call(index, a1t, rights, shards):
    own = a1t.shape[0] // shards
    cols = sum(right.shape[1] for right in rights)
    return call(
        grad_qkv_body,
        "grad_qkv",
        (1,),
        [fixed(array.shape) for array in (a1t, *rights)],
        [fixed((2, own, cols))] * 2,
        [vmem((2, own, cols), bf16)] * 2,
        [],
        10,
        1.0 + cols / 1000.0,
        near=range(1 + len(rights)),
    )(index, a1t, *rights)


def input_body(groups, idx_ref, x_ref, dx1_ref, vec_ref, w_ref, *refs):
    grads, (dx_ref,) = refs[: 3 * groups], refs[3 * groups :]
    width = x_ref.shape[1]
    here = step_rows(x_ref.shape[0])
    scaled, inverse = norm_rows(x_ref[...].astype(f32))
    d_a1 = 0.0
    for part in range(3):
        at = part * width
        for g in range(groups):
            ref = grads[3 * g + part]
            cols = ref.shape[1]
            d_a1 = d_a1 + nt(ref[here, :], w_ref[:, at : at + cols])
            at += cols
    d_x = dx1_ref[...] + norm_back(d_a1, scaled, inverse, vec_ref[0:1, :width])
    dx_ref[...] = d_x.astype(bf16)


def input_call(index, x, dx1, vec, d_groups, weight):
    rows, width = x.shape
    step = 256

    def row(cols):
        return pl.BlockSpec((step, cols), lambda i, s: (i, 0))

    flat = [array for group in d_groups for array in group]
    return call(
        functools.partial(input_body, len(d_groups)),
        "grad_input",
        (rows // step,),
        [row(width), row(width)] + [fixed(array.shape) for array in (vec, weight, *flat)],
        row(width),
        hbm((rows, width), bf16),
        [],
        14,
        9,
        near=range(4, 4 + len(flat)),
    )(index, x, dx1, vec, weight, *flat)


def output_body(idx_ref, x1_ref, h_ref, vec_ref, w_ref, out_ref):
    y = x1_ref[...] + nn(h_ref[...], w_ref[...]) + vec_ref[2:3, : x1_ref.shape[1]]
    out_ref[...] = y.astype(bf16)


def output_call(index, x1, h, vec, weight):
    rows, width = x1.shape

    def row(cols):
        return pl.BlockSpec((256, cols), lambda i, s: (i, 0))

    return call(
        output_body,
        "layer_output",
        (rows // 256,),
        [row(width), row(h.shape[1]), fixed(vec.shape), fixed(weight.shape)],
        row(width),
        hbm((rows, width), bf16),
        [],
        14,
        8,
        near=(3,),
    )(index, x1, h, vec, weight)


def pace_body(idx_ref, tile_ref, out_ref):
    out_ref[...] = tile_ref[:8, :]


def pace_call(index, tile):
    return call(
        pace_body,
        "pace",
        (1,),
        [fixed(tile.shape)],
        fixed((8, tile.shape[1])),
        vmem((8, tile.shape[1]), f32),
        [],
        2,
        5,
        near=(0,),
    )(index, tile)


def whole_call(name, jobs):
    arrays = [array for _, ins, _, _ in jobs for array in ins]
    results = [place(shape, dtype) for _, _, outs, place in jobs for shape, dtype in outs]

    def run(*refs):
        ins, outs = refs[: len(arrays)], refs[len(arrays) :]
        at, to = 0, 0
        for body, job_ins, job_outs, _ in jobs:
            body(ins[at : at + len(job_ins)], outs[to : to + len(job_outs)])
            at, to = at + len(job_ins), to + len(job_outs)

    flat = pl.pallas_call(
        run,
        name=name,
        in_specs=[pl.BlockSpec(memory_space=pltpu.VMEM)] * len(arrays),
        out_specs=[pl.BlockSpec(memory_space=pltpu.VMEM)] * len(results),
        out_shape=results,
        compiler_params=pltpu.CompilerParams(vmem_limit_bytes=10 * MIB),
        cost_estimate=pl.CostEstimate(
            flops=0,
            bytes_accessed=sum(array.size * array.dtype.itemsize for array in arrays),
            transcendentals=0,
        ),
    )(*(pltpu.with_memory_space_constraint(array, pltpu.VMEM) for array in arrays))
    groups, at = [], 0
    for _, _, outs, _ in jobs:
        groups.append(flat[at : at + len(outs)])
        at += len(outs)
    return groups


def half_of(bit, flip, rows):
    mine = (lax.axis_index("wide") // bit) % 2
    return pl.ds(pl.multiple_of((1 - mine if flip else mine) * rows, math.gcd(rows, 256)), rows)


def add_job(terms, rows, cols):
    def body(ins, outs):
        outs[0][...] = sum(
            (ref[...] if lead is None else ref[lead]).astype(f32) for ref, (_, lead) in zip(ins, terms)
        ).astype(bf16)

    return body, [a for a, _ in terms], [((rows, cols), bf16)], vmem


def halve_job(terms, rows, cols, bit):
    def body(ins, outs):
        for flip, out in ((1, outs[0]), (0, outs[1])):
            half = half_of(bit, flip, rows)
            out[...] = sum(
                (ref[half, :] if lead is None else ref[lead, half, :]).astype(f32)
                for ref, (_, lead) in zip(ins, terms)
            ).astype(out.dtype)

    return body, [a for a, _ in terms], [((rows, cols), bf16), ((rows, cols), f32)], vmem


def part_job(keep, core, rows, cols):
    def body(ins, outs):
        kept, got = ins
        for j, out in ((1, outs[0]), (0, outs[1])):
            out[...] = (kept[j].astype(f32) + got[j].astype(f32)).astype(out.dtype)

    return body, [keep, core], [((rows, cols), bf16), ((rows, cols), f32)], vmem


def fork_job(keep, core, rows, cols, left):
    rest = cols - left

    def body(ins, outs):
        kept, got = ins
        for j, out in ((1, outs[0]), (0, outs[2])):
            out[...] = (kept[j, :, :left].astype(f32) + got[j, :, :left].astype(f32)).astype(out.dtype)
        for flip, out in ((1, outs[1]), (0, outs[3])):
            half = half_of(1, flip, rows // 2)
            for j in range(2):
                out[j] = (kept[j, half, left:].astype(f32) + got[j, half, left:].astype(f32)).astype(out.dtype)

    shapes = [(rows, left), (2, rows // 2, rest)]
    return body, [keep, core], [(shape, dtype) for dtype in (bf16, f32) for shape in shapes], vmem


def cross_job(own_left, own_right, got_left, got_right, rows, cols, left):
    rows //= 2

    def body(ins, outs):
        lefts, rights, from_left, from_right = ins
        for flip, out in ((1, outs[0]), (0, outs[2])):
            half = half_of(1, flip, rows)
            out[...] = (lefts[half, :] + from_left[half, :].astype(f32)).astype(out.dtype)
        for j, out in ((1, outs[1]), (0, outs[3])):
            out[...] = (rights[j] + from_right[j].astype(f32)).astype(out.dtype)

    shapes = [(rows, left), (rows, cols - left)]
    return (
        body, [own_left, own_right, got_left, got_right], [(shape, dtype) for dtype in (bf16, f32) for shape in shapes],
        vmem,
    )


def merge_job(lefts, rights, rows, cols, left, bit):
    def body(ins, outs):
        for flip, out in ((1, outs[0]), (0, outs[1])):
            half = half_of(bit, flip, rows)
            out[:, :left] = (ins[0][half, :].astype(f32) + ins[1][half, :].astype(f32)).astype(out.dtype)
            out[:, left:] = (ins[2][half, :].astype(f32) + ins[3][half, :].astype(f32)).astype(out.dtype)

    return body, [*lefts, *rights], [((rows, cols), bf16), ((rows, cols), f32)], vmem


def join_job(mine, other, bit):
    rows, cols = mine.shape

    def body(ins, outs):
        for flip in (0, 1):
            outs[0][half_of(bit, flip, rows), :] = ins[flip][...]

    return body, [mine, other], [((2 * rows, cols), bf16)], vmem


def turn_job(mine, other, bit):
    rows, cols = mine.shape

    def body(ins, outs):
        for flip in (0, 1):
            outs[0][:, half_of(bit, flip, rows)] = ins[flip][...].astype(f32).T

    return body, [mine, other], [((cols, 2 * rows), f32)], hbm


def spread_body(plans, w_ref, gain_ref, *refs):
    ins, outs = refs[: 2 * len(plans)], refs[2 * len(plans) :]
    for c, plan in enumerate(plans):
        mine_ref, other_ref = ins[2 * c], ins[2 * c + 1]
        rows = mine_ref.shape[0]
        for flip, ref in ((0, mine_ref), (1, other_ref)):
            for begin, length, out, to in plan:
                outs[out][half_of(1, flip, rows), to : to + length] = ref[:, begin : begin + length].astype(f32)
    share = jnp.sum(outs[0][...] * w_ref[...].astype(f32), axis=1, keepdims=True)
    share = jnp.broadcast_to(share, (share.shape[0], PAIR)).T[0:1]
    outs[-1][...] = (share / gain_ref[...].astype(f32).reshape(1, -1)).reshape(-1)


def spread_job(weight, gain, sums, plans, shapes):
    arrays = [array for pair in sums for array in pair]
    outs = [(shape, f32) for shape in (*shapes, gain.shape)]
    return lambda ins, outs: spread_body(plans, *ins, *outs), [weight, gain, *arrays], outs, hbm


def after(value, *deps):
    return lax.optimization_barrier((value, *deps))[0] if deps else value


class Moves:
    def __init__(self, narrow, wide):
        self.narrow, self.wide = narrow, wide
        self.n = lax.axis_index("narrow")
        self.w = lax.axis_index("wide")
        self.starts = [self.n, self.w % 2, (self.w // 2) % 2]

    def swap(self, value, axis, bit):
        size = self.narrow if axis == "narrow" else self.wide
        return lax.ppermute(value, axis, [(i, i ^ bit) for i in range(size)])

    def place(self, start):
        self.starts.append(start)
        return len(self.starts) - 1

    def reduce(self, send, keep, left=0):
        rows, cols = send.shape[1:]
        core = self.swap(send, "narrow", 1)
        deps = yield (send,)
        core = after(core, *deps)
        if left:
            to_left, to_right, mine_left, mine_right = yield fork_job(keep, core, rows, cols, left)
            got_left, got_right = self.swap(to_left, "narrow", 2), self.swap(to_right, "wide", 1)
            deps = yield to_left, to_right
            to_left, to_right, mine_left, mine_right = yield cross_job(
                mine_left, mine_right, after(got_left, *deps), after(got_right, *deps), rows, cols, left
            )
            got_left, got_right = self.swap(to_left, "wide", 1), self.swap(to_right, "narrow", 2)
            deps = yield to_left, to_right
            rows //= 4
            total, mine = yield merge_job(
                (mine_left, after(got_left, *deps)), (mine_right, after(got_right, *deps)), rows, cols, left, 2
            )
        else:
            total, mine = yield part_job(keep, core, rows, cols)
            got = self.swap(total, "narrow", 2)
            deps = yield (total,)
            total, mine = yield halve_job([(mine, None), (after(got, *deps), None)], rows // 2, cols, 1)
            got = self.swap(total, "wide", 1)
            deps = yield (total,)
            rows //= 4
            total, mine = yield halve_job([(mine, None), (after(got, *deps), None)], rows, cols, 2)
        got = self.swap(total, "wide", 2)
        deps = yield (total,)
        terms = [(mine, None), (after(got, *deps), None)]
        bit = 4
        while bit < self.wide:
            if bit == 4:
                (total,) = yield add_job(terms, rows, cols)
            else:
                total = whole_call("add_terms", [add_job(terms, rows, cols)])[0][0]
            got = self.swap(total, "wide", bit)
            deps = (yield (total,)) if bit == 4 else ()
            terms = [(total, None), (after(got, *deps), None)]
            bit *= 2
        (total,) = yield add_job(terms, rows, cols)
        got = self.swap(total, "wide", 2)
        deps = yield (total,)
        (total,) = yield join_job(total, after(got, *deps), 2)
        got = self.swap(total, "wide", 1)
        deps = yield (total,)
        yield total, after(got, *deps)


def begin(chain):
    return next(chain)


def close(chain, *deps):
    return chain.send(deps)


def advance(chains, *deps):
    jobs = [chain.send(deps) for chain in chains]
    results = whole_call("gradient_sums", jobs)
    return [array for chain, result in zip(chains, results) for array in chain.send(result)]


def shards(narrow, wide, layer_input, cotangent, block_size, gain_attn, w_qkv, w_out, gain_mlp, w_up, b_up, w_down, b_down):
    moves = Moves(narrow, wide)
    x, d_y = layer_input[0], cotangent[0]
    rows, width = x.shape
    seq = rows // 2
    pairs = width // PAIR
    ff = w_up.shape[1]
    n, bit = moves.n, moves.w % 2

    size = w_qkv.shape[0] // 3
    at_qkv = [
        moves.place((n ^ j) * w_qkv.shape[0] + extra)
        for j, extra in (
            (0, 0), (1, 0), (2, bit * size), (2, 2 * size), (2, (1 - bit) * size),
            (3, bit * size), (3, 2 * size), (3, (1 - bit) * size),
        )
    ]
    at_row = [moves.place((n ^ j) * w_out.shape[0]) for j in range(4)]

    at_down = [moves.place((n ^ j) * w_down.shape[0]) for j in range(4)]
    size_up = w_up.shape[0] // 3
    at_up = [
        moves.place((n ^ j) * w_up.shape[0] + extra)
        for j, extra in (
            (0, 0), (1, 0), (2, bit * size_up), (2, 2 * size_up), (2, (1 - bit) * size_up),
            (3, bit * size_up), (3, 2 * size_up), (3, (1 - bit) * size_up),
        )
    ]
    index = jnp.stack(moves.starts).astype(jnp.int32)

    def ready(*deps):
        return after(index, *deps)

    freq = 10000.0 ** (-jnp.arange(HEAD // 2).astype(f32) / (HEAD // 2))
    angles = jnp.arange(seq).astype(f32)[:, None] * freq[None, :]
    cosine, sine = jnp.cos(angles), jnp.sin(angles)
    cosine = jnp.tile(cosine, (1, 4))
    sine = jnp.concatenate([-sine, sine, -sine, sine], axis=1)

    (first,) = thirds_call(index, w_qkv, (1,))
    got_first = moves.swap(first, "narrow", 2)
    second, small = vector_call(ready(first), w_qkv, gain_attn, gain_mlp, b_down, b_up)
    got_second = moves.swap(second, "narrow", 2)
    up_first, up_second = thirds_call(ready(second), w_up, (1, None))
    got_near, got_small, up_near, out_near = (
        moves.swap(after(v, first), "narrow", 1) for v in (w_qkv, small, w_up, w_out)
    )
    up_far, up_more = moves.swap(up_first, "narrow", 2), moves.swap(up_second, "narrow", 2)
    paced = pace_call(ready(up_first), cosine)
    got_first, got_near, got_small, up_near, out_near, _ = lax.optimization_barrier(
        (got_first, got_near, got_small, up_near, out_near, paced)
    )
    got_cross = moves.swap(got_first, "wide", 1)
    far_first = moves.swap(got_first, "narrow", 1)
    out_far = moves.swap(after(w_out, got_first), "narrow", 2)
    far_second, far_cross = (moves.swap(v, "narrow", 1) for v in (got_second, got_cross))
    count = w_qkv.shape[0]
    qkv_w = Weight(
        [
            (array, rows_of, place)
            for (array, rows_of), place in zip(
                (
                    (w_qkv, count), (got_near, count), (got_first, size), (got_second, size), (got_cross, size),
                    (far_first, size), (far_second, size), (far_cross, size),
                ),
                at_qkv,
            )
        ]
    )
    smalls = [small, got_small, got_second, far_second]

    block = jnp.arange(TILE, dtype=jnp.int32) // block_size[0]
    row_block, col_block = block[:, None], block[None, :]
    same, less, upto, less_t, upto_t = (
        jnp.where(ok, 0.0, -1e30).astype(f32)
        for ok in (
            row_block == col_block, col_block < row_block, col_block <= row_block,
            row_block < col_block, row_block <= col_block,
        )
    )
    dyt = d_y.T

    qkv, a1t, vec, qkv_full = qkv_call(index, x, qkv_w, smalls, ff, cosine, sine)
    up_far = after(up_far, vec)
    up_cross = moves.swap(up_far, "wide", 1)
    down_far = moves.swap(after(w_down, up_far), "narrow", 2)
    o, ot, lse = att_call(ready(up_far), qkv, (same, less_t, upto_t))
    up_pieces = [after(v, lse) for v in (up_far, up_more, up_cross)]
    up_last = [moves.swap(v, "narrow", 1) for v in up_pieces]
    out_far = after(out_far, lse)
    out_last = moves.swap(out_far, "narrow", 1)
    out_w = Weight([(a, w_out.shape[0], p) for a, p in zip((w_out, out_near, out_far, out_last), at_row)])
    up_w = Weight(
        [
            (a, r, p)
            for a, r, p in zip(
                (w_up, up_near, *up_pieces, *up_last), (w_up.shape[0],) * 2 + (size_up,) * 6, at_up
            )
        ]
    )
    x1, a2t, h, g, out_full, up_full = up_call(ready(lse), x, o, vec, out_w, up_w)
    send = grad_down_call(index, dyt, h, (1, 2), narrow)
    keep = grad_down_call(ready(send), dyt, h, (0, 2), narrow)
    down_far = after(down_far, keep)
    down_last = moves.swap(down_far, "narrow", 1)
    down_near = moves.swap(after(w_down, send), "narrow", 1)
    down_w = Weight([(a, w_down.shape[0], p) for a, p in zip((w_down, down_near, down_far, down_last), at_down)])
    chain_a = moves.reduce(send, keep, width // 2)
    begin(chain_a)
    d_u, dx1, d_o, biases, down_full = down_call(
        ready(keep, *advance([chain_a], keep)), d_y, x1, g, vec, up_full, out_full, down_w
    )
    send, keep = grad_up_call(ready(*advance([chain_a], biases)), a2t, ot, d_u, biases, narrow)
    chain_b = moves.reduce(send, keep, 2048)
    begin(chain_b)

    def back(start, count, *deps):
        return att_back_call(
            ready(*deps), qkv, d_o, o, lse, (same, less_t, upto_t), cosine, sine, start, count
        )

    paced = pace_call(ready(send), same)
    sent = advance([chain_a], keep, pace_call(ready(keep), same))
    g0 = back(0, 4, keep, *sent, *advance([chain_b], keep, paced, *sent))
    sent = advance([chain_a], g0[0])
    g1 = back(4, pairs - 4, g0[0], *sent, *advance([chain_b], g0[0], *sent))
    groups = [g0, g1]
    rights = [array for group in groups for array in group]
    send, keep = grad_qkv_call(ready(*advance([chain_b], g1[0])), a1t, rights, narrow)
    chain_c = moves.reduce(send, keep, 1152)
    begin(chain_c)
    paced = pace_call(ready(send), same)
    sent = advance([chain_a], keep)
    sent = advance([chain_b, chain_c], keep, paced, *sent)
    output = output_call(ready(keep, *sent), x1, h, vec, down_full)
    sent_a = advance([chain_a], output)
    sent = advance([chain_c], output, *sent_a)
    d_input = input_call(ready(output, *sent_a, *sent), x, dx1, vec, groups, qkv_full)
    sent = advance([chain_b, chain_c], d_input)
    sent = advance([chain_b, chain_c], *sent)
    sum_a = close(chain_a, *sent)
    (grad_down,) = whole_call("last_down", [turn_job(*sum_a, 1)])[0]
    sent = advance([chain_c], *sent, grad_down)
    sent = advance([chain_c], *sent)
    sum_b = close(chain_b, *sent)
    sum_c = close(chain_c)

    own = width // narrow
    grad_up, grad_out, biases, grad_gain_mlp = whole_call(
        "last_up",
        [
            spread_job(
                w_up, gain_mlp, [sum_b], [[(0, ff, 0, 0), (ff, width, 1, 0), (ff + width, TILE, 2, 0)]],
                [(own, ff), (own, width), (own, TILE)],
            )
        ],
    )[0]
    biases = biases[:8].reshape(-1)
    plan, begin_at, to = [], 0, 0
    for group in groups:
        cols = group[0].shape[1]
        for part in range(3):
            plan.append((begin_at, cols, 0, part * width + to))
            begin_at += cols
        to += cols
    grad_qkv, grad_gain_attn = whole_call("last_qkv", [spread_job(w_qkv, gain_attn, [sum_c], [plan], [(own, 3 * width)])])[0]
    return (
        output[None],
        d_input[None],
        grad_gain_attn,
        grad_qkv,
        grad_out,
        grad_gain_mlp,
        grad_up,
        biases[:width],
        grad_down,
        biases[width : width + own],
    )


def solution(mesh):
    return jax.shard_map(
        functools.partial(shards, mesh.shape["narrow"], mesh.shape["wide"]),
        mesh=mesh,
        in_specs=(
            P(("wide", "narrow"), None, None),
            P(("wide", "narrow"), None, None),
            P(("wide", "narrow")),
            P("narrow"),
            P("narrow", None),
            P("narrow", None),
            P("narrow"),
            P("narrow", None),
            P("narrow"),
            P("narrow", None),
            P("narrow"),
        ),
        out_specs=(
            P(("wide", "narrow"), None, None),
            P(("wide", "narrow"), None, None),
            P("narrow"),
            P("narrow", None),
            P("narrow", None),
            P("narrow"),
            P("narrow", None),
            P("narrow"),
            P("narrow", None),
            P("narrow"),
        ),
        check_vma=False,
    )
```
